128 devices in a mesh: grp: 4 (over y), ffn: 32 (over x, z, core).
Axes of the slice: x: 4, y: 4, z: 4, core: 2. Of those that a mesh axis runs over, the one named last changes fastest.
Arguments:
- layer_input: bfloat16 [288, 5120], P(None, 'ffn')
- norm_gain: float32 [5120], P('ffn'), may hold values from 0.1 to 1.9
- qkv_weight: bfloat16 [3, 5120, 2560], P(None, 'ffn', 'grp'), may hold values from -0.078125 to 0.078125
- key_cache: bfloat16 [896, 128, 2560], P('ffn', None, 'grp'), may hold values from -256 to 256
- value_cache: bfloat16 [896, 128, 2560], P('ffn', None, 'grp'), may hold values from -4 to 4
- out_weight: bfloat16 [2560, 5120], P('grp', 'ffn'), may hold values from -0.125 to 0.125
- ffn_gain: float32 [5120], replicated, may hold values from 0.1 to 1.9
- gate_up_weight: bfloat16 [2, 5120, 13824], P(None, None, 'ffn'), may hold values from -0.078125 to 0.078125
- down_weight: bfloat16 [13824, 5120], P('ffn'), may hold values from -0.09375 to 0.09375
- span_offsets: int32 [2], replicated, may hold values from 0 to 16256, as said below
- decode_lengths: int32 [32], replicated, may hold values from 1 to 16383, as said below
- page_table: int32 [34, 128], replicated, may hold values from -1 to 895, as said below
Outputs:
- layer_output: bfloat16 [288, 5120], P('grp', 'ffn')
The draws below stay inside these ranges and needn't reach their ends.
Inputs may be any that keep to these rules, and one draw needn't show every extreme that they name: `span_offsets`: the largest offset equals 16256. `decode_lengths`: one length equals 16383, the others are under 2048. `page_table`: row r holds page ids in its first ceil(n / 128) slots, where n is its prefix length plus its new tokens (128 for prefill, 1 for decode), and -1 in the others; no page id appears twice in the table.
All inputs are finite; a program needn't handle non-finite values.
Results may differ from the reference program's by a relative error of at most 0.025.
Values may be sent and summed in bfloat16 or wider, within the bound.
No kernel may reach another device: no remote copies, remote signals or barrier semaphores. Data moves between devices by JAX's collectives and lax.ppermute only.
A program may use at most 128 MiB of HBM per device.

```python
import math
import jax
import jax.numpy as jnp
from jax import lax

D = 5120
HEADS = 20
HD = 128
FF = 13824
PAGE = 128
MAXLEN = 16384
SPAN = 128
PRE = 2
DEC = 32
DECAP = 2048
MAXP = 128
TOKENS = 288
PAGES = 896


def request_plan(key):
    key_offsets = jax.random.fold_in(key, 101)
    key_lengths = jax.random.fold_in(key, 102)
    key_order = jax.random.fold_in(key, 103)
    key_choose = jax.random.fold_in(key, 104)
    offsets = jax.random.randint(key_offsets, (PRE,), 0, MAXLEN - SPAN + 1)
    chosen = jax.random.randint(key_choose, (2,), 0, 1048576)
    offsets = jnp.where(jnp.arange(PRE) == chosen[0] % PRE, MAXLEN - SPAN, offsets)
    lengths = jax.random.randint(key_lengths, (DEC,), 1, DECAP)
    lengths = jnp.where(jnp.arange(DEC) == chosen[1] % DEC, MAXLEN - 1, lengths)
    needed = jnp.concatenate([(offsets + SPAN + PAGE - 1) // PAGE, (lengths + PAGE) // PAGE])
    starting = jnp.cumsum(needed) - needed
    ordering = jax.random.permutation(key_order, PAGES)
    leader = ordering[0]
    ordering = jnp.where(ordering == PAGES - 1, leader, jnp.where(ordering == leader, PAGES - 1, ordering))
    slot_index = jnp.arange(MAXP)[None, :]
    picked = ordering[jnp.clip(starting[:, None] + slot_index, 0, PAGES - 1)]
    table = jnp.where(slot_index < needed[:, None], picked, -1)
    return (offsets.astype(jnp.int32), lengths.astype(jnp.int32), table.astype(jnp.int32))


def draw_span_offsets(key, part):
    return request_plan(key)[0]


def draw_decode_lengths(key, part):
    return request_plan(key)[1]


def draw_page_table(key, part):
    return request_plan(key)[2]


def draw_layer_input(key, part):
    key_base, key_rows, key_cols = jax.random.split(key, 3)
    row_scale = jnp.exp(jax.random.uniform(key_rows, (TOKENS, 1), minval=math.log(0.4), maxval=math.log(2.5)))
    col_scale = jnp.exp(jax.random.uniform(key_cols, (1, D), minval=math.log(0.6), maxval=math.log(1.6)))
    ramp_scale = jnp.exp(math.log(3.0) * (jnp.arange(D, dtype=jnp.float32) / D - 0.5))[None, :]
    base = jnp.clip(jax.random.normal(key_base, (TOKENS, D)), -4.0, 4.0)
    return (base * row_scale * col_scale * ramp_scale).astype(jnp.bfloat16)


def draw_key_cache(key, part):
    key_base = jax.random.fold_in(key, 0)
    base = jnp.clip(jax.random.normal(key_base, (PAGES, PAGE, HEADS * HD)), -4.0, 4.0)
    return base.astype(jnp.bfloat16)


def draw_value_cache(key, part):
    key_mean, key_noise = jax.random.split(key, 2)
    centre = jax.random.normal(key_mean, (PAGES, 1, HEADS * HD))
    noise = 0.5 * jax.random.normal(key_noise, (PAGES, PAGE, HEADS * HD))
    return jnp.clip(centre + noise, -4.0, 4.0).astype(jnp.bfloat16)


def with_spikes(drawn, rng, source, target, parts, factor):
    def block_of(dim):
        return (jnp.arange(drawn.shape[dim]) // (drawn.shape[dim] // parts)).reshape((-1,) + (1,) * (drawn.ndim - 1 - dim))

    first = jax.random.permutation(rng, parts)[block_of(target)]
    second = (block_of(target) + parts // 2) % parts
    return jnp.where((block_of(source) == first) | (block_of(source) == second), factor * drawn, drawn)


def shard_levels(key, extent, pieces, least, top_value):
    factor_of = 1.0
    for axis_at, blocks in pieces:
        draws = jax.random.uniform(jax.random.fold_in(jax.random.fold_in(key, 6), axis_at), (blocks,), jnp.float32, least / len(pieces), top_value / len(pieces))
        factor_of = factor_of * jnp.repeat(jnp.exp(draws), extent[axis_at] // blocks).reshape((-1,) + (1,) * (len(extent) - 1 - axis_at))
    return factor_of


def gaussian(key, extent, spread, most, cuts=(), kind=jnp.bfloat16):
    level = shard_levels(key, extent, cuts, -0.22, 0.18) if cuts else 1.0
    result = jax.random.normal(key, extent, jnp.float32) * spread * level
    return jnp.minimum(jnp.maximum(result, -most), most).astype(kind)


def gaussian_with(rng, shape, deviation, bound, cuts, heavy, kind=jnp.bfloat16):
    result = deviation * jax.random.normal(rng, shape, jnp.float32)
    if cuts:
        result = result * shard_levels(rng, shape, cuts, -0.22, 0.18)
    return jnp.clip(with_spikes(result, jax.random.fold_in(rng, 3), *heavy), -bound, bound).astype(kind)


def setup_inputs(seed: int = 0) -> dict:
    keys = jax.random.split(jax.random.key(seed), 13)
    layer_input = draw_layer_input(jax.random.fold_in(keys[12], 71), 0)
    norm_gain = jnp.clip(1.0 + 0.18 * jax.random.normal(keys[1], (D,), jnp.float32), 0.1, 1.9)
    qkv_weight = gaussian(keys[2], (3, D, HEADS * HD), D ** -0.5, 0.078125, ((1, 32), (2, 4)))
    key_cache = draw_key_cache(jax.random.fold_in(keys[12], 71), 0)
    value_cache = draw_value_cache(jax.random.fold_in(keys[12], 71), 0)
    out_weight = gaussian(keys[5], (HEADS * HD, D), (HEADS * HD) ** -0.5, 0.125, ((0, 4), (1, 32)))
    ffn_gain = jnp.clip(1.0 + 0.18 * jax.random.normal(keys[6], (D,), jnp.float32), 0.1, 1.9)
    gate_up_weight = gaussian(keys[7], (2, D, FF), D ** -0.5, 0.078125, ((2, 32),))
    down_weight = gaussian_with(keys[8], (FF, D), FF ** -0.5, 0.09375, ((0, 32),), (0, 1, 32, 2.75))
    span_offsets = draw_span_offsets(jax.random.fold_in(keys[12], 71), 0)
    decode_lengths = draw_decode_lengths(jax.random.fold_in(keys[12], 71), 0)
    page_table = draw_page_table(jax.random.fold_in(keys[12], 71), 0)
    return {"layer_input": layer_input, "norm_gain": norm_gain, "qkv_weight": qkv_weight, "key_cache": key_cache, "value_cache": value_cache, "out_weight": out_weight, "ffn_gain": ffn_gain, "gate_up_weight": gate_up_weight, "down_weight": down_weight, "span_offsets": span_offsets, "decode_lengths": decode_lengths, "page_table": page_table}


EPS = 1e-05
NEG = -1e+30

def rotate(values, positions):
    half_width = values.shape[-1] // 2
    frequency = jnp.exp(jnp.arange(half_width, dtype=jnp.float32) * (-2.0 * math.log(10000.0) / values.shape[-1]))
    angles = positions.astype(jnp.float32)[:, None] * frequency[None, :]
    cosine = jnp.cos(angles)[:, None, :]
    sine_table = jnp.sin(angles)[:, None, :]
    leading = values[..., :half_width]
    trailing = values[..., half_width:]
    return jnp.concatenate([leading * cosine - trailing * sine_table, trailing * cosine + leading * sine_table], axis=-1)

def token_positions(span_offsets, decode_lengths):
    within = jnp.arange(SPAN, dtype=jnp.int32)
    prefill = (span_offsets[:, None] + within[None, :]).reshape(PRE * SPAN)
    return jnp.concatenate([prefill, decode_lengths]).astype(jnp.int32)

def request_keys(page_row, prefix_len, row_start, key_cache, value_cache, new_keys, new_values):
    key_positions = jnp.arange(MAXLEN, dtype=jnp.int32)
    page_ids = jnp.clip(page_row, 0, PAGES - 1).astype(jnp.int32)
    cached_keys = key_cache[page_ids].reshape(MAXLEN, HEADS, HD)
    cached_values = value_cache[page_ids].reshape(MAXLEN, HEADS, HD)
    key_rows = jnp.clip(row_start + key_positions - prefix_len, 0, TOKENS - 1).astype(jnp.int32)
    earlier = (key_positions < prefix_len)[:, None, None]
    return (jnp.where(earlier, cached_keys, new_keys[key_rows]), jnp.where(earlier, cached_values, new_values[key_rows]))

def head_attention(queries, query_positions, all_keys, all_values):
    key_positions = jnp.arange(MAXLEN, dtype=jnp.int32)
    visible = key_positions[None, :] <= query_positions[:, None]
    score_scale = HD ** (-0.5)

    def single_head(operands):
        head_queries, head_keys, head_values = operands
        scores = jnp.dot(head_queries, head_keys.T, preferred_element_type=jnp.float32) * score_scale
        capped = jnp.where(visible, scores, NEG)
        maxima = lax.optimization_barrier(jnp.max(capped, axis=1, keepdims=True))
        weights = jnp.where(visible, jnp.exp(capped - maxima), 0.0)
        totals = lax.optimization_barrier(jnp.sum(weights, axis=1, keepdims=True))
        return jnp.dot(weights.astype(jnp.bfloat16), head_values, preferred_element_type=jnp.float32) / totals
    outputs = lax.map(single_head, (jnp.swapaxes(queries, 0, 1), jnp.swapaxes(all_keys, 0, 1), jnp.swapaxes(all_values, 0, 1)))
    return jnp.swapaxes(outputs, 0, 1).reshape(queries.shape[0], HEADS * HD).astype(jnp.bfloat16)

def reference(layer_input, norm_gain, qkv_weight, key_cache, value_cache, out_weight, ffn_gain, gate_up_weight, down_weight, span_offsets, decode_lengths, page_table):
    input_f32 = layer_input.astype(jnp.float32)
    scaled = (input_f32 * norm_gain[None, :]).astype(jnp.bfloat16)
    inverse = lax.rsqrt(lax.optimization_barrier(jnp.sum(input_f32 * input_f32, axis=1)) / D + EPS)[:, None]
    positions = token_positions(span_offsets, decode_lengths)

    def project(which):
        projected = jnp.dot(scaled, qkv_weight[which], preferred_element_type=jnp.float32) * inverse
        return projected.reshape(TOKENS, HEADS, HD)
    queries = rotate(project(0), positions).astype(jnp.bfloat16)
    new_keys = rotate(project(1), positions).astype(jnp.bfloat16)
    new_values = project(2).astype(jnp.bfloat16)
    blocks = []
    for request in range(PRE):
        all_keys, all_values = request_keys(page_table[request], span_offsets[request], request * SPAN, key_cache, value_cache, new_keys, new_values)
        lower = request * SPAN
        blocks.append(head_attention(queries[lower:lower + SPAN], positions[lower:lower + SPAN], all_keys, all_values))

    def decode_one(operands):
        page_row, length, row_index = operands
        all_keys, all_values = request_keys(page_row, length, row_index, key_cache, value_cache, new_keys, new_values)
        query = lax.dynamic_slice_in_dim(queries, row_index, 1, 0)
        return head_attention(query, length[None], all_keys, all_values)[0]
    decode_rows = PRE * SPAN + jnp.arange(DEC, dtype=jnp.int32)
    blocks.append(lax.map(decode_one, (page_table[PRE:], decode_lengths, decode_rows)))
    heads_out = jnp.concatenate(blocks, axis=0)
    residual = (input_f32 + jnp.dot(heads_out, out_weight, preferred_element_type=jnp.float32)).astype(jnp.bfloat16)
    residual_f32 = residual.astype(jnp.float32)
    normed = (residual_f32 * lax.rsqrt(lax.optimization_barrier(jnp.sum(residual_f32 * residual_f32, axis=1)) / D + EPS)[:, None] * ffn_gain[None, :]).astype(jnp.bfloat16)
    gate = jnp.dot(normed, gate_up_weight[0], preferred_element_type=jnp.float32)
    up_part = jnp.dot(normed, gate_up_weight[1], preferred_element_type=jnp.float32)
    hidden = (jax.nn.silu(gate) * up_part).astype(jnp.bfloat16)
    return (residual_f32 + jnp.dot(hidden, down_weight, preferred_element_type=jnp.float32)).astype(jnp.bfloat16)
```

```python
import functools
import math

import jax
import jax.numpy as jnp
from jax import lax
from jax.experimental import pallas as pl
from jax.experimental.pallas import tpu as pltpu
from jax.sharding import PartitionSpec as P

D = 5120
HD = 128
PAGE = 128
SPAN = 128
PRE = 2
DEC = 32
MAXP = 128
TOKENS = 288
GH = 5
HALF = 144
ROWS = 48
QUARTER = 72
COLS = 160
MSG = 96

EPS = 1e-05
NEG = -1e30
SCALE2 = HD ** (-0.5) * math.log2(math.e)
F32 = jnp.float32
BF16 = jnp.bfloat16
LIMIT = 48 << 20
GROUP = 4
CHUNKS = 4
FCHUNK = 512

vmem = pl.BlockSpec(memory_space=pltpu.VMEM)
smem = pl.BlockSpec(memory_space=pltpu.SMEM)
hbm = pl.BlockSpec(memory_space=pl.ANY)


def params():
    return pltpu.CompilerParams(vmem_limit_bytes=LIMIT)


def lanes(shape):
    return lax.broadcasted_iota(jnp.int32, shape, len(shape) - 1)


def rows_of(shape):
    return lax.broadcasted_iota(jnp.int32, shape, len(shape) - 2)


def split3(value):
    high = value.astype(BF16).astype(F32)
    rest = value - high
    middle = rest.astype(BF16).astype(F32)
    return high, middle, rest - middle


def project_kernel(x_ref, gain_ref, w_ref, out_ref):
    x = x_ref[...].astype(F32)
    scaled = (x * gain_ref[...]).astype(BF16)
    for k in range(3):
        product = jnp.dot(scaled, w_ref[k], preferred_element_type=F32)
        for h in range(GH):
            out_ref[k * GH + h] = product[:, h * HD : (h + 1) * HD].astype(BF16)
    squares = jnp.sum(x * x, axis=1, keepdims=True)
    high, middle, low = split3(squares)
    lane = lanes((TOKENS, HD))
    block = jnp.where(lane == 0, high, jnp.where(lane == 1, middle, jnp.where(lane == 2, low, 0.0)))
    out_ref[3 * GH] = block.astype(BF16)


def rotate_kernel(f_ref, in_ref, cos_ref, sin_ref, out_ref):
    total = in_ref[0].astype(F32)
    for s in range(1, in_ref.shape[0]):
        total = total + in_ref[s].astype(F32)
    turned = jnp.concatenate([total[:, HD // 2 :], total[:, : HD // 2]], axis=1)
    rotated = total * cos_ref[...] + turned * sin_ref[...]
    squares = total[:, 0:1] + total[:, 1:2] + total[:, 2:3]
    high, middle, low = split3(squares)
    lane = lanes((HALF, HD))
    block = jnp.where(lane == 0, high, jnp.where(lane == 1, middle, jnp.where(lane == 2, low, 0.0)))
    result = jnp.where(f_ref[0] >= 6 * GH, block, rotated).astype(BF16)
    for s in range(out_ref.shape[0]):
        out_ref[s] = result


def attention_kernel(
    code_ref,
    prefix_ref,
    f_ref,
    fresh_ref,
    key_hbm,
    value_hbm,
    out_ref,
    keys,
    values,
    sems,
    lists,
    scores,
    self_scores,
    peak,
    summed,
    factor,
    new_keys,
    new_values,
    dec_query,
    dec_peak,
    dec_total,
    dec_sum,
    final,
    lse,
):
    pages = key_hbm.shape[0]
    step = pages // CHUNKS
    copies = []
    for c in range(CHUNKS):
        part = pl.ds(c * step, step)
        copies.append(pltpu.make_async_copy(key_hbm.at[part], keys.at[part], sems.at[0, c]))
        copies.append(pltpu.make_async_copy(value_hbm.at[part], values.at[part], sems.at[1, c]))
    for copy in copies:
        copy.start()

    peak[...] = jnp.full(peak.shape, NEG, F32)
    summed[...] = jnp.zeros(summed.shape, F32)
    dec_peak[...] = jnp.full(dec_peak.shape, NEG, F32)
    dec_total[...] = jnp.zeros(dec_total.shape, F32)
    dec_sum[...] = jnp.zeros(dec_sum.shape, F32)

    squares = fresh_ref[3 * GH].astype(F32)
    squares = squares[:, 0:1] + squares[:, 1:2] + squares[:, 2:3]
    inverse = jnp.broadcast_to(lax.rsqrt(squares / D + EPS), (TOKENS, HD))
    factor[...] = inverse * SCALE2
    for h in range(GH):
        new_keys[h] = (fresh_ref[GH + h].astype(F32) * inverse).astype(BF16)
        new_values[h] = (fresh_ref[2 * GH + h].astype(F32) * inverse).astype(BF16)
        dec_query[h] = fresh_ref[h, PRE * SPAN :, :].astype(F32)

    def classify(p, counts):
        n_pre, n_dec = counts
        code = code_ref[p]
        owner = (code - 1) >> 7
        slot = (code - 1) & 127
        live = (code > 0) & (slot * PAGE < prefix_ref[jnp.maximum(owner, 0)])
        is_pre = live & (owner < PRE)
        is_dec = live & (owner >= PRE)

        @pl.when(is_pre)
        def _():
            lists[0, n_pre] = p

        @pl.when(is_dec)
        def _():
            lists[1, n_dec] = p

        return n_pre + is_pre.astype(jnp.int32), n_dec + is_dec.astype(jnp.int32)

    n_pre, n_dec = lax.fori_loop(0, pages, classify, (0, 0))

    f = f_ref[0]
    has_self = f < PRE * GH
    self_request = jnp.where(f >= GH, 1, 0)
    self_head = jnp.where(has_self, f - GH * self_request, 0)

    def span_rows(request):
        return pl.ds(pl.multiple_of(request * SPAN, SPAN), SPAN)

    def scored(query, key, scale):
        product = lax.dot_general(
            query, key, (((1,), (1,)), ((), ())), preferred_element_type=F32
        )
        return product * scale

    @pl.when(has_self)
    def _():
        part = span_rows(self_request)
        result = scored(fresh_ref[self_head, part, :], new_keys[self_head, part, :], factor[part, :])
        result = jnp.where(lanes((SPAN, SPAN)) <= rows_of((SPAN, SPAN)), result, NEG)
        self_scores[...] = result
        unit = self_request * GH + self_head
        peak[unit] = jnp.maximum(peak[unit], result)

    for copy in copies:
        copy.wait()

    def first_pass(i, _):
        p = lists[0, i]
        code = code_ref[p] - 1
        request = code >> 7
        left = prefix_ref[request] - (code & 127) * PAGE
        part = span_rows(request)
        scale = factor[part, :]
        visible = lanes((SPAN, PAGE)) < left
        for h in range(GH):
            result = scored(fresh_ref[h, part, :], keys[p, :, h * HD : (h + 1) * HD], scale)
            result = jnp.where(visible, result, NEG)
            scores[i, h] = result
            unit = request * GH + h
            peak[unit] = jnp.maximum(peak[unit], result)
        return 0

    lax.fori_loop(0, n_pre, first_pass, 0)

    for unit in range(PRE * GH):
        peak[unit] = jnp.broadcast_to(
            jnp.max(peak[unit], axis=1, keepdims=True), (SPAN, SPAN)
        )

    ones = jnp.ones((PAGE, HD), BF16)

    def weigh(unit, result, value):
        weights = jnp.exp2(result - peak[unit]).astype(BF16)
        both = jnp.concatenate([value, ones], axis=1)
        summed[unit] += jnp.dot(weights, both, preferred_element_type=F32)

    def second_pass(i, _):
        p = lists[0, i]
        request = (code_ref[p] - 1) >> 7
        for h in range(GH):
            weigh(request * GH + h, scores[i, h], values[p, :, h * HD : (h + 1) * HD])
        return 0

    lax.fori_loop(0, n_pre, second_pass, 0)

    @pl.when(has_self)
    def _():
        part = span_rows(self_request)
        weigh(self_request * GH + self_head, self_scores[...], new_values[self_head, part, :])

    def decode_pass(step_index, _):
        found = []
        for j in range(GROUP):
            position = step_index * GROUP + j
            p = lists[1, jnp.minimum(position, n_dec - 1)]
            code = code_ref[p] - 1
            owner = code >> 7
            token = owner - PRE
            left = jnp.where(position < n_dec, prefix_ref[owner] - (code & 127) * PAGE, 0)
            row = rows_of((8, HD))
            query = jnp.concatenate(
                [
                    jnp.where(row == h, jnp.broadcast_to(dec_query[h, pl.ds(token, 1), :], (8, HD)), 0.0)
                    for h in range(GH)
                ],
                axis=1,
            ).astype(BF16)
            result = scored(query, keys[p], factor[pl.ds(PRE * SPAN + token, 1), :])
            visible = lanes((8, PAGE)) < left
            result = jnp.where(visible, result, NEG)
            top = jnp.max(result, axis=1, keepdims=True)
            weights = jnp.where(visible, jnp.exp2(result - top), 0.0)
            total = jnp.sum(weights, axis=1, keepdims=True)
            product = jnp.dot(weights.astype(BF16), values[p], preferred_element_type=F32)
            found.append((token, top, total, product))
        for token, top, total, product in found:
            before = dec_peak[token]
            after = jnp.maximum(before, top)
            keep = jnp.exp2(before - after)
            take = jnp.exp2(top - after)
            dec_peak[token] = after
            dec_total[token] = dec_total[token] * keep + total * take
            wide = jnp.concatenate([keep] * GH, axis=1)
            wide_take = jnp.concatenate([take] * GH, axis=1)
            dec_sum[token] = dec_sum[token] * wide + product * wide_take
        return 0

    lax.fori_loop(0, (n_dec + GROUP - 1) // GROUP, decode_pass, 0)

    for request in range(PRE):
        for h in range(GH):
            unit = request * GH + h
            total = summed[unit, :, HD:]
            some = total > 0.0
            safe = jnp.where(some, total, 1.0)
            part = pl.ds(request * SPAN, SPAN)
            final[h, part, :] = summed[unit, :, :HD] / safe
            lse[h, part, :] = jnp.where(some, peak[unit] + jnp.log2(safe), NEG)

    dec_factor = factor[PRE * SPAN :, :]
    dec_rows = pl.ds(PRE * SPAN, DEC)
    for h in range(GH):
        own = jnp.sum(
            dec_query[h] * new_keys[h, dec_rows, :].astype(F32), axis=1, keepdims=True
        )
        own = jnp.where(f == PRE * GH, jnp.broadcast_to(own, (DEC, HD)) * dec_factor, NEG)
        before = dec_peak[:, h, :]
        after = jnp.maximum(before, own)
        keep = jnp.exp2(before - after)
        take = jnp.where(f == PRE * GH, jnp.exp2(own - after), 0.0)
        total = dec_total[:, h, :] * keep + take
        value = dec_sum[:, h, h * HD : (h + 1) * HD] * keep
        value = value + take * new_values[h, dec_rows, :].astype(F32)
        some = total > 0.0
        safe = jnp.where(some, total, 1.0)
        final[h, dec_rows, :] = value / safe
        lse[h, dec_rows, :] = jnp.where(some, after + jnp.log2(safe), NEG)

    diagonal = rows_of((ROWS, HD)) == lanes((ROWS, HD))
    row = rows_of((16, HD))
    for h in range(GH):
        for b in range(TOKENS // ROWS):
            part = pl.ds(b * ROWS, ROWS)
            target = h * (TOKENS // ROWS) + b
            out_ref[target, :ROWS, :] = final[h, part, :].astype(BF16)
            stat = jnp.sum(jnp.where(diagonal, lse[h, part, :], 0.0), axis=0, keepdims=True)
            high, middle, low = split3(stat)
            block = jnp.where(
                row == 0, high, jnp.where(row == 1, middle, jnp.where(row == 2, low, 0.0))
            )
            out_ref[target, ROWS:, :] = block.astype(BF16)
    for target in range(GH * (TOKENS // ROWS), out_ref.shape[0]):
        out_ref[target] = jnp.zeros(out_ref.shape[1:], BF16)


def merge_kernel(in_ref, out_ref):
    sources = in_ref.shape[0]
    stats = jnp.concatenate(
        [
            jnp.sum(in_ref[s, ROWS:, :].astype(F32), axis=0, keepdims=True)
            for s in range(sources)
        ],
        axis=0,
    )
    top = jnp.max(stats, axis=0, keepdims=True)
    weights = jnp.exp2(stats - top)
    weights = weights / jnp.sum(weights, axis=0, keepdims=True)
    padded = jnp.concatenate([weights, jnp.zeros((HD - sources, HD), F32)], axis=0)
    turned = jnp.transpose(padded)
    total = jnp.zeros((ROWS, HD), F32)
    for s in range(sources):
        total = total + turned[:ROWS, s : s + 1] * in_ref[s, :ROWS, :].astype(F32)
    result = total.astype(BF16)
    for s in range(sources):
        out_ref[s] = result


def output_kernel(in_ref, w_ref, out_ref):
    blocks = TOKENS // ROWS
    heads = jnp.concatenate(
        [
            jnp.concatenate([in_ref[h * blocks + b] for b in range(blocks)], axis=0)
            for h in range(GH)
        ],
        axis=1,
    )
    product = jnp.dot(heads, w_ref[...], preferred_element_type=F32)
    for i in range(out_ref.shape[0]):
        out_ref[i] = product[i * QUARTER : (i + 1) * QUARTER].astype(BF16)


def packed(value):
    third = QUARTER // 3
    tail = value[:, HD:]
    extra = jnp.concatenate(
        [tail[i * third : (i + 1) * third] for i in range(3)]
        + [jnp.zeros((third, HD - 3 * (COLS - HD)), F32)],
        axis=1,
    )
    return jnp.concatenate([value[:, :HD], extra], axis=0).astype(BF16)


def unpacked(message):
    third = QUARTER // 3
    wide = COLS - HD
    extra = message[QUARTER:]
    tail = jnp.concatenate([extra[:, i * wide : (i + 1) * wide] for i in range(3)], axis=0)
    assert tail.shape == (3 * third, wide)
    return jnp.concatenate([message[:QUARTER], tail], axis=1)


def residual_kernel(g_ref, in_ref, x_ref, own_ref, out_ref):
    attended = in_ref[0].astype(F32)
    for i in range(1, in_ref.shape[0]):
        attended = attended + in_ref[i].astype(F32)
    x = x_ref[...].astype(F32)
    own = jnp.zeros((QUARTER, COLS), F32)
    for i in range(in_ref.shape[0]):
        own = jnp.where(g_ref[0] == i, x[i * QUARTER : (i + 1) * QUARTER], own)
    own = (own + attended).astype(BF16)
    own_ref[...] = own
    message = packed(own.astype(F32))
    for s in range(out_ref.shape[0]):
        out_ref[s] = message


def ffn_kernel(
    in_ref, gain_ref, gate_hbm, down_hbm, out_ref, rows, normed, gates, down, sems
):
    copies = []
    for c in range(D // FCHUNK):
        part = pl.ds(c * FCHUNK, FCHUNK)
        copies.append(
            pltpu.make_async_copy(gate_hbm.at[:, part, :], gates.at[:, part, :], sems.at[c])
        )
    copies.append(pltpu.make_async_copy(down_hbm, down, sems.at[D // FCHUNK]))
    for copy in copies:
        copy.start()
    for s in range(in_ref.shape[0]):
        rows[:, s * COLS : (s + 1) * COLS] = unpacked(in_ref[s].astype(F32))
    full = rows[...]
    inverse = lax.rsqrt(jnp.sum(full * full, axis=1, keepdims=True) / D + EPS)
    normed[...] = (full * inverse * gain_ref[...]).astype(BF16)
    hidden_units = down.shape[0]
    gate = jnp.zeros((QUARTER, hidden_units), F32)
    up = jnp.zeros((QUARTER, hidden_units), F32)
    for c in range(D // FCHUNK):
        copies[c].wait()
        part = pl.ds(c * FCHUNK, FCHUNK)
        block = normed[:, part]
        gate = gate + jnp.dot(block, gates[0, part, :], preferred_element_type=F32)
        up = up + jnp.dot(block, gates[1, part, :], preferred_element_type=F32)
    hidden = (gate / (1.0 + jnp.exp(-gate)) * up).astype(BF16)
    copies[-1].wait()
    wide = 4 * COLS
    for s in range(in_ref.shape[0] // 4):
        product = jnp.dot(
            hidden, down[:, s * wide : (s + 1) * wide], preferred_element_type=F32
        )
        for j in range(4):
            out_ref[4 * s + j] = packed(product[:, j * COLS : (j + 1) * COLS])


def finish_kernel(in_ref, own_ref, out_ref):
    total = in_ref[0].astype(F32)
    for s in range(1, in_ref.shape[0]):
        total = total + in_ref[s].astype(F32)
    out_ref[...] = (own_ref[...].astype(F32) + unpacked(total)).astype(BF16)


def call(kernel, out, specs, scratch=(), out_specs=None):
    return pl.pallas_call(
        kernel,
        out_shape=out,
        in_specs=specs,
        out_specs=out_specs if out_specs is not None else vmem,
        scratch_shapes=list(scratch),
        compiler_params=params(),
    )


def shape(*dims, kind=BF16):
    return jax.ShapeDtypeStruct(dims, kind)


def swap(value, axis):
    return lax.all_to_all(value, axis, 0, 0)


def tables(f, span_offsets, decode_lengths):
    within = jnp.arange(SPAN, dtype=jnp.int32)
    prefill = (span_offsets[:, None] + within[None, :]).reshape(PRE * SPAN)
    positions = jnp.concatenate([prefill, decode_lengths])
    positions = jnp.where(f % 2 == 0, positions[:HALF], positions[HALF:])
    half_width = HD // 2
    lane = jnp.arange(HD, dtype=jnp.int32)
    frequency = jnp.exp(
        (lane % half_width).astype(F32) * (-2.0 * math.log(10000.0) / HD)
    )
    angles = positions.astype(F32)[:, None] * frequency[None, :]
    turning = f < 4 * GH
    cosine = jnp.where(turning, jnp.cos(angles), 1.0)
    sine = jnp.where(
        turning, jnp.sin(angles) * jnp.where(lane < half_width, -1.0, 1.0)[None, :], 0.0
    )
    return cosine, sine


def shards(
    layer_input,
    norm_gain,
    qkv_weight,
    key_cache,
    value_cache,
    out_weight,
    ffn_gain,
    gate_up_weight,
    down_weight,
    span_offsets,
    decode_lengths,
    page_table,
):
    ffn = lax.axis_size("ffn")
    grp = lax.axis_size("grp")
    f = lax.axis_index("ffn")
    g = lax.axis_index("grp")
    f1 = f.astype(jnp.int32).reshape(1)
    g1 = g.astype(jnp.int32).reshape(1)
    pages = key_cache.shape[0]
    hidden_units = down_weight.shape[0]

    cosine, sine = tables(f, span_offsets, decode_lengths)
    local_ids = f * pages + jnp.arange(pages, dtype=jnp.int32)
    requests = PRE + DEC
    numbers = jnp.arange(requests * MAXP, dtype=jnp.int32).reshape(requests, MAXP) + 1
    codes = jnp.sum(
        jnp.where(page_table[None] == local_ids[:, None, None], numbers[None], 0), axis=(1, 2)
    )
    prefixes = jnp.concatenate([span_offsets, decode_lengths])

    partial = call(project_kernel, shape(3 * GH + 1, TOKENS, HD), [vmem] * 3)(
        layer_input, norm_gain.reshape(1, -1), qkv_weight
    )
    partial = swap(partial.reshape(ffn, HALF, HD), "ffn")
    fresh = call(rotate_kernel, shape(ffn, HALF, HD), [smem] + [vmem] * 3)(
        f1, partial, cosine, sine
    )
    fresh = swap(fresh, "ffn").reshape(3 * GH + 1, TOKENS, HD)

    units = PRE * GH
    message = call(
        attention_kernel,
        shape(ffn, ROWS + 16, HD),
        [smem] * 3 + [vmem] + [hbm] * 2,
        [
            pltpu.VMEM((pages, PAGE, GH * HD), BF16),
            pltpu.VMEM((pages, PAGE, GH * HD), BF16),
            pltpu.SemaphoreType.DMA((2, CHUNKS)),
            pltpu.SMEM((2, pages), jnp.int32),
            pltpu.VMEM((pages, GH, SPAN, PAGE), F32),
            pltpu.VMEM((SPAN, SPAN), F32),
            pltpu.VMEM((units, SPAN, PAGE), F32),
            pltpu.VMEM((units, SPAN, 2 * HD), F32),
            pltpu.VMEM((TOKENS, HD), F32),
            pltpu.VMEM((GH, TOKENS, HD), BF16),
            pltpu.VMEM((GH, TOKENS, HD), BF16),
            pltpu.VMEM((GH, DEC, HD), F32),
            pltpu.VMEM((DEC, 8, HD), F32),
            pltpu.VMEM((DEC, 8, HD), F32),
            pltpu.VMEM((DEC, 8, GH * HD), F32),
            pltpu.VMEM((GH, TOKENS, HD), F32),
            pltpu.VMEM((GH, TOKENS, HD), F32),
        ],
    )(codes, prefixes, f1, fresh, key_cache, value_cache)
    message = swap(message, "ffn")
    heads = call(merge_kernel, shape(ffn, ROWS, HD), [vmem])(message)
    heads = swap(heads, "ffn")

    product = call(output_kernel, shape(grp, QUARTER, COLS), [vmem] * 2)(heads, out_weight)
    product = swap(product, "grp")
    own, rows = call(
        residual_kernel,
        (shape(QUARTER, COLS), shape(ffn, MSG, HD)),
        [smem] + [vmem] * 2,
        out_specs=(vmem, vmem),
    )(g1, product, layer_input)
    rows = swap(rows, "ffn")

    down_terms = call(
        ffn_kernel,
        shape(ffn, MSG, HD),
        [vmem] * 2 + [hbm] * 2,
        [
            pltpu.VMEM((QUARTER, D), F32),
            pltpu.VMEM((QUARTER, D), BF16),
            pltpu.VMEM((2, D, hidden_units), BF16),
            pltpu.VMEM((hidden_units, D), BF16),
            pltpu.SemaphoreType.DMA((D // FCHUNK + 1,)),
        ],
    )(rows, ffn_gain.reshape(1, -1), gate_up_weight, down_weight)
    down_terms = swap(down_terms, "ffn")
    return call(finish_kernel, shape(QUARTER, COLS), [vmem] * 2)(down_terms, own)


def solution(mesh):
    in_specs = (
        P(None, "ffn"),
        P("ffn"),
        P(None, "ffn", "grp"),
        P("ffn", None, "grp"),
        P("ffn", None, "grp"),
        P("grp", "ffn"),
        P(),
        P(None, None, "ffn"),
        P("ffn", None),
        P(),
        P(),
        P(),
    )
    out_specs = P("grp", "ffn")
    return jax.shard_map(shards, mesh=mesh, in_specs=in_specs, out_specs=out_specs, check_vma=False)
```

```python
import functools
import math

import jax
import jax.numpy as jnp
from jax import lax
from jax.experimental import pallas as pl
from jax.experimental.pallas import tpu as pltpu
from jax.sharding import PartitionSpec as P

D = 5120
HD = 128
PAGE = 128
SPAN = 128
PRE = 2
DEC = 32
MAXP = 128
TOKENS = 288
GH = 5
ROWS = 48
QUARTER = 72
COLS = 160
MSG = 96
FEW = 12
STATS = 8

EPS = 1e-05
NEG = -1e30
SCALE2 = HD ** (-0.5) * math.log2(math.e)
F32 = jnp.float32
BF16 = jnp.bfloat16
LIMIT = 32 << 20
GROUP = 4
CHUNKS = 4
FCHUNK = 512

vmem = pl.BlockSpec(memory_space=pltpu.VMEM)
smem = pl.BlockSpec(memory_space=pltpu.SMEM)
hbm = pl.BlockSpec(memory_space=pl.ANY)


def params():
    return pltpu.CompilerParams(vmem_limit_bytes=LIMIT)


def lanes(shape):
    return lax.broadcasted_iota(jnp.int32, shape, len(shape) - 1)


def rows_of(shape):
    return lax.broadcasted_iota(jnp.int32, shape, len(shape) - 2)


def split3(value):
    high = value.astype(BF16).astype(F32)
    rest = value - high
    middle = rest.astype(BF16).astype(F32)
    return high, middle, rest - middle


def project_kernel(x_hbm, gain_hbm, w_hbm, out_ref, x_vmem, gain_ref, w_vmem, sems):
    copies = [pltpu.make_async_copy(x_hbm, x_vmem, sems.at[3])]
    gain_copy = pltpu.make_async_copy(gain_hbm, gain_ref, sems.at[4])
    gain_copy.start()
    for k in range(3):
        copies.append(pltpu.make_async_copy(w_hbm.at[k], w_vmem.at[k], sems.at[k]))
    for copy in copies:
        copy.start()
    copies[0].wait()
    gain_copy.wait()
    x = jnp.transpose(x_vmem[...].astype(F32))
    scaled = (x * gain_ref[...]).astype(BF16)
    squares = jnp.sum(x * x, axis=1, keepdims=True)
    blocks = TOKENS // ROWS
    diagonal = rows_of((ROWS, HD)) == lanes((ROWS, HD))
    row = rows_of((STATS, HD))
    for b in range(blocks):
        part = jnp.broadcast_to(squares[b * ROWS : (b + 1) * ROWS], (ROWS, HD))
        stat = jnp.sum(jnp.where(diagonal, part, 0.0), axis=0, keepdims=True)
        high, middle, low = split3(stat)
        block = jnp.where(
            row == 0, high, jnp.where(row == 1, middle, jnp.where(row == 2, low, 0.0))
        ).astype(BF16)
        for h in range(GH):
            out_ref[h * blocks + b, 3 * ROWS :, :] = block
    for k in range(3):
        copies[1 + k].wait()
        product = jnp.dot(scaled, w_vmem[k], preferred_element_type=F32).astype(BF16)
        for h in range(GH):
            for b in range(blocks):
                out_ref[h * blocks + b, k * ROWS : (k + 1) * ROWS, :] = product[
                    b * ROWS : (b + 1) * ROWS, h * HD : (h + 1) * HD
                ]
    for target in range(GH * blocks, out_ref.shape[0]):
        out_ref[target] = jnp.zeros(out_ref.shape[1:], BF16)


def rotate_kernel(in_ref, cos_ref, sin_ref, out_ref, own_ref):
    total = in_ref[0].astype(F32)
    for s in range(1, in_ref.shape[0]):
        total = total + in_ref[s].astype(F32)
    diagonal = rows_of((ROWS, HD)) == lanes((ROWS, HD))
    stat = jnp.sum(total[3 * ROWS :], axis=0, keepdims=True)
    squares = jnp.sum(
        jnp.where(diagonal, jnp.broadcast_to(stat, (ROWS, HD)), 0.0), axis=1, keepdims=True
    )
    inverse = lax.rsqrt(squares / D + EPS)

    def rotated(value):
        value = value * inverse
        turned = jnp.concatenate([value[:, HD // 2 :], value[:, : HD // 2]], axis=1)
        return (value * cos_ref[...] + turned * sin_ref[...]).astype(BF16)

    own_ref[0] = rotated(total[ROWS : 2 * ROWS])
    own_ref[1] = (total[2 * ROWS : 3 * ROWS] * inverse).astype(BF16)
    query = rotated(total[:ROWS])
    for s in range(out_ref.shape[0]):
        out_ref[s] = query


def attention_kernel(
    code_ref,
    prefix_ref,
    f_ref,
    fresh_ref,
    own_ref,
    key_hbm,
    value_hbm,
    out_ref,
    keys,
    values,
    sems,
    lists,
    scores,
    peak,
    summed,
    dec_query,
    dec_peak,
    dec_total,
    dec_sum,
    final,
    lse,
):
    pages = key_hbm.shape[0]
    step = pages // CHUNKS
    parts = [pl.ds(c * step, step) for c in range(CHUNKS)]
    copies = [
        pltpu.make_async_copy(key_hbm.at[part], keys.at[part], sems.at[0, c])
        for c, part in enumerate(parts)
    ] + [
        pltpu.make_async_copy(value_hbm.at[part], values.at[part], sems.at[1, c])
        for c, part in enumerate(parts)
    ]
    for copy in copies:
        copy.start()

    peak[...] = jnp.full(peak.shape, NEG, F32)
    summed[...] = jnp.zeros(summed.shape, F32)
    dec_peak[...] = jnp.full(dec_peak.shape, NEG, F32)
    dec_total[...] = jnp.zeros(dec_total.shape, F32)
    dec_sum[...] = jnp.zeros(dec_sum.shape, F32)
    final[:, TOKENS:, :] = jnp.zeros((GH, 16, HD), F32)
    lse[:, TOKENS:, :] = jnp.zeros((GH, 16, HD), F32)
    for h in range(GH):
        dec_query[h] = fresh_ref[h * TOKENS + PRE * SPAN : (h + 1) * TOKENS, :].astype(F32)

    def classify(p, counts):
        n_pre, n_dec = counts
        code = code_ref[p]
        owner = (code - 1) >> 7
        slot = (code - 1) & 127
        live = (code > 0) & (slot * PAGE < prefix_ref[jnp.maximum(owner, 0)])
        is_pre = live & (owner < PRE)
        is_dec = live & (owner >= PRE)

        @pl.when(is_pre)
        def _():
            lists[0, n_pre] = p

        @pl.when(is_dec)
        def _():
            lists[1, n_dec] = p

        return n_pre + is_pre.astype(jnp.int32), n_dec + is_dec.astype(jnp.int32)

    n_pre, n_dec = lax.fori_loop(0, pages, classify, (0, 0))

    f = f_ref[0]
    blocks = TOKENS // ROWS
    has_own = f < GH * blocks
    own_head = jnp.where(has_own, f // blocks, 0)
    own_block = jnp.where(has_own, f - own_head * blocks, 0)
    filler = jnp.zeros((PAGE - ROWS, HD), BF16)
    own_keys = jnp.concatenate([own_ref[0], filler], axis=0)
    own_values = jnp.concatenate([own_ref[1], filler], axis=0)
    own_token = own_block * ROWS + lanes((SPAN, PAGE))
    in_block = lanes((SPAN, PAGE)) < ROWS

    def query_rows(request, h):
        return fresh_ref[pl.ds(pl.multiple_of(h * TOKENS + request * SPAN, 16), SPAN), :]

    def scored(query, key):
        product = lax.dot_general(
            query, key, (((1,), (1,)), ((), ())), preferred_element_type=F32
        )
        return product * SCALE2

    def own_scores(request):
        within = own_token - request * SPAN
        visible = in_block & (within >= 0) & (within <= rows_of((SPAN, PAGE)))
        return jnp.where(visible, scored(query_rows(request, own_head), own_keys), NEG), visible

    @pl.when(has_own)
    def _():
        for request in range(PRE):
            unit = request * GH + own_head
            peak[unit] = jnp.maximum(peak[unit], own_scores(request)[0])

    for copy in copies[:CHUNKS]:
        copy.wait()

    def first_pass(i, _):
        p = lists[0, i]
        code = code_ref[p] - 1
        request = code >> 7
        left = prefix_ref[request] - (code & 127) * PAGE
        visible = lanes((SPAN, PAGE)) < left
        for h in range(GH):
            result = scored(query_rows(request, h), keys[p, :, h * HD : (h + 1) * HD])
            result = jnp.where(visible, result, NEG)
            scores[i, h] = result
            unit = request * GH + h
            peak[unit] = jnp.maximum(peak[unit], result)
        return 0

    lax.fori_loop(0, n_pre, first_pass, 0)

    for unit in range(PRE * GH):
        peak[unit] = jnp.broadcast_to(
            jnp.max(peak[unit], axis=1, keepdims=True), (SPAN, SPAN)
        )

    for copy in copies[CHUNKS:]:
        copy.wait()

    ones = jnp.ones((PAGE, HD), BF16)

    def weigh(unit, weights, value):
        both = jnp.concatenate([value, ones], axis=1)
        summed[unit] += jnp.dot(weights.astype(BF16), both, preferred_element_type=F32)

    def second_pass(i, _):
        p = lists[0, i]
        request = (code_ref[p] - 1) >> 7
        for h in range(GH):
            unit = request * GH + h
            weights = jnp.exp2(scores[i, h] - peak[unit])
            weigh(unit, weights, values[p, :, h * HD : (h + 1) * HD])
        return 0

    lax.fori_loop(0, n_pre, second_pass, 0)

    @pl.when(has_own)
    def _():
        for request in range(PRE):
            unit = request * GH + own_head
            result, visible = own_scores(request)
            weigh(unit, jnp.where(visible, jnp.exp2(result - peak[unit]), 0.0), own_values)

    def decode_pass(step_index, _):
        found = []
        for j in range(GROUP):
            position = step_index * GROUP + j
            p = lists[1, jnp.minimum(position, n_dec - 1)]
            code = code_ref[p] - 1
            owner = code >> 7
            token = owner - PRE
            left = jnp.where(position < n_dec, prefix_ref[owner] - (code & 127) * PAGE, 0)
            row = rows_of((8, HD))
            query = jnp.concatenate(
                [
                    jnp.where(row == h, jnp.broadcast_to(dec_query[h, pl.ds(token, 1), :], (8, HD)), 0.0)
                    for h in range(GH)
                ],
                axis=1,
            ).astype(BF16)
            visible = lanes((8, PAGE)) < left
            result = jnp.where(visible, scored(query, keys[p]), NEG)
            top = jnp.max(result, axis=1, keepdims=True)
            weights = jnp.where(visible, jnp.exp2(result - top), 0.0)
            total = jnp.sum(weights, axis=1, keepdims=True)
            product = jnp.dot(weights.astype(BF16), values[p], preferred_element_type=F32)
            found.append((token, top, total, product))
        for token, top, total, product in found:
            before = dec_peak[token]
            after = jnp.maximum(before, top)
            keep = jnp.exp2(before - after)
            take = jnp.exp2(top - after)
            dec_peak[token] = after
            dec_total[token] = dec_total[token] * keep + total * take
            wide = jnp.concatenate([keep] * GH, axis=1)
            wide_take = jnp.concatenate([take] * GH, axis=1)
            dec_sum[token] = dec_sum[token] * wide + product * wide_take
        return 0

    lax.fori_loop(0, (n_dec + GROUP - 1) // GROUP, decode_pass, 0)

    for request in range(PRE):
        for h in range(GH):
            unit = request * GH + h
            total = summed[unit, :, HD:]
            some = total > 0.0
            safe = jnp.where(some, total, 1.0)
            part = pl.ds(request * SPAN, SPAN)
            final[h, part, :] = summed[unit, :, :HD] / safe
            lse[h, part, :] = jnp.where(some, peak[unit] + jnp.log2(safe), NEG)

    first = ROWS - DEC
    dec_rows = pl.ds(PRE * SPAN, DEC)
    for h in range(GH):
        mine = f == h * blocks + blocks - 1
        own = jnp.sum(dec_query[h] * own_ref[0].astype(F32)[first:], axis=1, keepdims=True)
        own = jnp.where(mine, jnp.broadcast_to(own, (DEC, HD)) * SCALE2, NEG)
        before = dec_peak[:, h, :]
        after = jnp.maximum(before, own)
        keep = jnp.exp2(before - after)
        take = jnp.where(mine, jnp.exp2(own - after), 0.0)
        total = dec_total[:, h, :] * keep + take
        value = dec_sum[:, h, h * HD : (h + 1) * HD] * keep
        value = value + take * own_ref[1].astype(F32)[first:]
        some = total > 0.0
        safe = jnp.where(some, total, 1.0)
        final[h, dec_rows, :] = value / safe
        lse[h, dec_rows, :] = jnp.where(some, after + jnp.log2(safe), NEG)

    row = rows_of((16, HD))
    diagonal = (row == lanes((16, HD))) & (row < FEW)
    ffn = out_ref.shape[0] // (TOKENS // QUARTER)
    for q in range(TOKENS // QUARTER):
        for h in range(GH):
            for b in range(QUARTER // FEW):
                part = pl.ds(q * QUARTER + b * FEW, 16)
                stat = jnp.sum(jnp.where(diagonal, lse[h, part, :], 0.0), axis=0, keepdims=True)
                high, middle, low = split3(stat)
                block = jnp.where(row < FEW, final[h, part, :], 0.0)
                block = jnp.where(row == FEW, high, block)
                block = jnp.where(row == FEW + 1, middle, block)
                block = jnp.where(row == FEW + 2, low, block)
                out_ref[q * ffn + h * (QUARTER // FEW) + b] = block.astype(BF16)
        for target in range(GH * (QUARTER // FEW), ffn):
            out_ref[q * ffn + target] = jnp.zeros((16, HD), BF16)


def merge_kernel(in_ref, out_ref):
    sources = out_ref.shape[0]
    groups = in_ref.shape[0] // sources
    row = rows_of((16, HD))
    all_weights = []
    for g in range(groups):
        stats = jnp.concatenate(
            [
                jnp.sum(
                    jnp.where(row >= FEW, in_ref[g * sources + s].astype(F32), 0.0),
                    axis=0,
                    keepdims=True,
                )
                for s in range(sources)
            ],
            axis=0,
        )
        weights = jnp.exp2(stats - jnp.max(stats, axis=0, keepdims=True))
        all_weights.append(weights / jnp.sum(weights, axis=0, keepdims=True))
    turned = jnp.transpose(jnp.concatenate(all_weights, axis=0))
    pieces = []
    for g in range(groups):
        total = jnp.zeros((16, HD), F32)
        for s in range(sources):
            source = g * sources + s
            total = total + turned[:16, source : source + 1] * in_ref[source].astype(F32)
        pieces.append(total[:FEW])
    result = jnp.concatenate(pieces, axis=0).astype(BF16)
    for s in range(sources):
        out_ref[s] = result


def output_kernel(g_ref, in_ref, x_ref, *refs):
    *w_refs, own_ref, out_ref, spread, heads, product = refs
    blocks = QUARTER // FEW
    groups = len(w_refs)
    for source in range(GH * blocks):
        spread[source, :ROWS, :] = in_ref[source].astype(F32)
        spread[source, ROWS:, :] = jnp.zeros((16, HD), F32)
    for g in range(groups):
        for h in range(GH):
            for b in range(blocks):
                heads[g, b * 16 : (b + 1) * 16, h * HD : (h + 1) * HD] = spread[
                    h * blocks + b, g * FEW : g * FEW + 16, :
                ].astype(BF16)
    attended = jnp.zeros((16 * blocks, COLS), F32)
    for s in range(groups):
        source = lax.rem(g_ref[0] + groups - s, groups)
        attended = attended + turned_dot(heads[source], w_refs[s][...])
    for b in range(blocks):
        product[b * FEW : (b + 1) * FEW, :] = attended[b * 16 : b * 16 + FEW]
    x = x_ref[...].astype(F32)
    own = jnp.zeros((QUARTER, COLS), F32)
    for i in range(groups):
        own = jnp.where(g_ref[0] == i, x[i * QUARTER : (i + 1) * QUARTER], own)
    own = (own + product[...]).astype(BF16)
    own_ref[...] = own
    message = packed(own.astype(F32))
    for s in range(out_ref.shape[0]):
        out_ref[s] = message


def packed(value):
    third = QUARTER // 3
    tail = value[:, HD:]
    extra = jnp.concatenate(
        [tail[i * third : (i + 1) * third] for i in range(3)]
        + [jnp.zeros((third, HD - 3 * (COLS - HD)), F32)],
        axis=1,
    )
    return jnp.concatenate([value[:, :HD], extra], axis=0).astype(BF16)


def unpacked(message):
    third = QUARTER // 3
    wide = COLS - HD
    extra = message[QUARTER:]
    tail = jnp.concatenate([extra[:, i * wide : (i + 1) * wide] for i in range(3)], axis=0)
    assert tail.shape == (3 * third, wide)
    return jnp.concatenate([message[:QUARTER], tail], axis=1)


def turned_dot(left, right):
    return lax.dot_general(left, right, (((1,), (1,)), ((), ())), preferred_element_type=F32)


def ffn_kernel(
    in_ref, gain_ref, gate_hbm, down_hbm, out_ref, rows, normed, gates, down, sems
):
    copies = []
    for c in range(D // FCHUNK):
        part = pl.ds(c * FCHUNK, FCHUNK)
        copies.append(
            pltpu.make_async_copy(gate_hbm.at[:, :, part], gates.at[:, :, part], sems.at[c])
        )
    copies.append(pltpu.make_async_copy(down_hbm, down, sems.at[D // FCHUNK]))
    for copy in copies:
        copy.start()
    for s in range(in_ref.shape[0]):
        rows[:, s * COLS : (s + 1) * COLS] = unpacked(in_ref[s].astype(F32))
    full = rows[...]
    inverse = lax.rsqrt(jnp.sum(full * full, axis=1, keepdims=True) / D + EPS)
    normed[...] = (full * inverse * gain_ref[...]).astype(BF16)
    hidden_units = down.shape[0]
    gate = jnp.zeros((QUARTER, hidden_units), F32)
    up = jnp.zeros((QUARTER, hidden_units), F32)
    for c in range(D // FCHUNK):
        copies[c].wait()
        part = pl.ds(c * FCHUNK, FCHUNK)
        block = normed[:, part]
        gate = gate + turned_dot(block, gates[0, :, part])
        up = up + turned_dot(block, gates[1, :, part])
    hidden = (gate / (1.0 + jnp.exp(-gate)) * up).astype(BF16)
    copies[-1].wait()
    wide = 4 * COLS
    for s in range(in_ref.shape[0] // 4):
        product = jnp.dot(
            hidden, down[:, s * wide : (s + 1) * wide], preferred_element_type=F32
        )
        for j in range(4):
            out_ref[4 * s + j] = packed(product[:, j * COLS : (j + 1) * COLS])


def finish_kernel(in_ref, own_ref, out_ref):
    total = in_ref[0].astype(F32)
    for s in range(1, in_ref.shape[0]):
        total = total + in_ref[s].astype(F32)
    out_ref[...] = (own_ref[...].astype(F32) + unpacked(total)).astype(BF16)


def call(kernel, out, specs, scratch=(), out_specs=None):
    function = pl.pallas_call(
        kernel,
        out_shape=out,
        in_specs=specs,
        out_specs=out_specs if out_specs is not None else vmem,
        scratch_shapes=list(scratch),
        compiler_params=params(),
    )

    def placed(*args):
        return function(
            *[
                pltpu.with_memory_space_constraint(a, pltpu.HBM) if spec is hbm else a
                for a, spec in zip(args, specs)
            ]
        )

    return placed


def shape(*dims, kind=BF16):
    return jax.ShapeDtypeStruct(dims, kind)


def swap(value, axis):
    return lax.all_to_all(value, axis, 0, 0)


def tables(f, span_offsets, decode_lengths):
    within = jnp.arange(SPAN, dtype=jnp.int32)
    prefill = (span_offsets[:, None] + within[None, :]).reshape(PRE * SPAN)
    positions = jnp.concatenate([prefill, decode_lengths])
    block = lax.rem(f, TOKENS // ROWS)
    positions = lax.dynamic_slice_in_dim(positions, block * ROWS, ROWS)
    half_width = HD // 2
    lane = jnp.arange(HD, dtype=jnp.int32)
    frequency = jnp.exp((lane % half_width).astype(F32) * (-2.0 * math.log(10000.0) / HD))
    angles = positions.astype(F32)[:, None] * frequency[None, :]
    sine = jnp.sin(angles) * jnp.where(lane < half_width, -1.0, 1.0)[None, :]
    return jnp.cos(angles), sine


def shards(
    layer_input,
    norm_gain,
    qkv_weight,
    key_cache,
    value_cache,
    out_weight,
    ffn_gain,
    gate_up_weight,
    down_weight,
    span_offsets,
    decode_lengths,
    page_table,
):
    ffn = lax.axis_size("ffn")
    grp = lax.axis_size("grp")
    f = lax.axis_index("ffn")
    g = lax.axis_index("grp")
    f1 = f.astype(jnp.int32).reshape(1)
    g1 = g.astype(jnp.int32).reshape(1)
    pages = key_cache.shape[0]
    hidden_units = down_weight.shape[0]

    cosine, sine = tables(f, span_offsets, decode_lengths)
    local_ids = f * pages + jnp.arange(pages, dtype=jnp.int32)
    requests = PRE + DEC
    numbers = jnp.arange(requests * MAXP, dtype=jnp.int32).reshape(requests, MAXP) + 1
    codes = jnp.sum(
        jnp.where(page_table[None] == local_ids[:, None, None], numbers[None], 0), axis=(1, 2)
    )
    prefixes = jnp.concatenate([span_offsets, decode_lengths])

    partial = call(
        project_kernel,
        shape(ffn, 3 * ROWS + STATS, HD),
        [hbm, hbm, hbm],
        [
            pltpu.VMEM((COLS, TOKENS), BF16),
            pltpu.VMEM((1, COLS), F32),
            pltpu.VMEM(qkv_weight.shape, BF16),
            pltpu.SemaphoreType.DMA((5,)),
        ],
    )(layer_input.T, norm_gain.reshape(1, -1), qkv_weight)
    turned_weight, partial = lax.optimization_barrier((out_weight.T, partial))
    out_weights = [turned_weight] + [
        lax.ppermute(turned_weight, "grp", [(i, (i + s) % grp) for i in range(grp)])
        for s in range(1, grp)
    ]
    partial, *out_weights = lax.optimization_barrier((swap(partial, "ffn"), *out_weights))
    fresh, own_block = call(
        rotate_kernel,
        (shape(ffn, ROWS, HD), shape(2, ROWS, HD)),
        [vmem] * 3,
        out_specs=(vmem, vmem),
    )(partial, cosine, sine)
    fresh = swap(fresh, "ffn").reshape(ffn * ROWS, HD)
    units = PRE * GH
    message = call(
        attention_kernel,
        shape(grp * ffn, 16, HD),
        [smem] * 3 + [vmem] * 2 + [hbm] * 2,
        [
            pltpu.VMEM((pages, PAGE, GH * HD), BF16),
            pltpu.VMEM((pages, PAGE, GH * HD), BF16),
            pltpu.SemaphoreType.DMA((2, CHUNKS)),
            pltpu.SMEM((2, pages), jnp.int32),
            pltpu.VMEM((pages, GH, SPAN, PAGE), F32),
            pltpu.VMEM((units, SPAN, PAGE), F32),
            pltpu.VMEM((units, SPAN, 2 * HD), F32),
            pltpu.VMEM((GH, DEC, HD), F32),
            pltpu.VMEM((DEC, 8, HD), F32),
            pltpu.VMEM((DEC, 8, HD), F32),
            pltpu.VMEM((DEC, 8, GH * HD), F32),
            pltpu.VMEM((GH, TOKENS + 16, HD), F32),
            pltpu.VMEM((GH, TOKENS + 16, HD), F32),
        ],
    )(codes, prefixes, f1, fresh, own_block, key_cache, value_cache)
    message = swap(message, ("grp", "ffn"))
    heads = call(merge_kernel, shape(ffn, ROWS, HD), [vmem])(message)
    heads = swap(heads, "ffn")
    own, rows = call(
        output_kernel,
        (shape(QUARTER, COLS), shape(ffn, MSG, HD)),
        [smem] + [vmem] * (2 + grp),
        [
            pltpu.VMEM((GH * (QUARTER // FEW), ROWS + 16, HD), F32),
            pltpu.VMEM((grp, 16 * (QUARTER // FEW), GH * HD), BF16),
            pltpu.VMEM((QUARTER, COLS), F32),
        ],
        out_specs=(vmem, vmem),
    )(g1, heads, layer_input, *out_weights)
    rows = swap(rows, "ffn")

    down_terms = call(
        ffn_kernel,
        shape(ffn, MSG, HD),
        [vmem] * 2 + [hbm] * 2,
        [
            pltpu.VMEM((QUARTER, D), F32),
            pltpu.VMEM((QUARTER, D), BF16),
            pltpu.VMEM((2, hidden_units, D), BF16),
            pltpu.VMEM((hidden_units, D), BF16),
            pltpu.SemaphoreType.DMA((D // FCHUNK + 1,)),
        ],
    )(rows, ffn_gain.reshape(1, -1), jnp.swapaxes(gate_up_weight, 1, 2), down_weight)
    down_terms = swap(down_terms, "ffn")
    return call(finish_kernel, shape(QUARTER, COLS), [vmem] * 2)(down_terms, own)


def solution(mesh):
    in_specs = (
        P(None, "ffn"),
        P("ffn"),
        P(None, "ffn", "grp"),
        P("ffn", None, "grp"),
        P("ffn", None, "grp"),
        P("grp", "ffn"),
        P(),
        P(None, None, "ffn"),
        P("ffn", None),
        P(),
        P(),
        P(),
    )
    out_specs = P("grp", "ffn")
    return jax.shard_map(shards, mesh=mesh, in_specs=in_specs, out_specs=out_specs, check_vma=False)
```

```python
import functools
import math

import jax
import jax.numpy as jnp
from jax import lax
from jax.experimental import pallas as pl
from jax.experimental.pallas import tpu as pltpu
from jax.sharding import PartitionSpec as P

D = 5120
HD = 128
PAGE = 128
SPAN = 128
PRE = 2
DEC = 32
MAXP = 128
TOKENS = 288
GH = 5
ROWS = 48
QUARTER = 72
COLS = 160
MSG = 96
FEW = 12
STATS = 8

EPS = 1e-05
NEG = -1e30
SCALE2 = HD ** (-0.5) * math.log2(math.e)
F32 = jnp.float32
BF16 = jnp.bfloat16
LIMIT = 32 << 20
GROUP = 4
CHUNKS = 4
FCHUNK = 640

vmem = pl.BlockSpec(memory_space=pltpu.VMEM)
smem = pl.BlockSpec(memory_space=pltpu.SMEM)
hbm = pl.BlockSpec(memory_space=pl.ANY)


def params():
    return pltpu.CompilerParams(vmem_limit_bytes=LIMIT)


def lanes(shape):
    return lax.broadcasted_iota(jnp.int32, shape, len(shape) - 1)


def rows_of(shape):
    return lax.broadcasted_iota(jnp.int32, shape, len(shape) - 2)


def split3(value):
    high = value.astype(BF16).astype(F32)
    rest = value - high
    middle = rest.astype(BF16).astype(F32)
    return high, middle, rest - middle


def project_kernel(x_hbm, gain_hbm, w_hbm, out_ref, x_vmem, gain_ref, w_vmem, sems):
    copies = [pltpu.make_async_copy(x_hbm, x_vmem, sems.at[3])]
    gain_copy = pltpu.make_async_copy(gain_hbm, gain_ref, sems.at[4])
    gain_copy.start()
    for k in range(3):
        copies.append(pltpu.make_async_copy(w_hbm.at[k], w_vmem.at[k], sems.at[k]))
    for copy in copies:
        copy.start()
    copies[0].wait()
    gain_copy.wait()
    x = jnp.transpose(x_vmem[...].astype(F32))
    scaled = (x * gain_ref[...]).astype(BF16)
    squares = jnp.sum(x * x, axis=1, keepdims=True)
    blocks = TOKENS // ROWS
    diagonal = rows_of((ROWS, HD)) == lanes((ROWS, HD))
    row = rows_of((STATS, HD))
    for b in range(blocks):
        part = jnp.broadcast_to(squares[b * ROWS : (b + 1) * ROWS], (ROWS, HD))
        stat = jnp.sum(jnp.where(diagonal, part, 0.0), axis=0, keepdims=True)
        high, middle, low = split3(stat)
        block = jnp.where(
            row == 0, high, jnp.where(row == 1, middle, jnp.where(row == 2, low, 0.0))
        ).astype(BF16)
        for h in range(GH):
            out_ref[h * blocks + b, 3 * ROWS :, :] = block
    for k in range(3):
        copies[1 + k].wait()
        product = jnp.dot(scaled, w_vmem[k], preferred_element_type=F32).astype(BF16)
        for h in range(GH):
            for b in range(blocks):
                out_ref[h * blocks + b, k * ROWS : (k + 1) * ROWS, :] = product[
                    b * ROWS : (b + 1) * ROWS, h * HD : (h + 1) * HD
                ]
    for target in range(GH * blocks, out_ref.shape[0]):
        out_ref[target] = jnp.zeros(out_ref.shape[1:], BF16)


def rotate_kernel(in_ref, cos_ref, sin_ref, out_ref, own_ref):
    total = in_ref[0].astype(F32)
    for s in range(1, in_ref.shape[0]):
        total = total + in_ref[s].astype(F32)
    diagonal = rows_of((ROWS, HD)) == lanes((ROWS, HD))
    stat = jnp.sum(total[3 * ROWS :], axis=0, keepdims=True)
    squares = jnp.sum(
        jnp.where(diagonal, jnp.broadcast_to(stat, (ROWS, HD)), 0.0), axis=1, keepdims=True
    )
    inverse = lax.rsqrt(squares / D + EPS)

    def rotated(value):
        value = value * inverse
        turned = jnp.concatenate([value[:, HD // 2 :], value[:, : HD // 2]], axis=1)
        return (value * cos_ref[...] + turned * sin_ref[...]).astype(BF16)

    own_ref[0] = rotated(total[ROWS : 2 * ROWS])
    own_ref[1] = (total[2 * ROWS : 3 * ROWS] * inverse).astype(BF16)
    query = rotated(total[:ROWS])
    for s in range(out_ref.shape[0]):
        out_ref[s] = query


def attention_kernel(
    lists,
    left_ref,
    token_ref,
    f_ref,
    fresh_ref,
    own_ref,
    key_hbm,
    value_hbm,
    out_ref,
    keys,
    values,
    sems,
    scores,
    peak,
    summed,
    dec_query,
    dec_peak,
    dec_total,
    dec_sum,
    final,
    lse,
):
    pages = key_hbm.shape[0]
    step = pages // CHUNKS
    parts = [pl.ds(c * step, step) for c in range(CHUNKS)]
    copies = [
        pltpu.make_async_copy(key_hbm.at[part], keys.at[part], sems.at[0, c])
        for c, part in enumerate(parts)
    ] + [
        pltpu.make_async_copy(value_hbm.at[part], values.at[part], sems.at[1, c])
        for c, part in enumerate(parts)
    ]
    for copy in copies:
        copy.start()

    peak[...] = jnp.full(peak.shape, NEG, F32)
    summed[...] = jnp.zeros(summed.shape, F32)
    dec_peak[...] = jnp.full(dec_peak.shape, NEG, F32)
    dec_total[...] = jnp.zeros(dec_total.shape, F32)
    dec_sum[...] = jnp.zeros(dec_sum.shape, F32)
    final[:, TOKENS:, :] = jnp.zeros((GH, 16, HD), F32)
    lse[:, TOKENS:, :] = jnp.zeros((GH, 16, HD), F32)
    for h in range(GH):
        dec_query[h] = fresh_ref[h * TOKENS + PRE * SPAN : (h + 1) * TOKENS, :].astype(F32)

    n_pre = [lists[k, pages] for k in range(PRE)]
    n_dec = lists[PRE, pages]

    f = f_ref[0]
    blocks = TOKENS // ROWS
    has_own = f < GH * blocks
    own_head = jnp.where(has_own, f // blocks, 0)
    own_block = jnp.where(has_own, f - own_head * blocks, 0)
    filler = jnp.zeros((PAGE - ROWS, HD), BF16)
    own_keys = jnp.concatenate([own_ref[0], filler], axis=0)
    own_values = jnp.concatenate([own_ref[1], filler], axis=0)
    own_token = own_block * ROWS + lanes((SPAN, PAGE))
    in_block = lanes((SPAN, PAGE)) < ROWS

    def query_rows(request, h):
        return fresh_ref[pl.ds(pl.multiple_of(h * TOKENS + request * SPAN, 16), SPAN), :]

    def scored(query, key):
        product = lax.dot_general(
            query, key, (((1,), (1,)), ((), ())), preferred_element_type=F32
        )
        return product * SCALE2

    def own_scores(request):
        within = own_token - request * SPAN
        visible = in_block & (within >= 0) & (within <= rows_of((SPAN, PAGE)))
        return jnp.where(visible, scored(query_rows(request, own_head), own_keys), NEG), visible

    @pl.when(has_own)
    def _():
        for request in range(PRE):
            unit = request * GH + own_head
            peak[unit] = jnp.maximum(peak[unit], own_scores(request)[0])

    for copy in copies[:CHUNKS]:
        copy.wait()

    def pair(request, i):
        last = n_pre[request] - 1
        first_page = lists[request, 2 * i]
        second_page = lists[request, jnp.minimum(2 * i + 1, last)]
        return first_page, second_page

    def joined(ref, pages_of, h):
        return jnp.concatenate([ref[p, :, h * HD : (h + 1) * HD] for p in pages_of], axis=0)

    wide_lane = lanes((SPAN, 2 * PAGE))
    pairs = [(n + 1) >> 1 for n in n_pre]
    for request in range(PRE):

        def first_pass(i, _, request=request):
            both = pair(request, i)
            left = left_ref[both[0]]
            other = jnp.where(2 * i + 1 < n_pre[request], left_ref[both[1]], 0) + PAGE
            visible = wide_lane < jnp.where(wide_lane < PAGE, left, other)
            for h in range(GH):
                result = scored(query_rows(request, h), joined(keys, both, h))
                result = jnp.where(visible, result, NEG)
                scores[i + request * pairs[0], h] = result
                unit = request * GH + h
                peak[unit] = jnp.maximum(
                    peak[unit], jnp.maximum(result[:, :PAGE], result[:, PAGE:])
                )
            return 0

        lax.fori_loop(0, pairs[request], first_pass, 0)

    for unit in range(PRE * GH):
        peak[unit] = jnp.broadcast_to(
            jnp.max(peak[unit], axis=1, keepdims=True), (SPAN, SPAN)
        )

    for copy in copies[CHUNKS:]:
        copy.wait()

    def weigh(unit, weights, value):
        ones = jnp.ones((value.shape[0], HD), BF16)
        both = jnp.concatenate([value, ones], axis=1)
        summed[unit] += jnp.dot(weights.astype(BF16), both, preferred_element_type=F32)

    for request in range(PRE):

        def second_pass(i, _, request=request):
            both = pair(request, i)
            for h in range(GH):
                unit = request * GH + h
                top = peak[unit]
                top = jnp.concatenate([top, top], axis=1)
                weights = jnp.exp2(scores[i + request * pairs[0], h] - top)
                weigh(unit, weights, joined(values, both, h))
            return 0

        lax.fori_loop(0, pairs[request], second_pass, 0)

    @pl.when(has_own)
    def _():
        for request in range(PRE):
            unit = request * GH + own_head
            result, visible = own_scores(request)
            weigh(unit, jnp.where(visible, jnp.exp2(result - peak[unit]), 0.0), own_values)

    tall = (8 * GROUP, GROUP * PAGE)
    owner_row = rows_of(tall) >> 3

    def decode_pass(step_index, _):
        tokens, picked, queries = [], [], []
        limit = jnp.zeros(tall, jnp.int32)
        row = rows_of((8, HD))
        for j in range(GROUP):
            position = step_index * GROUP + j
            p = lists[PRE, jnp.minimum(position, n_dec - 1)]
            token = token_ref[p]
            left = jnp.where(position < n_dec, left_ref[p], 0)
            limit = jnp.where(owner_row == j, j * PAGE + left, limit)
            tokens.append(token)
            picked.append(p)
            queries.append(
                jnp.concatenate(
                    [
                        jnp.where(
                            row == h,
                            jnp.broadcast_to(dec_query[h, pl.ds(token, 1), :], (8, HD)),
                            0.0,
                        )
                        for h in range(GH)
                    ],
                    axis=1,
                )
            )
        query = jnp.concatenate(queries, axis=0).astype(BF16)
        many_keys = jnp.concatenate([keys[p] for p in picked], axis=0)
        many_values = jnp.concatenate([values[p] for p in picked], axis=0)
        visible = (lanes(tall) >= owner_row * PAGE) & (lanes(tall) < limit)
        result = jnp.where(visible, scored(query, many_keys), NEG)
        tops = jnp.max(result, axis=1, keepdims=True)
        weights = jnp.where(visible, jnp.exp2(result - tops), 0.0)
        totals = jnp.sum(weights, axis=1, keepdims=True)
        products = jnp.dot(weights.astype(BF16), many_values, preferred_element_type=F32)
        found = [
            (
                tokens[j],
                tops[8 * j : 8 * j + 8],
                totals[8 * j : 8 * j + 8],
                products[8 * j : 8 * j + 8],
            )
            for j in range(GROUP)
        ]
        for token, top, total, product in found:
            before = dec_peak[token]
            after = jnp.maximum(before, top)
            keep = jnp.exp2(before - after)
            take = jnp.exp2(top - after)
            dec_peak[token] = after
            dec_total[token] = dec_total[token] * keep + total * take
            wide = jnp.concatenate([keep] * GH, axis=1)
            wide_take = jnp.concatenate([take] * GH, axis=1)
            dec_sum[token] = dec_sum[token] * wide + product * wide_take
        return 0

    lax.fori_loop(0, (n_dec + GROUP - 1) // GROUP, decode_pass, 0)

    for request in range(PRE):
        for h in range(GH):
            unit = request * GH + h
            total = summed[unit, :, HD:]
            some = total > 0.0
            safe = jnp.where(some, total, 1.0)
            part = pl.ds(request * SPAN, SPAN)
            final[h, part, :] = summed[unit, :, :HD] / safe
            lse[h, part, :] = jnp.where(some, peak[unit] + jnp.log2(safe), NEG)

    first = ROWS - DEC
    dec_rows = pl.ds(PRE * SPAN, DEC)
    for h in range(GH):
        mine = f == h * blocks + blocks - 1
        own = jnp.sum(dec_query[h] * own_ref[0].astype(F32)[first:], axis=1, keepdims=True)
        own = jnp.where(mine, jnp.broadcast_to(own, (DEC, HD)) * SCALE2, NEG)
        before = dec_peak[:, h, :]
        after = jnp.maximum(before, own)
        keep = jnp.exp2(before - after)
        take = jnp.where(mine, jnp.exp2(own - after), 0.0)
        total = dec_total[:, h, :] * keep + take
        value = dec_sum[:, h, h * HD : (h + 1) * HD] * keep
        value = value + take * own_ref[1].astype(F32)[first:]
        some = total > 0.0
        safe = jnp.where(some, total, 1.0)
        final[h, dec_rows, :] = value / safe
        lse[h, dec_rows, :] = jnp.where(some, after + jnp.log2(safe), NEG)

    row = rows_of((16, HD))
    diagonal = (row == lanes((16, HD))) & (row < FEW)
    ffn = out_ref.shape[0] // (TOKENS // QUARTER)
    for q in range(TOKENS // QUARTER):
        for h in range(GH):
            for b in range(QUARTER // FEW):
                part = pl.ds(q * QUARTER + b * FEW, 16)
                stat = jnp.sum(jnp.where(diagonal, lse[h, part, :], 0.0), axis=0, keepdims=True)
                high, middle, low = split3(stat)
                block = jnp.where(row < FEW, final[h, part, :], 0.0)
                block = jnp.where(row == FEW, high, block)
                block = jnp.where(row == FEW + 1, middle, block)
                block = jnp.where(row == FEW + 2, low, block)
                out_ref[q * ffn + h * (QUARTER // FEW) + b] = block.astype(BF16)
        for target in range(GH * (QUARTER // FEW), ffn):
            out_ref[q * ffn + target] = jnp.zeros((16, HD), BF16)


def merge_kernel(in_ref, out_ref):
    sources = out_ref.shape[0]
    groups = in_ref.shape[0] // sources
    row = rows_of((16, HD))
    all_weights = []
    for g in range(groups):
        stats = jnp.concatenate(
            [
                jnp.sum(
                    jnp.where(row >= FEW, in_ref[g * sources + s].astype(F32), 0.0),
                    axis=0,
                    keepdims=True,
                )
                for s in range(sources)
            ],
            axis=0,
        )
        weights = jnp.exp2(stats - jnp.max(stats, axis=0, keepdims=True))
        all_weights.append(weights / jnp.sum(weights, axis=0, keepdims=True))
    turned = jnp.transpose(jnp.concatenate(all_weights, axis=0))
    pieces = []
    for g in range(groups):
        total = jnp.zeros((16, HD), F32)
        for s in range(sources):
            source = g * sources + s
            total = total + turned[:16, source : source + 1] * in_ref[source].astype(F32)
        pieces.append(total[:FEW])
    result = jnp.concatenate(pieces, axis=0).astype(BF16)
    for s in range(sources):
        out_ref[s] = result


def output_kernel(g_ref, f_ref, in_ref, x_ref, *refs):
    *w_refs, own_ref, out_ref, spread, heads, product = refs
    blocks = QUARTER // FEW
    groups = len(w_refs)
    for source in range(GH * blocks):
        spread[source, :ROWS, :] = in_ref[source].astype(F32)
        spread[source, ROWS:, :] = jnp.zeros((16, HD), F32)
    for g in range(groups):
        for h in range(GH):
            for b in range(blocks):
                heads[g, b * 16 : (b + 1) * 16, h * HD : (h + 1) * HD] = spread[
                    h * blocks + b, g * FEW : g * FEW + 16, :
                ].astype(BF16)
    attended = jnp.zeros((16 * blocks, COLS), F32)
    for s in range(groups):
        source = lax.rem(g_ref[0] + groups - s, groups)
        attended = attended + turned_dot(heads[source], w_refs[s][...])
    for b in range(blocks):
        product[b * FEW : (b + 1) * FEW, :] = attended[b * 16 : b * 16 + FEW]
    x = x_ref[...].astype(F32)
    own = jnp.zeros((QUARTER, COLS), F32)
    for i in range(groups):
        own = jnp.where(g_ref[0] == i, x[i * QUARTER : (i + 1) * QUARTER], own)
    own = (own + product[...]).astype(BF16)
    own_ref[...] = own
    message = turned_lanes(packed(own.astype(F32)), lax.rem(f_ref[0], 4)).astype(BF16)
    for s in range(out_ref.shape[0]):
        out_ref[s] = message


def packed(value):
    third = QUARTER // 3
    tail = value[:, HD:]
    extra = jnp.concatenate(
        [tail[i * third : (i + 1) * third] for i in range(3)]
        + [jnp.zeros((third, HD - 3 * (COLS - HD)), F32)],
        axis=1,
    )
    return jnp.concatenate([value[:, :HD], extra], axis=0)


def unpacked(message):
    third = QUARTER // 3
    wide = COLS - HD
    extra = message[QUARTER:]
    tail = jnp.concatenate([extra[:, i * wide : (i + 1) * wide] for i in range(3)], axis=0)
    assert tail.shape == (3 * third, wide)
    return jnp.concatenate([message[:QUARTER], tail], axis=1)


def turned_dot(left, right):
    return lax.dot_general(left, right, (((1,), (1,)), ((), ())), preferred_element_type=F32)


def turned_lanes(message, amount):
    result = message
    for j in range(1, 4):
        result = jnp.where(amount == j, pltpu.roll(message, 32 * j, 1), result)
    return result


def tiles_of(messages):
    third = QUARTER // 3
    lane = lanes((QUARTER, HD))
    heads = [m[:QUARTER] for m in messages]
    tails = [
        jnp.concatenate(
            [m[QUARTER:]] + [pltpu.roll(m[QUARTER:], HD - 32 * i, 1) for i in (1, 2)], axis=0
        )
        for m in messages
    ]
    assert tails[0].shape == (3 * third, HD)
    result = [heads[0]]
    for k in range(1, 5):
        tile = jnp.where(lane >= 32 * (k - 1), tails[k - 1], heads[k - 1])
        result.append(jnp.where(lane >= 32 * k, heads[k], tile) if k < 4 else tile)
    return result


def messages_of(product):
    third = QUARTER // 3
    lane = lanes((QUARTER, HD))
    slot = lanes((third, HD)) >> 5
    tiles = [product[:, k * HD : (k + 1) * HD] for k in range(5)]
    result = []
    for j in range(4):
        head = jnp.where(lane >= 32 * j, tiles[j], tiles[j + 1]) if j else tiles[0]
        extra = jnp.zeros((third, HD), F32)
        for i in range(3):
            piece = tiles[j + 1][i * third : (i + 1) * third]
            piece = pltpu.roll(piece, 32 * i, 1) if i else piece
            extra = jnp.where(slot == (i + j) % 4, piece, extra)
        result.append(jnp.concatenate([head, extra], axis=0).astype(BF16))
    return result


def ffn_kernel(
    in_ref, gain_ref, gate_hbm, down_hbm, out_ref, rows, normed, gates, down, hidden, sems
):
    copies = []
    for c in range(D // FCHUNK):
        part = pl.ds(c * FCHUNK, FCHUNK)
        copies.append(
            pltpu.make_async_copy(gate_hbm.at[:, :, part], gates.at[:, :, part], sems.at[c])
        )
    copies.append(pltpu.make_async_copy(down_hbm, down, sems.at[D // FCHUNK]))
    for copy in copies:
        copy.start()
    for s in range(0, in_ref.shape[0], 4):
        tiles = tiles_of([in_ref[s + j].astype(F32) for j in range(4)])
        for k, tile in enumerate(tiles):
            at = s * COLS + k * HD
            rows[:, at : at + HD] = tile
    full = rows[...]
    inverse = lax.rsqrt(jnp.sum(full * full, axis=1, keepdims=True) / D + EPS)
    normed[...] = (full * inverse * gain_ref[...]).astype(BF16)
    gate = jnp.zeros((QUARTER, down.shape[0]), F32)
    up = jnp.zeros((QUARTER, down.shape[0]), F32)
    for c in range(D // FCHUNK):
        copies[c].wait()
        part = pl.ds(c * FCHUNK, FCHUNK)
        block = normed[:, part]
        gate = gate + turned_dot(block, gates[0, :, part])
        up = up + turned_dot(block, gates[1, :, part])
    hidden[...] = (gate / (1.0 + jnp.exp(-gate)) * up).astype(BF16)
    copies[-1].wait()
    wide = 4 * COLS
    for s in range(in_ref.shape[0] // 4):
        product = jnp.dot(
            hidden[...], down[:, s * wide : (s + 1) * wide], preferred_element_type=F32
        )
        for j, message in enumerate(messages_of(product)):
            out_ref[4 * s + j] = message


def finish_kernel(f_ref, in_ref, own_ref, out_ref):
    total = in_ref[0].astype(F32)
    for s in range(1, in_ref.shape[0]):
        total = total + in_ref[s].astype(F32)
    total = turned_lanes(total, lax.rem(4 - lax.rem(f_ref[0], 4), 4))
    out_ref[...] = (own_ref[...].astype(F32) + unpacked(total)).astype(BF16)


def call(kernel, out, specs, scratch=(), out_specs=None):
    function = pl.pallas_call(
        kernel,
        out_shape=out,
        in_specs=specs,
        out_specs=out_specs if out_specs is not None else vmem,
        scratch_shapes=list(scratch),
        compiler_params=params(),
    )

    def placed(*args):
        return function(
            *[
                pltpu.with_memory_space_constraint(a, pltpu.HBM) if spec is hbm else a
                for a, spec in zip(args, specs)
            ]
        )

    return placed


def shape(*dims, kind=BF16):
    return jax.ShapeDtypeStruct(dims, kind)


def swap(value, axis):
    return lax.all_to_all(value, axis, 0, 0)


def tables(f, span_offsets, decode_lengths):
    within = jnp.arange(SPAN, dtype=jnp.int32)
    prefill = (span_offsets[:, None] + within[None, :]).reshape(PRE * SPAN)
    positions = jnp.concatenate([prefill, decode_lengths])
    block = lax.rem(f, TOKENS // ROWS)
    positions = lax.dynamic_slice_in_dim(positions, block * ROWS, ROWS)
    half_width = HD // 2
    lane = jnp.arange(HD, dtype=jnp.int32)
    frequency = jnp.exp((lane % half_width).astype(F32) * (-2.0 * math.log(10000.0) / HD))
    angles = positions.astype(F32)[:, None] * frequency[None, :]
    sine = jnp.sin(angles) * jnp.where(lane < half_width, -1.0, 1.0)[None, :]
    return jnp.cos(angles), sine


def run_attention(
    lists, lefts, tokens, f1, fresh, own_block, key_cache, value_cache, grp, ffn
):
    pages = key_cache.shape[0]
    units = PRE * GH
    return call(
        attention_kernel,
        shape(grp * ffn, 16, HD),
        [smem] * 4 + [vmem] * 2 + [hbm] * 2,
        [
            pltpu.VMEM((pages, PAGE, GH * HD), BF16),
            pltpu.VMEM((pages, PAGE, GH * HD), BF16),
            pltpu.SemaphoreType.DMA((2, CHUNKS)),
            pltpu.VMEM((pages // 2 + 1, GH, SPAN, 2 * PAGE), F32),
            pltpu.VMEM((units, SPAN, PAGE), F32),
            pltpu.VMEM((units, SPAN, 2 * HD), F32),
            pltpu.VMEM((GH, DEC, HD), F32),
            pltpu.VMEM((DEC, 8, HD), F32),
            pltpu.VMEM((DEC, 8, HD), F32),
            pltpu.VMEM((DEC, 8, GH * HD), F32),
            pltpu.VMEM((GH, TOKENS + 16, HD), F32),
            pltpu.VMEM((GH, TOKENS + 16, HD), F32),
        ],
    )(lists, lefts, tokens, f1, fresh, own_block, key_cache, value_cache)


def run_ffn(rows, gain, gate_up, down):
    hidden_units = down.shape[0]
    return call(
        ffn_kernel,
        shape(rows.shape[0], MSG, HD),
        [vmem] * 2 + [hbm] * 2,
        [
            pltpu.VMEM((QUARTER, D), F32),
            pltpu.VMEM((QUARTER, D), BF16),
            pltpu.VMEM((2, hidden_units, D), BF16),
            pltpu.VMEM((hidden_units, D), BF16),
            pltpu.VMEM((QUARTER, hidden_units), BF16),
            pltpu.SemaphoreType.DMA((D // FCHUNK + 1,)),
        ],
    )(rows, gain, gate_up, down)


def shards(
    layer_input,
    norm_gain,
    qkv_weight,
    key_cache,
    value_cache,
    out_weight,
    ffn_gain,
    gate_up_weight,
    down_weight,
    span_offsets,
    decode_lengths,
    page_table,
):
    ffn = lax.axis_size("ffn")
    grp = lax.axis_size("grp")
    f = lax.axis_index("ffn")
    g = lax.axis_index("grp")
    f1 = f.astype(jnp.int32).reshape(1)
    g1 = g.astype(jnp.int32).reshape(1)
    pages = key_cache.shape[0]

    cosine, sine = tables(f, span_offsets, decode_lengths)
    partial = call(
        project_kernel,
        shape(ffn, 3 * ROWS + STATS, HD),
        [hbm, hbm, hbm],
        [
            pltpu.VMEM((COLS, TOKENS), BF16),
            pltpu.VMEM((1, COLS), F32),
            pltpu.VMEM(qkv_weight.shape, BF16),
            pltpu.SemaphoreType.DMA((5,)),
        ],
    )(layer_input.T, norm_gain.reshape(1, -1), qkv_weight)
    page_table, partial = lax.optimization_barrier((page_table, partial))
    local_ids = f * pages + jnp.arange(pages, dtype=jnp.int32)
    requests = PRE + DEC
    numbers = jnp.arange(requests * MAXP, dtype=jnp.int32).reshape(requests, MAXP) + 1
    codes = jnp.sum(
        jnp.where(page_table[None] == local_ids[:, None, None], numbers[None], 0), axis=(1, 2)
    )
    prefixes = jnp.concatenate([span_offsets, decode_lengths])
    owners = (codes - 1) >> 7
    lefts = jnp.sum(
        jnp.where(owners[:, None] == jnp.arange(requests)[None], prefixes[None], 0), axis=1
    )
    lefts = jnp.clip(lefts - ((codes - 1) & 127) * PAGE, 0, PAGE)
    kinds = jnp.where((codes > 0) & (lefts > 0), jnp.minimum(owners, PRE), PRE + 1)
    order = jnp.arange(pages, dtype=jnp.int32)
    same = kinds[:, None] == kinds[None, :]
    rank = jnp.sum(jnp.where(same & (order[None, :] < order[:, None]), 1, 0), axis=1)
    of_kind = kinds[None, :] == jnp.arange(PRE + 1, dtype=jnp.int32)[:, None]
    place = jnp.where(of_kind, rank[None, :], -1)
    lists = jnp.sum(
        jnp.where(place[:, None, :] == order[None, :, None], order[None, None, :], 0), axis=2
    )
    counts = jnp.sum(of_kind.astype(jnp.int32), axis=1, keepdims=True)
    lists = jnp.concatenate([lists, counts], axis=1)
    tokens = jnp.clip(owners - PRE, 0, DEC - 1)

    turned_weight, lists = lax.optimization_barrier((out_weight.T, lists))
    out_weights = [turned_weight] + [
        lax.ppermute(turned_weight, "grp", [(i, (i + s) % grp) for i in range(grp)])
        for s in range(1, grp)
    ]
    partial, *out_weights = lax.optimization_barrier((swap(partial, "ffn"), *out_weights))
    fresh, own_block = call(
        rotate_kernel,
        (shape(ffn, ROWS, HD), shape(2, ROWS, HD)),
        [vmem] * 3,
        out_specs=(vmem, vmem),
    )(partial, cosine, sine)
    fresh = swap(fresh, "ffn").reshape(ffn * ROWS, HD)
    message = run_attention(
        lists, lefts, tokens, f1, fresh, own_block, key_cache, value_cache, grp, ffn
    )
    message = swap(message, ("grp", "ffn"))
    heads = call(merge_kernel, shape(ffn, ROWS, HD), [vmem])(message)
    heads = swap(heads, "ffn")
    own, rows = call(
        output_kernel,
        (shape(QUARTER, COLS), shape(ffn, MSG, HD)),
        [smem] * 2 + [vmem] * (2 + grp),
        [
            pltpu.VMEM((GH * (QUARTER // FEW), ROWS + 16, HD), F32),
            pltpu.VMEM((grp, 16 * (QUARTER // FEW), GH * HD), BF16),
            pltpu.VMEM((QUARTER, COLS), F32),
        ],
        out_specs=(vmem, vmem),
    )(g1, f1, heads, layer_input, *out_weights)
    rows = swap(rows, "ffn")

    down_terms = run_ffn(
        rows, ffn_gain.reshape(1, -1), jnp.swapaxes(gate_up_weight, 1, 2), down_weight
    )
    down_terms = swap(down_terms, "ffn")
    return call(finish_kernel, shape(QUARTER, COLS), [smem] + [vmem] * 2)(f1, down_terms, own)


def solution(mesh):
    in_specs = (
        P(None, "ffn"),
        P("ffn"),
        P(None, "ffn", "grp"),
        P("ffn", None, "grp"),
        P("ffn", None, "grp"),
        P("grp", "ffn"),
        P(),
        P(None, None, "ffn"),
        P("ffn", None),
        P(),
        P(),
        P(),
    )
    out_specs = P("grp", "ffn")
    return jax.shard_map(shards, mesh=mesh, in_specs=in_specs, out_specs=out_specs, check_vma=False)
```

```python
import functools
import math

import jax
import jax.numpy as jnp
from jax import lax
from jax.experimental import pallas as pl
from jax.experimental.pallas import tpu as pltpu
from jax.sharding import PartitionSpec as P

D = 5120
HD = 128
PAGE = 128
SPAN = 128
PRE = 2
DEC = 32
MAXP = 128
TOKENS = 288
GH = 5
ROWS = 48
QUARTER = 72
COLS = 160
MSG = 96
FEW = 12
STATS = 8

EPS = 1e-05
NEG = -1e30
SCALE2 = HD ** (-0.5) * math.log2(math.e)
F32 = jnp.float32
BF16 = jnp.bfloat16
LIMIT = 32 << 20
GROUP = 4
CHUNKS = 4
FCHUNK = 640
AHEAD = 3

vmem = pl.BlockSpec(memory_space=pltpu.VMEM)
smem = pl.BlockSpec(memory_space=pltpu.SMEM)
hbm = pl.BlockSpec(memory_space=pl.ANY)


def params():
    return pltpu.CompilerParams(vmem_limit_bytes=LIMIT)


def lanes(shape):
    return lax.broadcasted_iota(jnp.int32, shape, len(shape) - 1)


def rows_of(shape):
    return lax.broadcasted_iota(jnp.int32, shape, len(shape) - 2)


def split3(value):
    high = value.astype(BF16).astype(F32)
    rest = value - high
    middle = rest.astype(BF16).astype(F32)
    return high, middle, rest - middle


def stat_block(stat):
    row = rows_of((STATS, HD))
    high, middle, low = split3(stat)
    return jnp.where(
        row == 0, high, jnp.where(row == 1, middle, jnp.where(row == 2, low, 0.0))
    ).astype(BF16)


def project_kernel(
    p_ref, x_hbm, gain_hbm, w_hbm, out_ref, x_vmem, gain_ref, w_vmem, x_rows, sems
):
    copies = [pltpu.make_async_copy(x_hbm, x_vmem, sems.at[3])]
    gain_copy = pltpu.make_async_copy(gain_hbm, gain_ref, sems.at[4])
    gain_copy.start()
    for k in range(3):
        copies.append(pltpu.make_async_copy(w_hbm.at[k], w_vmem.at[k], sems.at[k]))
    for copy in copies:
        copy.start()
    copies[0].wait()
    gain_copy.wait()
    x_rows[...] = jnp.transpose(x_vmem[...].astype(F32))
    half = TOKENS // ROWS // 2
    x = jnp.concatenate(
        [
            x_rows[pl.ds(pl.multiple_of((2 * i + p_ref[0]) * ROWS, 16), ROWS), :]
            for i in range(half)
        ],
        axis=0,
    )
    scaled = (x * gain_ref[...]).astype(BF16)
    squares = jnp.sum(x * x, axis=1, keepdims=True)
    diagonal = rows_of((ROWS, HD)) == lanes((ROWS, HD))
    for i in range(half):
        part = jnp.broadcast_to(squares[i * ROWS : (i + 1) * ROWS], (ROWS, HD))
        stat = jnp.sum(jnp.where(diagonal, part, 0.0), axis=0, keepdims=True)
        block = stat_block(stat)
        for h in range(GH):
            out_ref[h * half + i, 3 * ROWS :, :] = block
    for k in range(3):
        copies[1 + k].wait()
        product = jnp.dot(scaled, w_vmem[k], preferred_element_type=F32).astype(BF16)
        for h in range(GH):
            for i in range(half):
                out_ref[h * half + i, k * ROWS : (k + 1) * ROWS, :] = product[
                    i * ROWS : (i + 1) * ROWS, h * HD : (h + 1) * HD
                ]
    for target in range(GH * half, out_ref.shape[0]):
        out_ref[target] = jnp.zeros(out_ref.shape[1:], BF16)


def add_kernel(left_ref, right_ref, out_ref):
    for i in range(out_ref.shape[0]):
        total = left_ref[i].astype(F32) + right_ref[i].astype(F32)
        stat = jnp.sum(total[3 * ROWS :], axis=0, keepdims=True)
        out_ref[i, : 3 * ROWS, :] = total[: 3 * ROWS].astype(BF16)
        out_ref[i, 3 * ROWS :, :] = stat_block(stat)


def rotate_kernel(in_ref, cos_ref, sin_ref, out_ref, own_ref):
    total = in_ref[0].astype(F32)
    for s in range(1, in_ref.shape[0]):
        total = total + in_ref[s].astype(F32)
    diagonal = rows_of((ROWS, HD)) == lanes((ROWS, HD))
    stat = jnp.sum(total[3 * ROWS :], axis=0, keepdims=True)
    squares = jnp.sum(
        jnp.where(diagonal, jnp.broadcast_to(stat, (ROWS, HD)), 0.0), axis=1, keepdims=True
    )
    inverse = lax.rsqrt(squares / D + EPS)

    def rotated(value):
        value = value * inverse
        turned = jnp.concatenate([value[:, HD // 2 :], value[:, : HD // 2]], axis=1)
        return (value * cos_ref[...] + turned * sin_ref[...]).astype(BF16)

    own_ref[0] = rotated(total[ROWS : 2 * ROWS])
    own_ref[1] = (total[2 * ROWS : 3 * ROWS] * inverse).astype(BF16)
    query = rotated(total[:ROWS])
    for s in range(out_ref.shape[0]):
        out_ref[s] = query


def attention_kernel(
    lists,
    left_ref,
    token_ref,
    f_ref,
    fresh_ref,
    own_ref,
    key_hbm,
    value_hbm,
    out_ref,
    keys,
    values,
    sems,
    scores,
    peak,
    summed,
    dec_query,
    dec_peak,
    dec_total,
    dec_sum,
    final,
    lse,
):
    pages = key_hbm.shape[0]
    step = pages // CHUNKS
    parts = [pl.ds(c * step, step) for c in range(CHUNKS)]
    copies = [
        pltpu.make_async_copy(key_hbm.at[part], keys.at[part], sems.at[0, c])
        for c, part in enumerate(parts)
    ] + [
        pltpu.make_async_copy(value_hbm.at[part], values.at[part], sems.at[1, c])
        for c, part in enumerate(parts)
    ]
    for copy in copies:
        copy.start()

    peak[...] = jnp.full(peak.shape, NEG, F32)
    summed[...] = jnp.zeros(summed.shape, F32)
    dec_peak[...] = jnp.full(dec_peak.shape, NEG, F32)
    dec_total[...] = jnp.zeros(dec_total.shape, F32)
    dec_sum[...] = jnp.zeros(dec_sum.shape, F32)
    final[:, TOKENS:, :] = jnp.zeros((GH, 16, HD), F32)
    lse[:, TOKENS:, :] = jnp.zeros((GH, 16, HD), F32)
    for h in range(GH):
        dec_query[h] = fresh_ref[h * TOKENS + PRE * SPAN : (h + 1) * TOKENS, :].astype(F32)

    n_pre = [lists[k, pages] for k in range(PRE)]
    n_dec = lists[PRE, pages]
    pairs = [lists[k, pages + 1 + CHUNKS] for k in range(PRE)]

    f = f_ref[0]
    blocks = TOKENS // ROWS
    has_own = f < GH * blocks
    own_head = jnp.where(has_own, f // blocks, 0)
    own_block = jnp.where(has_own, f - own_head * blocks, 0)
    filler = jnp.zeros((PAGE - ROWS, HD), BF16)
    own_keys = jnp.concatenate([own_ref[0], filler], axis=0)
    own_values = jnp.concatenate([own_ref[1], filler], axis=0)
    own_token = own_block * ROWS + lanes((SPAN, PAGE))
    in_block = lanes((SPAN, PAGE)) < ROWS

    def query_rows(request, h):
        return fresh_ref[pl.ds(pl.multiple_of(h * TOKENS + request * SPAN, 16), SPAN), :]

    def scored(query, key):
        product = lax.dot_general(
            query, key, (((1,), (1,)), ((), ())), preferred_element_type=F32
        )
        return product * SCALE2

    def own_scores(request):
        within = own_token - request * SPAN
        visible = in_block & (within >= 0) & (within <= rows_of((SPAN, PAGE)))
        return jnp.where(visible, scored(query_rows(request, own_head), own_keys), NEG), visible

    @pl.when(has_own)
    def _():
        for request in range(PRE):
            unit = request * GH + own_head
            peak[unit] = jnp.maximum(peak[unit], own_scores(request)[0])

    def pair(request, i):
        last = n_pre[request] - 1
        first_page = lists[request, 2 * i]
        second_page = lists[request, jnp.minimum(2 * i + 1, last)]
        return first_page, second_page

    def joined(ref, pages_of, h):
        return jnp.concatenate([ref[p, :, h * HD : (h + 1) * HD] for p in pages_of], axis=0)

    wide_lane = lanes((SPAN, 2 * PAGE))
    def in_chunks(which, one_pass):
        def chunk(c, _):
            part = pl.ds(c * step, step)
            source, target = ((key_hbm, keys), (value_hbm, values))[which]
            pltpu.make_async_copy(source.at[part], target.at[part], sems.at[which, c]).wait()
            for request in range(PRE):
                lower = lists[request, pages + 1 + c]
                upper = lists[request, pages + 2 + c]
                lax.fori_loop(lower, upper, one_pass(request), 0)
            return 0

        lax.fori_loop(0, CHUNKS, chunk, 0)

    def first_pass(request):
        def one_pair(i, _):
            both = pair(request, i)
            left = left_ref[both[0]]
            other = jnp.where(2 * i + 1 < n_pre[request], left_ref[both[1]], 0) + PAGE
            visible = wide_lane < jnp.where(wide_lane < PAGE, left, other)
            for h in range(GH):
                result = scored(query_rows(request, h), joined(keys, both, h))
                result = jnp.where(visible, result, NEG)
                scores[i + request * pairs[0], h] = result
                unit = request * GH + h
                peak[unit] = jnp.maximum(
                    peak[unit], jnp.maximum(result[:, :PAGE], result[:, PAGE:])
                )
            return 0

        return one_pair

    in_chunks(0, first_pass)

    for unit in range(PRE * GH):
        peak[unit] = jnp.broadcast_to(
            jnp.max(peak[unit], axis=1, keepdims=True), (SPAN, SPAN)
        )

    def weigh(unit, weights, value):
        ones = jnp.ones((value.shape[0], HD), BF16)
        both = jnp.concatenate([value, ones], axis=1)
        summed[unit] += jnp.dot(weights.astype(BF16), both, preferred_element_type=F32)

    def second_pass(request):
        def one_pair(i, _):
            both = pair(request, i)
            for h in range(GH):
                unit = request * GH + h
                top = peak[unit]
                top = jnp.concatenate([top, top], axis=1)
                weights = jnp.exp2(scores[i + request * pairs[0], h] - top)
                weigh(unit, weights, joined(values, both, h))
            return 0

        return one_pair

    in_chunks(1, second_pass)

    @pl.when(has_own)
    def _():
        for request in range(PRE):
            unit = request * GH + own_head
            result, visible = own_scores(request)
            weigh(unit, jnp.where(visible, jnp.exp2(result - peak[unit]), 0.0), own_values)

    tall = (8 * GROUP, GROUP * PAGE)
    owner_row = rows_of(tall) >> 3

    def decode_pass(step_index, _):
        tokens, picked, queries = [], [], []
        limit = jnp.zeros(tall, jnp.int32)
        row = rows_of((8, HD))
        for j in range(GROUP):
            position = step_index * GROUP + j
            p = lists[PRE, jnp.minimum(position, n_dec - 1)]
            token = token_ref[p]
            left = jnp.where(position < n_dec, left_ref[p], 0)
            limit = jnp.where(owner_row == j, j * PAGE + left, limit)
            tokens.append(token)
            picked.append(p)
            queries.append(
                jnp.concatenate(
                    [
                        jnp.where(
                            row == h,
                            jnp.broadcast_to(dec_query[h, pl.ds(token, 1), :], (8, HD)),
                            0.0,
                        )
                        for h in range(GH)
                    ],
                    axis=1,
                )
            )
        query = jnp.concatenate(queries, axis=0).astype(BF16)
        many_keys = jnp.concatenate([keys[p] for p in picked], axis=0)
        many_values = jnp.concatenate([values[p] for p in picked], axis=0)
        visible = (lanes(tall) >= owner_row * PAGE) & (lanes(tall) < limit)
        result = jnp.where(visible, scored(query, many_keys), NEG)
        tops = jnp.max(result, axis=1, keepdims=True)
        weights = jnp.where(visible, jnp.exp2(result - tops), 0.0)
        totals = jnp.sum(weights, axis=1, keepdims=True)
        products = jnp.dot(weights.astype(BF16), many_values, preferred_element_type=F32)
        found = [
            (
                tokens[j],
                tops[8 * j : 8 * j + 8],
                totals[8 * j : 8 * j + 8],
                products[8 * j : 8 * j + 8],
            )
            for j in range(GROUP)
        ]
        for token, top, total, product in found:
            before = dec_peak[token]
            after = jnp.maximum(before, top)
            keep = jnp.exp2(before - after)
            take = jnp.exp2(top - after)
            dec_peak[token] = after
            dec_total[token] = dec_total[token] * keep + total * take
            wide = jnp.concatenate([keep] * GH, axis=1)
            wide_take = jnp.concatenate([take] * GH, axis=1)
            dec_sum[token] = dec_sum[token] * wide + product * wide_take
        return 0

    lax.fori_loop(0, (n_dec + GROUP - 1) // GROUP, decode_pass, 0)

    for request in range(PRE):
        for h in range(GH):
            unit = request * GH + h
            total = summed[unit, :, HD:]
            some = total > 0.0
            safe = jnp.where(some, total, 1.0)
            part = pl.ds(request * SPAN, SPAN)
            final[h, part, :] = summed[unit, :, :HD] / safe
            lse[h, part, :] = jnp.where(some, peak[unit] + jnp.log2(safe), NEG)

    first = ROWS - DEC
    dec_rows = pl.ds(PRE * SPAN, DEC)
    for h in range(GH):
        mine = f == h * blocks + blocks - 1
        own = jnp.sum(dec_query[h] * own_ref[0].astype(F32)[first:], axis=1, keepdims=True)
        own = jnp.where(mine, jnp.broadcast_to(own, (DEC, HD)) * SCALE2, NEG)
        before = dec_peak[:, h, :]
        after = jnp.maximum(before, own)
        keep = jnp.exp2(before - after)
        take = jnp.where(mine, jnp.exp2(own - after), 0.0)
        total = dec_total[:, h, :] * keep + take
        value = dec_sum[:, h, h * HD : (h + 1) * HD] * keep
        value = value + take * own_ref[1].astype(F32)[first:]
        some = total > 0.0
        safe = jnp.where(some, total, 1.0)
        final[h, dec_rows, :] = value / safe
        lse[h, dec_rows, :] = jnp.where(some, after + jnp.log2(safe), NEG)

    row = rows_of((16, HD))
    diagonal = (row == lanes((16, HD))) & (row < FEW)
    ffn = out_ref.shape[0] // (TOKENS // QUARTER)
    for q in range(TOKENS // QUARTER):
        for h in range(GH):
            for b in range(QUARTER // FEW):
                part = pl.ds(q * QUARTER + b * FEW, 16)
                stat = jnp.sum(jnp.where(diagonal, lse[h, part, :], 0.0), axis=0, keepdims=True)
                high, middle, low = split3(stat)
                block = jnp.where(row < FEW, final[h, part, :], 0.0)
                block = jnp.where(row == FEW, high, block)
                block = jnp.where(row == FEW + 1, middle, block)
                block = jnp.where(row == FEW + 2, low, block)
                out_ref[q * ffn + h * (QUARTER // FEW) + b] = block.astype(BF16)
        for target in range(GH * (QUARTER // FEW), ffn):
            out_ref[q * ffn + target] = jnp.zeros((16, HD), BF16)


def merge_kernel(in_ref, out_ref):
    sources = out_ref.shape[0]
    groups = in_ref.shape[0] // sources
    row = rows_of((16, HD))
    all_weights = []
    for g in range(groups):
        stats = jnp.concatenate(
            [
                jnp.sum(
                    jnp.where(row >= FEW, in_ref[g * sources + s].astype(F32), 0.0),
                    axis=0,
                    keepdims=True,
                )
                for s in range(sources)
            ],
            axis=0,
        )
        weights = jnp.exp2(stats - jnp.max(stats, axis=0, keepdims=True))
        all_weights.append(weights / jnp.sum(weights, axis=0, keepdims=True))
    turned = jnp.transpose(jnp.concatenate(all_weights, axis=0))
    pieces = []
    for g in range(groups):
        total = jnp.zeros((16, HD), F32)
        for s in range(sources):
            source = g * sources + s
            total = total + turned[:16, source : source + 1] * in_ref[source].astype(F32)
        pieces.append(total[:FEW])
    result = jnp.concatenate(pieces, axis=0).astype(BF16)
    for s in range(sources):
        out_ref[s] = result


def output_kernel(g_ref, f_ref, in_ref, x_ref, *refs):
    *w_refs, own_ref, out_ref, spread, heads, product = refs
    blocks = QUARTER // FEW
    groups = len(w_refs)
    for source in range(GH * blocks):
        spread[source, :ROWS, :] = in_ref[source].astype(F32)
        spread[source, ROWS:, :] = jnp.zeros((16, HD), F32)
    for g in range(groups):
        for h in range(GH):
            for b in range(blocks):
                heads[g, b * 16 : (b + 1) * 16, h * HD : (h + 1) * HD] = spread[
                    h * blocks + b, g * FEW : g * FEW + 16, :
                ].astype(BF16)
    attended = jnp.zeros((16 * blocks, COLS), F32)
    for s in range(groups):
        source = lax.rem(g_ref[0] + groups - s, groups)
        attended = attended + turned_dot(heads[source], w_refs[s][...])
    for b in range(blocks):
        product[b * FEW : (b + 1) * FEW, :] = attended[b * 16 : b * 16 + FEW]
    x = x_ref[...].astype(F32)
    own = jnp.zeros((QUARTER, COLS), F32)
    for i in range(groups):
        own = jnp.where(g_ref[0] == i, x[i * QUARTER : (i + 1) * QUARTER], own)
    own = (own + product[...]).astype(BF16)
    own_ref[...] = own
    message = turned_lanes(packed(own.astype(F32)), lax.rem(f_ref[0], 4)).astype(BF16)
    for s in range(out_ref.shape[0]):
        out_ref[s] = message


def packed(value):
    third = QUARTER // 3
    tail = value[:, HD:]
    extra = jnp.concatenate(
        [tail[i * third : (i + 1) * third] for i in range(3)]
        + [jnp.zeros((third, HD - 3 * (COLS - HD)), F32)],
        axis=1,
    )
    return jnp.concatenate([value[:, :HD], extra], axis=0)


def unpacked(message):
    third = QUARTER // 3
    wide = COLS - HD
    extra = message[QUARTER:]
    tail = jnp.concatenate([extra[:, i * wide : (i + 1) * wide] for i in range(3)], axis=0)
    assert tail.shape == (3 * third, wide)
    return jnp.concatenate([message[:QUARTER], tail], axis=1)


def turned_dot(left, right):
    return lax.dot_general(left, right, (((1,), (1,)), ((), ())), preferred_element_type=F32)


def turned_lanes(message, amount):
    result = message
    for j in range(1, 4):
        result = jnp.where(amount == j, pltpu.roll(message, 32 * j, 1), result)
    return result


def tiles_of(messages):
    third = QUARTER // 3
    lane = lanes((QUARTER, HD))
    heads = [m[:QUARTER] for m in messages]
    tails = [
        jnp.concatenate(
            [m[QUARTER:]] + [pltpu.roll(m[QUARTER:], HD - 32 * i, 1) for i in (1, 2)], axis=0
        )
        for m in messages
    ]
    assert tails[0].shape == (3 * third, HD)
    result = [heads[0]]
    for k in range(1, 5):
        tile = jnp.where(lane >= 32 * (k - 1), tails[k - 1], heads[k - 1])
        result.append(jnp.where(lane >= 32 * k, heads[k], tile) if k < 4 else tile)
    return result


def messages_of(product):
    third = QUARTER // 3
    lane = lanes((QUARTER, HD))
    slot = lanes((third, HD)) >> 5
    tiles = [product[:, k * HD : (k + 1) * HD] for k in range(5)]
    result = []
    for j in range(4):
        head = jnp.where(lane >= 32 * j, tiles[j], tiles[j + 1]) if j else tiles[0]
        extra = jnp.zeros((third, HD), F32)
        for i in range(3):
            piece = tiles[j + 1][i * third : (i + 1) * third]
            piece = pltpu.roll(piece, 32 * i, 1) if i else piece
            extra = jnp.where(slot == (i + j) % 4, piece, extra)
        result.append(jnp.concatenate([head, extra], axis=0).astype(BF16))
    return result


def ffn_kernel(f_ref, mine_ref, theirs_ref, gain_ref, gate_hbm, down_hbm, *refs):
    ahead, (out_ref, rows, normed, gates, down, hidden, sems) = refs[:AHEAD], refs[AHEAD:]
    copies = []
    for c in range(AHEAD, D // FCHUNK):
        part = pl.ds(c * FCHUNK, FCHUNK)
        copies.append(
            pltpu.make_async_copy(gate_hbm.at[:, :, part], gates.at[:, :, part], sems.at[c])
        )
    copies.append(pltpu.make_async_copy(down_hbm, down, sems.at[D // FCHUNK]))
    for copy in copies:
        copy.start()
    odd = lax.rem(f_ref[0], 2) == 1
    for s in range(0, 2 * mine_ref.shape[0], 4):
        messages = []
        for j in range(4):
            place = (s + j) // 2
            mine = mine_ref[place].astype(F32)
            theirs = theirs_ref[place].astype(F32)
            messages.append(
                jnp.where(odd, mine, theirs) if j % 2 else jnp.where(odd, theirs, mine)
            )
        for k, tile in enumerate(tiles_of(messages)):
            at = s * COLS + k * HD
            rows[:, at : at + HD] = tile
    full = rows[...]
    inverse = lax.rsqrt(jnp.sum(full * full, axis=1, keepdims=True) / D + EPS)
    normed[...] = (full * inverse * gain_ref[...]).astype(BF16)
    gate = jnp.zeros((QUARTER, down.shape[0]), F32)
    up = jnp.zeros((QUARTER, down.shape[0]), F32)
    for c in range(D // FCHUNK):
        part = pl.ds(c * FCHUNK, FCHUNK)
        block = normed[:, part]
        if c < AHEAD:
            both = ahead[c][0], ahead[c][1]
        else:
            copies[c - AHEAD].wait()
            both = gates[0, :, part], gates[1, :, part]
        gate = gate + turned_dot(block, both[0])
        up = up + turned_dot(block, both[1])
    hidden[...] = (gate / (1.0 + jnp.exp(-gate)) * up).astype(BF16)
    copies[-1].wait()
    wide = 4 * COLS
    for s in range(out_ref.shape[0] // 4):
        product = jnp.dot(
            hidden[...], down[:, s * wide : (s + 1) * wide], preferred_element_type=F32
        )
        for j, message in enumerate(messages_of(product)):
            out_ref[4 * s + j] = message


def finish_kernel(f_ref, in_ref, own_ref, out_ref):
    total = in_ref[0].astype(F32)
    for s in range(1, in_ref.shape[0]):
        total = total + in_ref[s].astype(F32)
    total = turned_lanes(total, lax.rem(4 - lax.rem(f_ref[0], 4), 4))
    out_ref[...] = (own_ref[...].astype(F32) + unpacked(total)).astype(BF16)


def fetch_kernel(in_ref, *refs):
    *targets, sems = refs
    copies = [
        pltpu.make_async_copy(in_ref.at[:, :, pl.ds(c * FCHUNK, FCHUNK)], target, sems.at[c])
        for c, target in enumerate(targets)
    ]
    for copy in copies:
        copy.start()
    for copy in copies:
        copy.wait()


def fetched(gate_up):
    out = tuple(shape(*gate_up.shape[:2], FCHUNK) for _ in range(AHEAD))
    return call(
        fetch_kernel,
        out,
        [hbm],
        [pltpu.SemaphoreType.DMA((AHEAD,))],
        out_specs=(vmem,) * AHEAD,
    )(gate_up)


def call(kernel, out, specs, scratch=(), out_specs=None):
    function = pl.pallas_call(
        kernel,
        out_shape=out,
        in_specs=specs,
        out_specs=out_specs if out_specs is not None else vmem,
        scratch_shapes=list(scratch),
        compiler_params=params(),
    )

    def placed(*args):
        return function(
            *[
                pltpu.with_memory_space_constraint(a, pltpu.HBM) if spec is hbm else a
                for a, spec in zip(args, specs)
            ]
        )

    return placed


def shape(*dims, kind=BF16):
    return jax.ShapeDtypeStruct(dims, kind)


def swap(value, axis):
    return lax.all_to_all(value, axis, 0, 0)


def tables(f, span_offsets, decode_lengths):
    within = jnp.arange(SPAN, dtype=jnp.int32)
    prefill = (span_offsets[:, None] + within[None, :]).reshape(PRE * SPAN)
    positions = jnp.concatenate([prefill, decode_lengths])
    block = lax.rem(f, TOKENS // ROWS)
    positions = lax.dynamic_slice_in_dim(positions, block * ROWS, ROWS)
    half_width = HD // 2
    lane = jnp.arange(HD, dtype=jnp.int32)
    frequency = jnp.exp((lane % half_width).astype(F32) * (-2.0 * math.log(10000.0) / HD))
    angles = positions.astype(F32)[:, None] * frequency[None, :]
    sine = jnp.sin(angles) * jnp.where(lane < half_width, -1.0, 1.0)[None, :]
    return jnp.cos(angles), sine


def run_attention(
    lists, lefts, tokens, f1, fresh, own_block, key_cache, value_cache, grp, ffn
):
    pages = key_cache.shape[0]
    units = PRE * GH
    return call(
        attention_kernel,
        shape(grp * ffn, 16, HD),
        [smem] * 4 + [vmem] * 2 + [hbm] * 2,
        [
            pltpu.VMEM((pages, PAGE, GH * HD), BF16),
            pltpu.VMEM((pages, PAGE, GH * HD), BF16),
            pltpu.SemaphoreType.DMA((2, CHUNKS)),
            pltpu.VMEM((pages // 2 + 1, GH, SPAN, 2 * PAGE), F32),
            pltpu.VMEM((units, SPAN, PAGE), F32),
            pltpu.VMEM((units, SPAN, 2 * HD), F32),
            pltpu.VMEM((GH, DEC, HD), F32),
            pltpu.VMEM((DEC, 8, HD), F32),
            pltpu.VMEM((DEC, 8, HD), F32),
            pltpu.VMEM((DEC, 8, GH * HD), F32),
            pltpu.VMEM((GH, TOKENS + 16, HD), F32),
            pltpu.VMEM((GH, TOKENS + 16, HD), F32),
        ],
    )(lists, lefts, tokens, f1, fresh, own_block, key_cache, value_cache)


def run_ffn(f1, mine, theirs, gain, gate_up, down, ahead):
    hidden_units = down.shape[0]
    return call(
        ffn_kernel,
        shape(2 * mine.shape[0], MSG, HD),
        [smem] + [vmem] * 3 + [hbm] * 2 + [vmem] * AHEAD,
        [
            pltpu.VMEM((QUARTER, D), F32),
            pltpu.VMEM((QUARTER, D), BF16),
            pltpu.VMEM((2, hidden_units, D), BF16),
            pltpu.VMEM((hidden_units, D), BF16),
            pltpu.VMEM((QUARTER, hidden_units), BF16),
            pltpu.SemaphoreType.DMA((D // FCHUNK + 1,)),
        ],
    )(f1, mine, theirs, gain, gate_up, down, *ahead)


def shards(
    layer_input,
    norm_gain,
    qkv_weight,
    key_cache,
    value_cache,
    out_weight,
    ffn_gain,
    gate_up_weight,
    down_weight,
    span_offsets,
    decode_lengths,
    page_table,
):
    ffn = lax.axis_size("ffn")
    grp = lax.axis_size("grp")
    f = lax.axis_index("ffn")
    g = lax.axis_index("grp")
    f1 = f.astype(jnp.int32).reshape(1)
    g1 = g.astype(jnp.int32).reshape(1)
    pages = key_cache.shape[0]

    parity = [[2 * i + c for i in range(ffn // 2)] for c in range(2)]
    neighbour = [(i, i ^ 1) for i in range(ffn)]

    def projected(which):
        return call(
            project_kernel,
            shape(ffn // 2, 3 * ROWS + STATS, HD),
            [smem, hbm, hbm, hbm],
            [
                pltpu.VMEM((COLS, TOKENS), BF16),
                pltpu.VMEM((1, COLS), F32),
                pltpu.VMEM(qkv_weight.shape, BF16),
                pltpu.VMEM((TOKENS, COLS), F32),
                pltpu.SemaphoreType.DMA((5,)),
            ],
        )(which, layer_input.T, norm_gain.reshape(1, -1), qkv_weight)

    core = lax.rem(f1, 2)
    sent = projected(1 - core)
    core, sent, page_table = lax.optimization_barrier((core, sent, page_table))
    received = lax.ppermute(sent, "ffn", neighbour)
    partial = call(add_kernel, shape(*sent.shape), [vmem] * 2)(projected(core), received)
    span_rows, partial = lax.optimization_barrier((span_offsets, partial))
    cosine, sine = tables(f, span_rows, decode_lengths)
    local_ids = f * pages + jnp.arange(pages, dtype=jnp.int32)
    requests = PRE + DEC
    numbers = jnp.arange(requests * MAXP, dtype=jnp.int32).reshape(requests, MAXP) + 1
    codes = jnp.sum(
        jnp.where(page_table[None] == local_ids[:, None, None], numbers[None], 0), axis=(1, 2)
    )
    prefixes = jnp.concatenate([span_offsets, decode_lengths])
    owners = (codes - 1) >> 7
    lefts = jnp.sum(
        jnp.where(owners[:, None] == jnp.arange(requests)[None], prefixes[None], 0), axis=1
    )
    lefts = jnp.clip(lefts - ((codes - 1) & 127) * PAGE, 0, PAGE)
    kinds = jnp.where((codes > 0) & (lefts > 0), jnp.minimum(owners, PRE), PRE + 1)
    order = jnp.arange(pages, dtype=jnp.int32)
    same = kinds[:, None] == kinds[None, :]
    rank = jnp.sum(jnp.where(same & (order[None, :] < order[:, None]), 1, 0), axis=1)
    of_kind = kinds[None, :] == jnp.arange(PRE + 1, dtype=jnp.int32)[:, None]
    place = jnp.where(of_kind, rank[None, :], -1)
    lists = jnp.sum(
        jnp.where(place[:, None, :] == order[None, :, None], order[None, None, :], 0), axis=2
    )
    bound = jnp.arange(CHUNKS + 1, dtype=jnp.int32) * (pages // CHUNKS)
    here = of_kind[:, None, :] & (order[None, None, :] < bound[None, :, None])
    counts = jnp.sum(here.astype(jnp.int32), axis=2)
    last = jnp.arange(CHUNKS + 1) == CHUNKS
    lists = jnp.concatenate(
        [lists, counts[:, CHUNKS:], (counts + last[None].astype(jnp.int32)) >> 1], axis=1
    )
    tokens = jnp.clip(owners - PRE, 0, DEC - 1)

    turned_weight, cosine = lax.optimization_barrier((out_weight.T, cosine))
    def passed(weight, amount):
        return lax.ppermute(weight, "grp", [(i, (i + amount) % grp) for i in range(grp)])

    near = [passed(turned_weight, 1), passed(turned_weight, grp - 1)]
    partial = lax.all_to_all(partial, "ffn", 0, 0, axis_index_groups=parity)
    partial, *near = lax.optimization_barrier((partial, *near))
    fresh, own_block = call(
        rotate_kernel,
        (shape(ffn, ROWS, HD), shape(2, ROWS, HD)),
        [vmem] * 3,
        out_specs=(vmem, vmem),
    )(partial, cosine, sine)
    middle = []
    for _ in range(2, grp - 1):
        last, own_block = lax.optimization_barrier((middle[-1] if middle else near[0], own_block))
        middle.append(passed(last, 1))
    fresh = swap(fresh, "ffn").reshape(ffn * ROWS, HD)
    fresh, *middle = lax.optimization_barrier((fresh, *middle))
    message = run_attention(
        lists, lefts, tokens, f1, fresh, own_block, key_cache, value_cache, grp, ffn
    )
    message = swap(message, ("grp", "ffn"))
    heads = call(merge_kernel, shape(ffn, ROWS, HD), [vmem])(message)
    heads = swap(heads, "ffn")
    out_weights = [turned_weight, near[0], *middle, near[1]]
    own, rows = call(
        output_kernel,
        (shape(QUARTER, COLS), shape(ffn // 2, MSG, HD)),
        [smem] * 2 + [vmem] * (2 + grp),
        [
            pltpu.VMEM((GH * (QUARTER // FEW), ROWS + 16, HD), F32),
            pltpu.VMEM((grp, 16 * (QUARTER // FEW), GH * HD), BF16),
            pltpu.VMEM((QUARTER, COLS), F32),
        ],
        out_specs=(vmem, vmem),
    )(g1, f1, heads, layer_input, *out_weights)
    gate_up, rows = lax.optimization_barrier((jnp.swapaxes(gate_up_weight, 1, 2), rows))
    mine = lax.all_to_all(rows, "ffn", 0, 0, axis_index_groups=parity)
    ahead = fetched(gate_up)
    theirs = lax.ppermute(mine, "ffn", neighbour)
    down_terms = run_ffn(
        f1, mine, theirs, ffn_gain.reshape(1, -1), gate_up, down_weight, ahead
    )
    down_terms = swap(down_terms, "ffn")
    return call(finish_kernel, shape(QUARTER, COLS), [smem] + [vmem] * 2)(f1, down_terms, own)


def solution(mesh):
    in_specs = (
        P(None, "ffn"),
        P("ffn"),
        P(None, "ffn", "grp"),
        P("ffn", None, "grp"),
        P("ffn", None, "grp"),
        P("grp", "ffn"),
        P(),
        P(None, None, "ffn"),
        P("ffn", None),
        P(),
        P(),
        P(),
    )
    out_specs = P("grp", "ffn")
    return jax.shard_map(shards, mesh=mesh, in_specs=in_specs, out_specs=out_specs, check_vma=False)
```

```python
import functools
import math

import jax
import jax.numpy as jnp
from jax import lax
from jax.experimental import pallas as pl
from jax.experimental.pallas import tpu as pltpu
from jax.sharding import PartitionSpec as P

D = 5120
HD = 128
PAGE = 128
SPAN = 128
PRE = 2
DEC = 32
MAXP = 128
TOKENS = 288
GH = 5
ROWS = 48
QUARTER = 72
COLS = 160
MSG = 96
FEW = 12
STATS = 8

EPS = 1e-05
NEG = -1e30
SCALE2 = HD ** (-0.5) * math.log2(math.e)
F32 = jnp.float32
BF16 = jnp.bfloat16
LIMIT = 32 << 20
GROUP = 4
CHUNKS = 4
FCHUNK = 640
AHEAD = 3

vmem = pl.BlockSpec(memory_space=pltpu.VMEM)
smem = pl.BlockSpec(memory_space=pltpu.SMEM)
hbm = pl.BlockSpec(memory_space=pl.ANY)


def params():
    return pltpu.CompilerParams(vmem_limit_bytes=LIMIT)


def lanes(shape):
    return lax.broadcasted_iota(jnp.int32, shape, len(shape) - 1)


def rows_of(shape):
    return lax.broadcasted_iota(jnp.int32, shape, len(shape) - 2)


def split3(value):
    high = value.astype(BF16).astype(F32)
    rest = value - high
    middle = rest.astype(BF16).astype(F32)
    return high, middle, rest - middle


def stat_block(stat):
    row = rows_of((STATS, HD))
    high, middle, low = split3(stat)
    return jnp.where(
        row == 0, high, jnp.where(row == 1, middle, jnp.where(row == 2, low, 0.0))
    ).astype(BF16)


def project_kernel(
    p_ref, x_hbm, gain_hbm, w_hbm, out_ref, x_vmem, gain_ref, w_vmem, x_rows, sems
):
    copies = [pltpu.make_async_copy(x_hbm, x_vmem, sems.at[3])]
    gain_copy = pltpu.make_async_copy(gain_hbm, gain_ref, sems.at[4])
    gain_copy.start()
    for k in range(3):
        copies.append(pltpu.make_async_copy(w_hbm.at[k], w_vmem.at[k], sems.at[k]))
    for copy in copies:
        copy.start()
    copies[0].wait()
    gain_copy.wait()
    x_rows[...] = jnp.transpose(x_vmem[...].astype(F32))
    half = TOKENS // ROWS // 2
    x = jnp.concatenate(
        [
            x_rows[pl.ds(pl.multiple_of((2 * i + p_ref[0]) * ROWS, 16), ROWS), :]
            for i in range(half)
        ],
        axis=0,
    )
    scaled = (x * gain_ref[...]).astype(BF16)
    squares = jnp.sum(x * x, axis=1, keepdims=True)
    diagonal = rows_of((ROWS, HD)) == lanes((ROWS, HD))
    for i in range(half):
        part = jnp.broadcast_to(squares[i * ROWS : (i + 1) * ROWS], (ROWS, HD))
        stat = jnp.sum(jnp.where(diagonal, part, 0.0), axis=0, keepdims=True)
        block = stat_block(stat)
        for h in range(GH):
            out_ref[h * half + i, 3 * ROWS :, :] = block
    for k in range(3):
        copies[1 + k].wait()
        product = jnp.dot(scaled, w_vmem[k], preferred_element_type=F32).astype(BF16)
        for h in range(GH):
            for i in range(half):
                out_ref[h * half + i, k * ROWS : (k + 1) * ROWS, :] = product[
                    i * ROWS : (i + 1) * ROWS, h * HD : (h + 1) * HD
                ]
    for target in range(GH * half, out_ref.shape[0]):
        out_ref[target] = jnp.zeros(out_ref.shape[1:], BF16)


def add_kernel(left_ref, right_ref, out_ref):
    for i in range(out_ref.shape[0]):
        total = left_ref[i].astype(F32) + right_ref[i].astype(F32)
        stat = jnp.sum(total[3 * ROWS :], axis=0, keepdims=True)
        out_ref[i, : 3 * ROWS, :] = total[: 3 * ROWS].astype(BF16)
        out_ref[i, 3 * ROWS :, :] = stat_block(stat)


def rotate_kernel(in_ref, cos_ref, sin_ref, out_ref, own_ref):
    total = in_ref[0].astype(F32)
    for s in range(1, in_ref.shape[0]):
        total = total + in_ref[s].astype(F32)
    diagonal = rows_of((ROWS, HD)) == lanes((ROWS, HD))
    stat = jnp.sum(total[3 * ROWS :], axis=0, keepdims=True)
    squares = jnp.sum(
        jnp.where(diagonal, jnp.broadcast_to(stat, (ROWS, HD)), 0.0), axis=1, keepdims=True
    )
    inverse = lax.rsqrt(squares / D + EPS)

    def rotated(value):
        value = value * inverse
        turned = jnp.concatenate([value[:, HD // 2 :], value[:, : HD // 2]], axis=1)
        return (value * cos_ref[...] + turned * sin_ref[...]).astype(BF16)

    own_ref[0] = rotated(total[ROWS : 2 * ROWS])
    own_ref[1] = (total[2 * ROWS : 3 * ROWS] * inverse).astype(BF16)
    query = rotated(total[:ROWS])
    for s in range(out_ref.shape[0]):
        out_ref[s] = query


def attention_kernel(
    lists,
    left_ref,
    token_ref,
    f_ref,
    fresh_ref,
    own_ref,
    key_hbm,
    value_hbm,
    out_ref,
    keys,
    values,
    sems,
    scores,
    peak,
    summed,
    dec_query,
    dec_peak,
    dec_total,
    dec_sum,
    final,
    lse,
):
    pages = key_hbm.shape[0]
    step = pages // CHUNKS
    parts = [pl.ds(c * step, step) for c in range(CHUNKS)]
    copies = [
        pltpu.make_async_copy(key_hbm.at[part], keys.at[part], sems.at[0, c])
        for c, part in enumerate(parts)
    ] + [
        pltpu.make_async_copy(value_hbm.at[part], values.at[part], sems.at[1, c])
        for c, part in enumerate(parts)
    ]
    for copy in copies:
        copy.start()

    peak[...] = jnp.full(peak.shape, NEG, F32)
    summed[...] = jnp.zeros(summed.shape, F32)
    dec_peak[...] = jnp.full(dec_peak.shape, NEG, F32)
    dec_total[...] = jnp.zeros(dec_total.shape, F32)
    dec_sum[...] = jnp.zeros(dec_sum.shape, F32)
    final[:, TOKENS:, :] = jnp.zeros((GH, 16, HD), F32)
    lse[:, TOKENS:, :] = jnp.zeros((GH, 16, HD), F32)
    for h in range(GH):
        dec_query[h] = fresh_ref[h * TOKENS + PRE * SPAN : (h + 1) * TOKENS, :].astype(F32)

    n_pre = [lists[k, pages] for k in range(PRE)]
    n_dec = lists[PRE, pages]
    pairs = [lists[k, pages + 1 + CHUNKS] for k in range(PRE)]

    f = f_ref[0]
    blocks = TOKENS // ROWS
    has_own = f < GH * blocks
    own_head = jnp.where(has_own, f // blocks, 0)
    own_block = jnp.where(has_own, f - own_head * blocks, 0)
    filler = jnp.zeros((PAGE - ROWS, HD), BF16)
    own_keys = jnp.concatenate([own_ref[0], filler], axis=0)
    own_values = jnp.concatenate([own_ref[1], filler], axis=0)
    own_token = own_block * ROWS + lanes((SPAN, PAGE))
    in_block = lanes((SPAN, PAGE)) < ROWS

    def query_rows(request, h):
        return fresh_ref[pl.ds(pl.multiple_of(h * TOKENS + request * SPAN, 16), SPAN), :]

    def scored(query, key):
        product = lax.dot_general(
            query, key, (((1,), (1,)), ((), ())), preferred_element_type=F32
        )
        return product * SCALE2

    def own_scores(request):
        within = own_token - request * SPAN
        visible = in_block & (within >= 0) & (within <= rows_of((SPAN, PAGE)))
        return jnp.where(visible, scored(query_rows(request, own_head), own_keys), NEG), visible

    @pl.when(has_own)
    def _():
        for request in range(PRE):
            unit = request * GH + own_head
            peak[unit] = jnp.maximum(peak[unit], own_scores(request)[0])

    def pair(request, i):
        last = n_pre[request] - 1
        first_page = lists[request, 2 * i]
        second_page = lists[request, jnp.minimum(2 * i + 1, last)]
        return first_page, second_page

    def joined(ref, pages_of, h):
        return jnp.concatenate([ref[p, :, h * HD : (h + 1) * HD] for p in pages_of], axis=0)

    wide_lane = lanes((SPAN, 2 * PAGE))
    def in_chunks(which, one_pass):
        def chunk(c, _):
            part = pl.ds(c * step, step)
            source, target = ((key_hbm, keys), (value_hbm, values))[which]
            pltpu.make_async_copy(source.at[part], target.at[part], sems.at[which, c]).wait()
            for request in range(PRE):
                lower = lists[request, pages + 1 + c]
                upper = lists[request, pages + 2 + c]
                lax.fori_loop(lower, upper, one_pass(request), 0)
            return 0

        lax.fori_loop(0, CHUNKS, chunk, 0)

    def first_pass(request):
        def one_pair(i, _):
            both = pair(request, i)
            left = left_ref[both[0]]
            other = jnp.where(2 * i + 1 < n_pre[request], left_ref[both[1]], 0) + PAGE
            visible = wide_lane < jnp.where(wide_lane < PAGE, left, other)
            for h in range(GH):
                result = scored(query_rows(request, h), joined(keys, both, h))
                result = jnp.where(visible, result, NEG)
                scores[i + request * pairs[0], h] = result
                unit = request * GH + h
                peak[unit] = jnp.maximum(
                    peak[unit], jnp.maximum(result[:, :PAGE], result[:, PAGE:])
                )
            return 0

        return one_pair

    in_chunks(0, first_pass)

    for unit in range(PRE * GH):
        peak[unit] = jnp.broadcast_to(
            jnp.max(peak[unit], axis=1, keepdims=True), (SPAN, SPAN)
        )

    def weigh(unit, weights, value):
        ones = jnp.ones((value.shape[0], HD), BF16)
        both = jnp.concatenate([value, ones], axis=1)
        summed[unit] += jnp.dot(weights.astype(BF16), both, preferred_element_type=F32)

    def second_pass(request):
        def one_pair(i, _):
            both = pair(request, i)
            for h in range(GH):
                unit = request * GH + h
                top = peak[unit]
                top = jnp.concatenate([top, top], axis=1)
                weights = jnp.exp2(scores[i + request * pairs[0], h] - top)
                weigh(unit, weights, joined(values, both, h))
            return 0

        return one_pair

    in_chunks(1, second_pass)

    @pl.when(has_own)
    def _():
        for request in range(PRE):
            unit = request * GH + own_head
            result, visible = own_scores(request)
            weigh(unit, jnp.where(visible, jnp.exp2(result - peak[unit]), 0.0), own_values)

    tall = (8 * GROUP, GROUP * PAGE)
    owner_row = rows_of(tall) >> 3

    def decode_pass(step_index, _):
        tokens, picked, queries = [], [], []
        limit = jnp.zeros(tall, jnp.int32)
        row = rows_of((8, HD))
        for j in range(GROUP):
            position = step_index * GROUP + j
            p = lists[PRE, jnp.minimum(position, n_dec - 1)]
            token = token_ref[p]
            left = jnp.where(position < n_dec, left_ref[p], 0)
            limit = jnp.where(owner_row == j, j * PAGE + left, limit)
            tokens.append(token)
            picked.append(p)
            queries.append(
                jnp.concatenate(
                    [
                        jnp.where(
                            row == h,
                            jnp.broadcast_to(dec_query[h, pl.ds(token, 1), :], (8, HD)),
                            0.0,
                        )
                        for h in range(GH)
                    ],
                    axis=1,
                )
            )
        query = jnp.concatenate(queries, axis=0).astype(BF16)
        many_keys = jnp.concatenate([keys[p] for p in picked], axis=0)
        many_values = jnp.concatenate([values[p] for p in picked], axis=0)
        visible = (lanes(tall) >= owner_row * PAGE) & (lanes(tall) < limit)
        result = jnp.where(visible, scored(query, many_keys), NEG)
        tops = jnp.max(result, axis=1, keepdims=True)
        weights = jnp.where(visible, jnp.exp2(result - tops), 0.0)
        totals = jnp.sum(weights, axis=1, keepdims=True)
        products = jnp.dot(weights.astype(BF16), many_values, preferred_element_type=F32)
        found = [
            (
                tokens[j],
                tops[8 * j : 8 * j + 8],
                totals[8 * j : 8 * j + 8],
                products[8 * j : 8 * j + 8],
            )
            for j in range(GROUP)
        ]
        for token, top, total, product in found:
            before = dec_peak[token]
            after = jnp.maximum(before, top)
            keep = jnp.exp2(before - after)
            take = jnp.exp2(top - after)
            dec_peak[token] = after
            dec_total[token] = dec_total[token] * keep + total * take
            wide = jnp.concatenate([keep] * GH, axis=1)
            wide_take = jnp.concatenate([take] * GH, axis=1)
            dec_sum[token] = dec_sum[token] * wide + product * wide_take
        return 0

    lax.fori_loop(0, (n_dec + GROUP - 1) // GROUP, decode_pass, 0)

    for request in range(PRE):
        for h in range(GH):
            unit = request * GH + h
            total = summed[unit, :, HD:]
            some = total > 0.0
            safe = jnp.where(some, total, 1.0)
            part = pl.ds(request * SPAN, SPAN)
            final[h, part, :] = summed[unit, :, :HD] / safe
            lse[h, part, :] = jnp.where(some, peak[unit] + jnp.log2(safe), NEG)

    first = ROWS - DEC
    dec_rows = pl.ds(PRE * SPAN, DEC)
    for h in range(GH):
        mine = f == h * blocks + blocks - 1
        own = jnp.sum(dec_query[h] * own_ref[0].astype(F32)[first:], axis=1, keepdims=True)
        own = jnp.where(mine, jnp.broadcast_to(own, (DEC, HD)) * SCALE2, NEG)
        before = dec_peak[:, h, :]
        after = jnp.maximum(before, own)
        keep = jnp.exp2(before - after)
        take = jnp.where(mine, jnp.exp2(own - after), 0.0)
        total = dec_total[:, h, :] * keep + take
        value = dec_sum[:, h, h * HD : (h + 1) * HD] * keep
        value = value + take * own_ref[1].astype(F32)[first:]
        some = total > 0.0
        safe = jnp.where(some, total, 1.0)
        final[h, dec_rows, :] = value / safe
        lse[h, dec_rows, :] = jnp.where(some, after + jnp.log2(safe), NEG)

    row = rows_of((16, HD))
    diagonal = (row == lanes((16, HD))) & (row < FEW)
    ffn = out_ref.shape[0] // (TOKENS // QUARTER)
    for q in range(TOKENS // QUARTER):
        for h in range(GH):
            for b in range(QUARTER // FEW):
                part = pl.ds(q * QUARTER + b * FEW, 16)
                stat = jnp.sum(jnp.where(diagonal, lse[h, part, :], 0.0), axis=0, keepdims=True)
                high, middle, low = split3(stat)
                block = jnp.where(row < FEW, final[h, part, :], 0.0)
                block = jnp.where(row == FEW, high, block)
                block = jnp.where(row == FEW + 1, middle, block)
                block = jnp.where(row == FEW + 2, low, block)
                out_ref[q * ffn + h * (QUARTER // FEW) + b] = block.astype(BF16)
        for target in range(GH * (QUARTER // FEW), ffn):
            out_ref[q * ffn + target] = jnp.zeros((16, HD), BF16)


def merge_kernel(in_ref, out_ref):
    sources = out_ref.shape[0]
    groups = in_ref.shape[0] // sources
    row = rows_of((16, HD))
    all_weights = []
    for g in range(groups):
        stats = jnp.concatenate(
            [
                jnp.sum(
                    jnp.where(row >= FEW, in_ref[g * sources + s].astype(F32), 0.0),
                    axis=0,
                    keepdims=True,
                )
                for s in range(sources)
            ],
            axis=0,
        )
        weights = jnp.exp2(stats - jnp.max(stats, axis=0, keepdims=True))
        all_weights.append(weights / jnp.sum(weights, axis=0, keepdims=True))
    turned = jnp.transpose(jnp.concatenate(all_weights, axis=0))
    pieces = []
    for g in range(groups):
        total = jnp.zeros((16, HD), F32)
        for s in range(sources):
            source = g * sources + s
            total = total + turned[:16, source : source + 1] * in_ref[source].astype(F32)
        pieces.append(total[:FEW])
    result = jnp.concatenate(pieces, axis=0).astype(BF16)
    for s in range(sources):
        out_ref[s] = result


def output_kernel(g_ref, f_ref, in_ref, x_ref, *refs):
    *w_refs, own_ref, out_ref, spread, heads, product = refs
    blocks = QUARTER // FEW
    groups = len(w_refs)
    for source in range(GH * blocks):
        spread[source, :ROWS, :] = in_ref[source].astype(F32)
        spread[source, ROWS:, :] = jnp.zeros((16, HD), F32)
    for g in range(groups):
        for h in range(GH):
            for b in range(blocks):
                heads[g, b * 16 : (b + 1) * 16, h * HD : (h + 1) * HD] = spread[
                    h * blocks + b, g * FEW : g * FEW + 16, :
                ].astype(BF16)
    attended = jnp.zeros((16 * blocks, COLS), F32)
    for s in range(groups):
        source = lax.rem(g_ref[0] + groups - s, groups)
        attended = attended + turned_dot(heads[source], w_refs[s][...])
    for b in range(blocks):
        product[b * FEW : (b + 1) * FEW, :] = attended[b * 16 : b * 16 + FEW]
    x = x_ref[...].astype(F32)
    own = jnp.zeros((QUARTER, COLS), F32)
    for i in range(groups):
        own = jnp.where(g_ref[0] == i, x[i * QUARTER : (i + 1) * QUARTER], own)
    own = (own + product[...]).astype(BF16)
    own_ref[...] = own
    message = turned_lanes(packed(own.astype(F32)), lax.rem(f_ref[0], 4)).astype(BF16)
    for s in range(out_ref.shape[0]):
        out_ref[s] = message


def packed(value):
    third = QUARTER // 3
    tail = value[:, HD:]
    extra = jnp.concatenate(
        [tail[i * third : (i + 1) * third] for i in range(3)]
        + [jnp.zeros((third, HD - 3 * (COLS - HD)), F32)],
        axis=1,
    )
    return jnp.concatenate([value[:, :HD], extra], axis=0)


def unpacked(message):
    third = QUARTER // 3
    wide = COLS - HD
    extra = message[QUARTER:]
    tail = jnp.concatenate([extra[:, i * wide : (i + 1) * wide] for i in range(3)], axis=0)
    assert tail.shape == (3 * third, wide)
    return jnp.concatenate([message[:QUARTER], tail], axis=1)


def turned_dot(left, right):
    return lax.dot_general(left, right, (((1,), (1,)), ((), ())), preferred_element_type=F32)


def turned_lanes(message, amount):
    result = message
    for j in range(1, 4):
        result = jnp.where(amount == j, pltpu.roll(message, 32 * j, 1), result)
    return result


def tiles_of(messages):
    third = QUARTER // 3
    lane = lanes((QUARTER, HD))
    heads = [m[:QUARTER] for m in messages]
    tails = [
        jnp.concatenate(
            [m[QUARTER:]] + [pltpu.roll(m[QUARTER:], HD - 32 * i, 1) for i in (1, 2)], axis=0
        )
        for m in messages
    ]
    assert tails[0].shape == (3 * third, HD)
    result = [heads[0]]
    for k in range(1, 5):
        tile = jnp.where(lane >= 32 * (k - 1), tails[k - 1], heads[k - 1])
        result.append(jnp.where(lane >= 32 * k, heads[k], tile) if k < 4 else tile)
    return result


def messages_of(product):
    third = QUARTER // 3
    lane = lanes((QUARTER, HD))
    slot = lanes((third, HD)) >> 5
    tiles = [product[:, k * HD : (k + 1) * HD] for k in range(5)]
    result = []
    for j in range(4):
        head = jnp.where(lane >= 32 * j, tiles[j], tiles[j + 1]) if j else tiles[0]
        extra = jnp.zeros((third, HD), F32)
        for i in range(3):
            piece = tiles[j + 1][i * third : (i + 1) * third]
            piece = pltpu.roll(piece, 32 * i, 1) if i else piece
            extra = jnp.where(slot == (i + j) % 4, piece, extra)
        result.append(jnp.concatenate([head, extra], axis=0).astype(BF16))
    return result


def ffn_kernel(f_ref, mine_ref, theirs_ref, gain_ref, gate_hbm, down_hbm, *refs):
    ahead, refs = refs[:AHEAD], refs[AHEAD:]
    keep_ref, send_ref, rows, normed, gates, down, hidden, sems = refs
    copies = []
    for c in range(AHEAD, D // FCHUNK):
        part = pl.ds(c * FCHUNK, FCHUNK)
        copies.append(
            pltpu.make_async_copy(gate_hbm.at[:, :, part], gates.at[:, :, part], sems.at[c])
        )
    copies.append(pltpu.make_async_copy(down_hbm, down, sems.at[D // FCHUNK]))
    for copy in copies:
        copy.start()
    odd = lax.rem(f_ref[0], 2) == 1
    for s in range(0, 2 * mine_ref.shape[0], 4):
        messages = []
        for j in range(4):
            place = (s + j) // 2
            mine = mine_ref[place].astype(F32)
            theirs = theirs_ref[place].astype(F32)
            messages.append(
                jnp.where(odd, mine, theirs) if j % 2 else jnp.where(odd, theirs, mine)
            )
        for k, tile in enumerate(tiles_of(messages)):
            at = s * COLS + k * HD
            rows[:, at : at + HD] = tile
    full = rows[...]
    inverse = lax.rsqrt(jnp.sum(full * full, axis=1, keepdims=True) / D + EPS)
    normed[...] = (full * inverse * gain_ref[...]).astype(BF16)
    gate = jnp.zeros((QUARTER, down.shape[0]), F32)
    up = jnp.zeros((QUARTER, down.shape[0]), F32)
    for c in range(D // FCHUNK):
        part = pl.ds(c * FCHUNK, FCHUNK)
        block = normed[:, part]
        if c < AHEAD:
            both = ahead[c][0], ahead[c][1]
        else:
            copies[c - AHEAD].wait()
            both = gates[0, :, part], gates[1, :, part]
        gate = gate + turned_dot(block, both[0])
        up = up + turned_dot(block, both[1])
    hidden[...] = (gate / (1.0 + jnp.exp(-gate)) * up).astype(BF16)
    copies[-1].wait()
    wide = 4 * COLS
    for s in range(keep_ref.shape[0] // 2):
        product = jnp.dot(
            hidden[...], down[:, s * wide : (s + 1) * wide], preferred_element_type=F32
        )
        messages = messages_of(product)
        for j in range(2):
            even, uneven = messages[2 * j], messages[2 * j + 1]
            keep_ref[2 * s + j] = jnp.where(odd, uneven, even)
            send_ref[2 * s + j] = jnp.where(odd, even, uneven)


def join_kernel(left_ref, right_ref, out_ref):
    for i in range(out_ref.shape[0]):
        out_ref[i] = (left_ref[i].astype(F32) + right_ref[i].astype(F32)).astype(BF16)


def finish_kernel(f_ref, in_ref, own_ref, out_ref):
    total = in_ref[0].astype(F32)
    for s in range(1, in_ref.shape[0]):
        total = total + in_ref[s].astype(F32)
    total = turned_lanes(total, lax.rem(4 - lax.rem(f_ref[0], 4), 4))
    out_ref[...] = (own_ref[...].astype(F32) + unpacked(total)).astype(BF16)


def fetch_kernel(in_ref, *refs):
    *targets, sems = refs
    copies = [
        pltpu.make_async_copy(in_ref.at[:, :, pl.ds(c * FCHUNK, FCHUNK)], target, sems.at[c])
        for c, target in enumerate(targets)
    ]
    for copy in copies:
        copy.start()
    for copy in copies:
        copy.wait()


def fetched(gate_up):
    out = tuple(shape(*gate_up.shape[:2], FCHUNK) for _ in range(AHEAD))
    return call(
        fetch_kernel,
        out,
        [hbm],
        [pltpu.SemaphoreType.DMA((AHEAD,))],
        out_specs=(vmem,) * AHEAD,
    )(gate_up)


def call(kernel, out, specs, scratch=(), out_specs=None):
    function = pl.pallas_call(
        kernel,
        out_shape=out,
        in_specs=specs,
        out_specs=out_specs if out_specs is not None else vmem,
        scratch_shapes=list(scratch),
        compiler_params=params(),
    )

    def placed(*args):
        return function(
            *[
                pltpu.with_memory_space_constraint(a, pltpu.HBM) if spec is hbm else a
                for a, spec in zip(args, specs)
            ]
        )

    return placed


def shape(*dims, kind=BF16):
    return jax.ShapeDtypeStruct(dims, kind)


def swap(value, axis):
    return lax.all_to_all(value, axis, 0, 0)


def tables(f, span_offsets, decode_lengths):
    within = jnp.arange(SPAN, dtype=jnp.int32)
    prefill = (span_offsets[:, None] + within[None, :]).reshape(PRE * SPAN)
    positions = jnp.concatenate([prefill, decode_lengths])
    block = lax.rem(f, TOKENS // ROWS)
    positions = lax.dynamic_slice_in_dim(positions, block * ROWS, ROWS)
    half_width = HD // 2
    lane = jnp.arange(HD, dtype=jnp.int32)
    frequency = jnp.exp((lane % half_width).astype(F32) * (-2.0 * math.log(10000.0) / HD))
    angles = positions.astype(F32)[:, None] * frequency[None, :]
    sine = jnp.sin(angles) * jnp.where(lane < half_width, -1.0, 1.0)[None, :]
    return jnp.cos(angles), sine


def run_attention(
    lists, lefts, tokens, f1, fresh, own_block, key_cache, value_cache, grp, ffn
):
    pages = key_cache.shape[0]
    units = PRE * GH
    return call(
        attention_kernel,
        shape(grp * ffn, 16, HD),
        [smem] * 4 + [vmem] * 2 + [hbm] * 2,
        [
            pltpu.VMEM((pages, PAGE, GH * HD), BF16),
            pltpu.VMEM((pages, PAGE, GH * HD), BF16),
            pltpu.SemaphoreType.DMA((2, CHUNKS)),
            pltpu.VMEM((pages // 2 + 1, GH, SPAN, 2 * PAGE), F32),
            pltpu.VMEM((units, SPAN, PAGE), F32),
            pltpu.VMEM((units, SPAN, 2 * HD), F32),
            pltpu.VMEM((GH, DEC, HD), F32),
            pltpu.VMEM((DEC, 8, HD), F32),
            pltpu.VMEM((DEC, 8, HD), F32),
            pltpu.VMEM((DEC, 8, GH * HD), F32),
            pltpu.VMEM((GH, TOKENS + 16, HD), F32),
            pltpu.VMEM((GH, TOKENS + 16, HD), F32),
        ],
    )(lists, lefts, tokens, f1, fresh, own_block, key_cache, value_cache)


def run_ffn(f1, mine, theirs, gain, gate_up, down, ahead):
    hidden_units = down.shape[0]
    return call(
        ffn_kernel,
        (shape(*mine.shape), shape(*mine.shape)),
        [smem] + [vmem] * 3 + [hbm] * 2 + [vmem] * AHEAD,
        [
            pltpu.VMEM((QUARTER, D), F32),
            pltpu.VMEM((QUARTER, D), BF16),
            pltpu.VMEM((2, hidden_units, D), BF16),
            pltpu.VMEM((hidden_units, D), BF16),
            pltpu.VMEM((QUARTER, hidden_units), BF16),
            pltpu.SemaphoreType.DMA((D // FCHUNK + 1,)),
        ],
        out_specs=(vmem, vmem),
    )(f1, mine, theirs, gain, gate_up, down, *ahead)


def shards(
    layer_input,
    norm_gain,
    qkv_weight,
    key_cache,
    value_cache,
    out_weight,
    ffn_gain,
    gate_up_weight,
    down_weight,
    span_offsets,
    decode_lengths,
    page_table,
):
    ffn = lax.axis_size("ffn")
    grp = lax.axis_size("grp")
    f = lax.axis_index("ffn")
    g = lax.axis_index("grp")
    f1 = f.astype(jnp.int32).reshape(1)
    g1 = g.astype(jnp.int32).reshape(1)
    pages = key_cache.shape[0]

    parity = [[2 * i + c for i in range(ffn // 2)] for c in range(2)]
    neighbour = [(i, i ^ 1) for i in range(ffn)]

    def projected(which):
        return call(
            project_kernel,
            shape(ffn // 2, 3 * ROWS + STATS, HD),
            [smem, hbm, hbm, hbm],
            [
                pltpu.VMEM((COLS, TOKENS), BF16),
                pltpu.VMEM((1, COLS), F32),
                pltpu.VMEM(qkv_weight.shape, BF16),
                pltpu.VMEM((TOKENS, COLS), F32),
                pltpu.SemaphoreType.DMA((5,)),
            ],
        )(which, layer_input.T, norm_gain.reshape(1, -1), qkv_weight)

    core = lax.rem(f1, 2)
    sent = projected(1 - core)
    core, sent, page_table = lax.optimization_barrier((core, sent, page_table))
    received = lax.ppermute(sent, "ffn", neighbour)
    partial = call(add_kernel, shape(*sent.shape), [vmem] * 2)(projected(core), received)
    span_rows, partial = lax.optimization_barrier((span_offsets, partial))
    cosine, sine = tables(f, span_rows, decode_lengths)
    local_ids = f * pages + jnp.arange(pages, dtype=jnp.int32)
    requests = PRE + DEC
    numbers = jnp.arange(requests * MAXP, dtype=jnp.int32).reshape(requests, MAXP) + 1
    codes = jnp.sum(
        jnp.where(page_table[None] == local_ids[:, None, None], numbers[None], 0), axis=(1, 2)
    )
    prefixes = jnp.concatenate([span_offsets, decode_lengths])
    owners = (codes - 1) >> 7
    lefts = jnp.sum(
        jnp.where(owners[:, None] == jnp.arange(requests)[None], prefixes[None], 0), axis=1
    )
    lefts = jnp.clip(lefts - ((codes - 1) & 127) * PAGE, 0, PAGE)
    kinds = jnp.where((codes > 0) & (lefts > 0), jnp.minimum(owners, PRE), PRE + 1)
    order = jnp.arange(pages, dtype=jnp.int32)
    same = kinds[:, None] == kinds[None, :]
    rank = jnp.sum(jnp.where(same & (order[None, :] < order[:, None]), 1, 0), axis=1)
    of_kind = kinds[None, :] == jnp.arange(PRE + 1, dtype=jnp.int32)[:, None]
    place = jnp.where(of_kind, rank[None, :], -1)
    lists = jnp.sum(
        jnp.where(place[:, None, :] == order[None, :, None], order[None, None, :], 0), axis=2
    )
    bound = jnp.arange(CHUNKS + 1, dtype=jnp.int32) * (pages // CHUNKS)
    here = of_kind[:, None, :] & (order[None, None, :] < bound[None, :, None])
    counts = jnp.sum(here.astype(jnp.int32), axis=2)
    last = jnp.arange(CHUNKS + 1) == CHUNKS
    lists = jnp.concatenate(
        [lists, counts[:, CHUNKS:], (counts + last[None].astype(jnp.int32)) >> 1], axis=1
    )
    tokens = jnp.clip(owners - PRE, 0, DEC - 1)

    turned_weight, cosine = lax.optimization_barrier((out_weight.T, cosine))
    def passed(weight, amount):
        return lax.ppermute(weight, "grp", [(i, (i + amount) % grp) for i in range(grp)])

    near = [passed(turned_weight, 1), passed(turned_weight, grp - 1)]
    partial = lax.all_to_all(partial, "ffn", 0, 0, axis_index_groups=parity)
    partial, *near = lax.optimization_barrier((partial, *near))
    fresh, own_block = call(
        rotate_kernel,
        (shape(ffn, ROWS, HD), shape(2, ROWS, HD)),
        [vmem] * 3,
        out_specs=(vmem, vmem),
    )(partial, cosine, sine)
    middle = []
    for _ in range(2, grp - 1):
        last, own_block = lax.optimization_barrier((middle[-1] if middle else near[0], own_block))
        middle.append(passed(last, 1))
    fresh = swap(fresh, "ffn").reshape(ffn * ROWS, HD)
    fresh, *middle = lax.optimization_barrier((fresh, *middle))
    message = run_attention(
        lists, lefts, tokens, f1, fresh, own_block, key_cache, value_cache, grp, ffn
    )
    message = swap(message, ("grp", "ffn"))
    heads = call(merge_kernel, shape(ffn, ROWS, HD), [vmem])(message)
    heads = swap(heads, "ffn")
    out_weights = [turned_weight, near[0], *middle, near[1]]
    own, rows = call(
        output_kernel,
        (shape(QUARTER, COLS), shape(ffn // 2, MSG, HD)),
        [smem] * 2 + [vmem] * (2 + grp),
        [
            pltpu.VMEM((GH * (QUARTER // FEW), ROWS + 16, HD), F32),
            pltpu.VMEM((grp, 16 * (QUARTER // FEW), GH * HD), BF16),
            pltpu.VMEM((QUARTER, COLS), F32),
        ],
        out_specs=(vmem, vmem),
    )(g1, f1, heads, layer_input, *out_weights)
    gate_up, rows = lax.optimization_barrier((jnp.swapaxes(gate_up_weight, 1, 2), rows))
    mine = lax.all_to_all(rows, "ffn", 0, 0, axis_index_groups=parity)
    ahead = fetched(gate_up)
    theirs = lax.ppermute(mine, "ffn", neighbour)
    kept, sent = run_ffn(
        f1, mine, theirs, ffn_gain.reshape(1, -1), gate_up, down_weight, ahead
    )
    received = lax.ppermute(sent, "ffn", neighbour)
    down_terms = call(join_kernel, shape(*kept.shape), [vmem] * 2)(kept, received)
    down_terms = lax.all_to_all(down_terms, "ffn", 0, 0, axis_index_groups=parity)
    return call(finish_kernel, shape(QUARTER, COLS), [smem] + [vmem] * 2)(f1, down_terms, own)


def solution(mesh):
    in_specs = (
        P(None, "ffn"),
        P("ffn"),
        P(None, "ffn", "grp"),
        P("ffn", None, "grp"),
        P("ffn", None, "grp"),
        P("grp", "ffn"),
        P(),
        P(None, None, "ffn"),
        P("ffn", None),
        P(),
        P(),
        P(),
    )
    out_specs = P("grp", "ffn")
    return jax.shard_map(shards, mesh=mesh, in_specs=in_specs, out_specs=out_specs, check_vma=False)
```

```python
import functools
import math

import jax
import jax.numpy as jnp
from jax import lax
from jax.experimental import pallas as pl
from jax.experimental.pallas import tpu as pltpu
from jax.sharding import PartitionSpec as P

D = 5120
HD = 128
PAGE = 128
SPAN = 128
PRE = 2
DEC = 32
MAXP = 128
TOKENS = 288
GH = 5
ROWS = 48
QUARTER = 72
COLS = 160
MSG = 96
FEW = 12
STATS = 8

EPS = 1e-05
NEG = -1e30
SCALE2 = HD ** (-0.5) * math.log2(math.e)
F32 = jnp.float32
BF16 = jnp.bfloat16
LIMIT = 32 << 20
GROUP = 4
CHUNKS = 4
FCHUNK = 640
AHEAD = 3

vmem = pl.BlockSpec(memory_space=pltpu.VMEM)
smem = pl.BlockSpec(memory_space=pltpu.SMEM)
hbm = pl.BlockSpec(memory_space=pl.ANY)


def params():
    return pltpu.CompilerParams(vmem_limit_bytes=LIMIT)


def lanes(shape):
    return lax.broadcasted_iota(jnp.int32, shape, len(shape) - 1)


def rows_of(shape):
    return lax.broadcasted_iota(jnp.int32, shape, len(shape) - 2)


def split3(value):
    high = value.astype(BF16).astype(F32)
    rest = value - high
    middle = rest.astype(BF16).astype(F32)
    return high, middle, rest - middle


def stat_block(stat):
    row = rows_of((STATS, HD))
    high, middle, low = split3(stat)
    return jnp.where(
        row == 0, high, jnp.where(row == 1, middle, jnp.where(row == 2, low, 0.0))
    ).astype(BF16)


def project_kernel(
    p_ref, x_hbm, gain_hbm, w_hbm, out_ref, x_vmem, gain_ref, w_vmem, x_rows, sems
):
    copies = [pltpu.make_async_copy(x_hbm, x_vmem, sems.at[3])]
    gain_copy = pltpu.make_async_copy(gain_hbm, gain_ref, sems.at[4])
    gain_copy.start()
    for k in range(3):
        copies.append(pltpu.make_async_copy(w_hbm.at[k], w_vmem.at[k], sems.at[k]))
    for copy in copies:
        copy.start()
    copies[0].wait()
    gain_copy.wait()
    x_rows[...] = jnp.transpose(x_vmem[...].astype(F32))
    half = TOKENS // ROWS // 2
    x = jnp.concatenate(
        [
            x_rows[pl.ds(pl.multiple_of((2 * i + p_ref[0]) * ROWS, 16), ROWS), :]
            for i in range(half)
        ],
        axis=0,
    )
    scaled = (x * gain_ref[...]).astype(BF16)
    squares = jnp.sum(x * x, axis=1, keepdims=True)
    diagonal = rows_of((ROWS, HD)) == lanes((ROWS, HD))
    for i in range(half):
        part = jnp.broadcast_to(squares[i * ROWS : (i + 1) * ROWS], (ROWS, HD))
        stat = jnp.sum(jnp.where(diagonal, part, 0.0), axis=0, keepdims=True)
        block = stat_block(stat)
        for h in range(GH):
            out_ref[h * half + i, 3 * ROWS :, :] = block
    for k in range(3):
        copies[1 + k].wait()
        product = jnp.dot(scaled, w_vmem[k], preferred_element_type=F32).astype(BF16)
        for h in range(GH):
            for i in range(half):
                out_ref[h * half + i, k * ROWS : (k + 1) * ROWS, :] = product[
                    i * ROWS : (i + 1) * ROWS, h * HD : (h + 1) * HD
                ]
    for target in range(GH * half, out_ref.shape[0]):
        out_ref[target] = jnp.zeros(out_ref.shape[1:], BF16)


def add_kernel(left_ref, right_ref, out_ref):
    for i in range(out_ref.shape[0]):
        total = left_ref[i].astype(F32) + right_ref[i].astype(F32)
        stat = jnp.sum(total[3 * ROWS :], axis=0, keepdims=True)
        out_ref[i, : 3 * ROWS, :] = total[: 3 * ROWS].astype(BF16)
        out_ref[i, 3 * ROWS :, :] = stat_block(stat)


def rotate_kernel(in_ref, cos_ref, sin_ref, out_ref, own_ref):
    total = in_ref[0].astype(F32)
    for s in range(1, in_ref.shape[0]):
        total = total + in_ref[s].astype(F32)
    diagonal = rows_of((ROWS, HD)) == lanes((ROWS, HD))
    stat = jnp.sum(total[3 * ROWS :], axis=0, keepdims=True)
    squares = jnp.sum(
        jnp.where(diagonal, jnp.broadcast_to(stat, (ROWS, HD)), 0.0), axis=1, keepdims=True
    )
    inverse = lax.rsqrt(squares / D + EPS)

    def rotated(value):
        value = value * inverse
        turned = jnp.concatenate([value[:, HD // 2 :], value[:, : HD // 2]], axis=1)
        return (value * cos_ref[...] + turned * sin_ref[...]).astype(BF16)

    own_ref[0] = rotated(total[ROWS : 2 * ROWS])
    own_ref[1] = (total[2 * ROWS : 3 * ROWS] * inverse).astype(BF16)
    query = rotated(total[:ROWS])
    for s in range(out_ref.shape[0]):
        out_ref[s] = query


def attention_kernel(
    lists,
    left_ref,
    token_ref,
    f_ref,
    fresh_ref,
    own_ref,
    key_hbm,
    value_hbm,
    keep_ref,
    send_ref,
    keys,
    values,
    sems,
    scores,
    peak,
    summed,
    dec_query,
    dec_peak,
    dec_total,
    dec_sum,
    final,
    lse,
):
    pages = key_hbm.shape[0]
    step = pages // CHUNKS
    parts = [pl.ds(c * step, step) for c in range(CHUNKS)]
    copies = [
        pltpu.make_async_copy(key_hbm.at[part], keys.at[part], sems.at[0, c])
        for c, part in enumerate(parts)
    ] + [
        pltpu.make_async_copy(value_hbm.at[part], values.at[part], sems.at[1, c])
        for c, part in enumerate(parts)
    ]
    for copy in copies:
        copy.start()

    peak[...] = jnp.full(peak.shape, NEG, F32)
    summed[...] = jnp.zeros(summed.shape, F32)
    dec_peak[...] = jnp.full(dec_peak.shape, NEG, F32)
    dec_total[...] = jnp.zeros(dec_total.shape, F32)
    dec_sum[...] = jnp.zeros(dec_sum.shape, F32)
    final[:, TOKENS:, :] = jnp.zeros((GH, 16, HD), F32)
    lse[:, TOKENS:, :] = jnp.zeros((GH, 16, HD), F32)
    for h in range(GH):
        dec_query[h] = fresh_ref[h * TOKENS + PRE * SPAN : (h + 1) * TOKENS, :].astype(F32)

    n_pre = [lists[k, pages] for k in range(PRE)]
    n_dec = lists[PRE, pages]
    pairs = [lists[k, pages + 1 + CHUNKS] for k in range(PRE)]

    f = f_ref[0]
    blocks = TOKENS // ROWS
    has_own = f < GH * blocks
    own_head = jnp.where(has_own, f // blocks, 0)
    own_block = jnp.where(has_own, f - own_head * blocks, 0)
    filler = jnp.zeros((PAGE - ROWS, HD), BF16)
    own_keys = jnp.concatenate([own_ref[0], filler], axis=0)
    own_values = jnp.concatenate([own_ref[1], filler], axis=0)
    own_token = own_block * ROWS + lanes((SPAN, PAGE))
    in_block = lanes((SPAN, PAGE)) < ROWS

    def query_rows(request, h):
        return fresh_ref[pl.ds(pl.multiple_of(h * TOKENS + request * SPAN, 16), SPAN), :]

    def scored(query, key):
        product = lax.dot_general(
            query, key, (((1,), (1,)), ((), ())), preferred_element_type=F32
        )
        return product * SCALE2

    def own_scores(request):
        within = own_token - request * SPAN
        visible = in_block & (within >= 0) & (within <= rows_of((SPAN, PAGE)))
        return jnp.where(visible, scored(query_rows(request, own_head), own_keys), NEG), visible

    @pl.when(has_own)
    def _():
        for request in range(PRE):
            unit = request * GH + own_head
            peak[unit] = jnp.maximum(peak[unit], own_scores(request)[0])

    def pair(request, i):
        last = n_pre[request] - 1
        first_page = lists[request, 2 * i]
        second_page = lists[request, jnp.minimum(2 * i + 1, last)]
        return first_page, second_page

    def joined(ref, pages_of, h):
        return jnp.concatenate([ref[p, :, h * HD : (h + 1) * HD] for p in pages_of], axis=0)

    wide_lane = lanes((SPAN, 2 * PAGE))
    def in_chunks(which, one_pass):
        def chunk(c, _):
            part = pl.ds(c * step, step)
            source, target = ((key_hbm, keys), (value_hbm, values))[which]
            pltpu.make_async_copy(source.at[part], target.at[part], sems.at[which, c]).wait()
            for request in range(PRE):
                lower = lists[request, pages + 1 + c]
                upper = lists[request, pages + 2 + c]
                lax.fori_loop(lower, upper, one_pass(request), 0)
            return 0

        lax.fori_loop(0, CHUNKS, chunk, 0)

    def first_pass(request):
        def one_pair(i, _):
            both = pair(request, i)
            left = left_ref[both[0]]
            other = jnp.where(2 * i + 1 < n_pre[request], left_ref[both[1]], 0) + PAGE
            visible = wide_lane < jnp.where(wide_lane < PAGE, left, other)
            for h in range(GH):
                result = scored(query_rows(request, h), joined(keys, both, h))
                result = jnp.where(visible, result, NEG)
                scores[i + request * pairs[0], h] = result
                unit = request * GH + h
                peak[unit] = jnp.maximum(
                    peak[unit], jnp.maximum(result[:, :PAGE], result[:, PAGE:])
                )
            return 0

        return one_pair

    in_chunks(0, first_pass)

    for unit in range(PRE * GH):
        peak[unit] = jnp.broadcast_to(
            jnp.max(peak[unit], axis=1, keepdims=True), (SPAN, SPAN)
        )

    def weigh(unit, weights, value):
        ones = jnp.ones((value.shape[0], HD), BF16)
        both = jnp.concatenate([value, ones], axis=1)
        summed[unit] += jnp.dot(weights.astype(BF16), both, preferred_element_type=F32)

    def second_pass(request):
        def one_pair(i, _):
            both = pair(request, i)
            for h in range(GH):
                unit = request * GH + h
                top = peak[unit]
                top = jnp.concatenate([top, top], axis=1)
                weights = jnp.exp2(scores[i + request * pairs[0], h] - top)
                weigh(unit, weights, joined(values, both, h))
            return 0

        return one_pair

    in_chunks(1, second_pass)

    @pl.when(has_own)
    def _():
        for request in range(PRE):
            unit = request * GH + own_head
            result, visible = own_scores(request)
            weigh(unit, jnp.where(visible, jnp.exp2(result - peak[unit]), 0.0), own_values)

    tall = (8 * GROUP, GROUP * PAGE)
    owner_row = rows_of(tall) >> 3

    def decode_pass(step_index, _):
        tokens, picked, queries = [], [], []
        limit = jnp.zeros(tall, jnp.int32)
        row = rows_of((8, HD))
        for j in range(GROUP):
            position = step_index * GROUP + j
            p = lists[PRE, jnp.minimum(position, n_dec - 1)]
            token = token_ref[p]
            left = jnp.where(position < n_dec, left_ref[p], 0)
            limit = jnp.where(owner_row == j, j * PAGE + left, limit)
            tokens.append(token)
            picked.append(p)
            queries.append(
                jnp.concatenate(
                    [
                        jnp.where(
                            row == h,
                            jnp.broadcast_to(dec_query[h, pl.ds(token, 1), :], (8, HD)),
                            0.0,
                        )
                        for h in range(GH)
                    ],
                    axis=1,
                )
            )
        query = jnp.concatenate(queries, axis=0).astype(BF16)
        many_keys = jnp.concatenate([keys[p] for p in picked], axis=0)
        many_values = jnp.concatenate([values[p] for p in picked], axis=0)
        visible = (lanes(tall) >= owner_row * PAGE) & (lanes(tall) < limit)
        result = jnp.where(visible, scored(query, many_keys), NEG)
        tops = jnp.max(result, axis=1, keepdims=True)
        weights = jnp.where(visible, jnp.exp2(result - tops), 0.0)
        totals = jnp.sum(weights, axis=1, keepdims=True)
        products = jnp.dot(weights.astype(BF16), many_values, preferred_element_type=F32)
        found = [
            (
                tokens[j],
                tops[8 * j : 8 * j + 8],
                totals[8 * j : 8 * j + 8],
                products[8 * j : 8 * j + 8],
            )
            for j in range(GROUP)
        ]
        for token, top, total, product in found:
            before = dec_peak[token]
            after = jnp.maximum(before, top)
            keep = jnp.exp2(before - after)
            take = jnp.exp2(top - after)
            dec_peak[token] = after
            dec_total[token] = dec_total[token] * keep + total * take
            wide = jnp.concatenate([keep] * GH, axis=1)
            wide_take = jnp.concatenate([take] * GH, axis=1)
            dec_sum[token] = dec_sum[token] * wide + product * wide_take
        return 0

    lax.fori_loop(0, (n_dec + GROUP - 1) // GROUP, decode_pass, 0)

    for request in range(PRE):
        for h in range(GH):
            unit = request * GH + h
            total = summed[unit, :, HD:]
            some = total > 0.0
            safe = jnp.where(some, total, 1.0)
            part = pl.ds(request * SPAN, SPAN)
            final[h, part, :] = summed[unit, :, :HD] / safe
            lse[h, part, :] = jnp.where(some, peak[unit] + jnp.log2(safe), NEG)

    first = ROWS - DEC
    dec_rows = pl.ds(PRE * SPAN, DEC)
    for h in range(GH):
        mine = f == h * blocks + blocks - 1
        own = jnp.sum(dec_query[h] * own_ref[0].astype(F32)[first:], axis=1, keepdims=True)
        own = jnp.where(mine, jnp.broadcast_to(own, (DEC, HD)) * SCALE2, NEG)
        before = dec_peak[:, h, :]
        after = jnp.maximum(before, own)
        keep = jnp.exp2(before - after)
        take = jnp.where(mine, jnp.exp2(own - after), 0.0)
        total = dec_total[:, h, :] * keep + take
        value = dec_sum[:, h, h * HD : (h + 1) * HD] * keep
        value = value + take * own_ref[1].astype(F32)[first:]
        some = total > 0.0
        safe = jnp.where(some, total, 1.0)
        final[h, dec_rows, :] = value / safe
        lse[h, dec_rows, :] = jnp.where(some, after + jnp.log2(safe), NEG)

    row = rows_of((16, HD))
    diagonal = (row == lanes((16, HD))) & (row < FEW)
    odd = lax.rem(f, 2) == 1
    half = keep_ref.shape[0] // (TOKENS // QUARTER)
    per_head = QUARTER // FEW

    def block_of(q, h, b):
        part = pl.ds(q * QUARTER + b * FEW, 16)
        stat = jnp.sum(jnp.where(diagonal, lse[h, part, :], 0.0), axis=0, keepdims=True)
        return with_stat(jnp.where(row < FEW, final[h, part, :], 0.0), stat, row)

    for q in range(TOKENS // QUARTER):
        for h in range(GH):
            for b in range(0, per_head, 2):
                even, uneven = block_of(q, h, b), block_of(q, h, b + 1)
                target = q * half + (h * per_head + b) // 2
                keep_ref[target] = jnp.where(odd, uneven, even).astype(BF16)
                send_ref[target] = jnp.where(odd, even, uneven).astype(BF16)
        for target in range(GH * per_head // 2, half):
            keep_ref[q * half + target] = jnp.zeros((16, HD), BF16)
            send_ref[q * half + target] = jnp.zeros((16, HD), BF16)


def with_stat(block, stat, row):
    high, middle, low = split3(stat)
    block = jnp.where(row == FEW, high, block)
    block = jnp.where(row == FEW + 1, middle, block)
    return jnp.where(row == FEW + 2, low, block)


def stat_of(block, row):
    return jnp.sum(jnp.where(row >= FEW, block.astype(F32), 0.0), axis=0, keepdims=True)


def pair_kernel(left_ref, right_ref, out_ref):
    blocks = out_ref.shape[0]
    row = rows_of((16, HD))
    left = jnp.concatenate([stat_of(left_ref[i], row) for i in range(blocks)], axis=0)
    right = jnp.concatenate([stat_of(right_ref[i], row) for i in range(blocks)], axis=0)
    top = jnp.maximum(left, right)
    left = jnp.exp2(left - top)
    right = jnp.exp2(right - top)
    total = left + right
    stats = top + jnp.log2(total)
    turned = jnp.transpose(jnp.concatenate([left / total, right / total], axis=0))
    for i in range(blocks):
        block = turned[:16, i : i + 1] * left_ref[i].astype(F32)
        block = block + turned[:16, blocks + i : blocks + i + 1] * right_ref[i].astype(F32)
        block = jnp.where(row < FEW, block, 0.0)
        out_ref[i] = with_stat(block, stats[i : i + 1], row).astype(BF16)


def merge_kernel(in_ref, out_ref):
    sources = out_ref.shape[0]
    groups = in_ref.shape[0] // sources
    row = rows_of((16, HD))
    all_weights = []
    for g in range(groups):
        stats = jnp.concatenate(
            [
                jnp.sum(
                    jnp.where(row >= FEW, in_ref[g * sources + s].astype(F32), 0.0),
                    axis=0,
                    keepdims=True,
                )
                for s in range(sources)
            ],
            axis=0,
        )
        weights = jnp.exp2(stats - jnp.max(stats, axis=0, keepdims=True))
        all_weights.append(weights / jnp.sum(weights, axis=0, keepdims=True))
    filler = jnp.zeros((HD - groups * sources, HD), F32)
    turned = jnp.transpose(jnp.concatenate(all_weights + [filler], axis=0))
    pieces = []
    for g in range(groups):
        total = jnp.zeros((16, HD), F32)
        for s in range(sources):
            source = g * sources + s
            total = total + turned[:16, source : source + 1] * in_ref[source].astype(F32)
        pieces.append(total[:FEW])
    result = jnp.concatenate(pieces, axis=0).astype(BF16)
    for s in range(out_ref.shape[0]):
        out_ref[s] = result


def output_kernel(g_ref, f_ref, mine_ref, theirs_ref, x_ref, *refs):
    *w_refs, own_ref, out_ref, spread, heads, product = refs
    blocks = QUARTER // FEW
    groups = len(w_refs)
    odd = lax.rem(f_ref[0], 2) == 1
    for source in range(GH * blocks):
        pair = mine_ref[source // 2].astype(F32), theirs_ref[source // 2].astype(F32)
        first, second = pair if source % 2 else pair[::-1]
        spread[source, :ROWS, :] = jnp.where(odd, first, second)
        spread[source, ROWS:, :] = jnp.zeros((16, HD), F32)
    for g in range(groups):
        for h in range(GH):
            for b in range(blocks):
                heads[g, b * 16 : (b + 1) * 16, h * HD : (h + 1) * HD] = spread[
                    h * blocks + b, g * FEW : g * FEW + 16, :
                ].astype(BF16)
    attended = jnp.zeros((16 * blocks, COLS), F32)
    for s in range(groups):
        source = lax.rem(g_ref[0] + groups - s, groups)
        attended = attended + turned_dot(heads[source], w_refs[s][...])
    for b in range(blocks):
        product[b * FEW : (b + 1) * FEW, :] = attended[b * 16 : b * 16 + FEW]
    x = x_ref[...].astype(F32)
    own = jnp.zeros((QUARTER, COLS), F32)
    for i in range(groups):
        own = jnp.where(g_ref[0] == i, x[i * QUARTER : (i + 1) * QUARTER], own)
    own = (own + product[...]).astype(BF16)
    own_ref[...] = own
    message = turned_lanes(packed(own.astype(F32)), lax.rem(f_ref[0], 4)).astype(BF16)
    for s in range(out_ref.shape[0]):
        out_ref[s] = message


def packed(value):
    third = QUARTER // 3
    tail = value[:, HD:]
    extra = jnp.concatenate(
        [tail[i * third : (i + 1) * third] for i in range(3)]
        + [jnp.zeros((third, HD - 3 * (COLS - HD)), F32)],
        axis=1,
    )
    return jnp.concatenate([value[:, :HD], extra], axis=0)


def unpacked(message):
    third = QUARTER // 3
    wide = COLS - HD
    extra = message[QUARTER:]
    tail = jnp.concatenate([extra[:, i * wide : (i + 1) * wide] for i in range(3)], axis=0)
    assert tail.shape == (3 * third, wide)
    return jnp.concatenate([message[:QUARTER], tail], axis=1)


def turned_dot(left, right):
    return lax.dot_general(left, right, (((1,), (1,)), ((), ())), preferred_element_type=F32)


def turned_lanes(message, amount):
    result = message
    for j in range(1, 4):
        result = jnp.where(amount == j, pltpu.roll(message, 32 * j, 1), result)
    return result


def tiles_of(messages):
    third = QUARTER // 3
    lane = lanes((QUARTER, HD))
    heads = [m[:QUARTER] for m in messages]
    tails = [
        jnp.concatenate(
            [m[QUARTER:]] + [pltpu.roll(m[QUARTER:], HD - 32 * i, 1) for i in (1, 2)], axis=0
        )
        for m in messages
    ]
    assert tails[0].shape == (3 * third, HD)
    result = [heads[0]]
    for k in range(1, 5):
        tile = jnp.where(lane >= 32 * (k - 1), tails[k - 1], heads[k - 1])
        result.append(jnp.where(lane >= 32 * k, heads[k], tile) if k < 4 else tile)
    return result


def messages_of(product):
    third = QUARTER // 3
    lane = lanes((QUARTER, HD))
    slot = lanes((third, HD)) >> 5
    tiles = [product[:, k * HD : (k + 1) * HD] for k in range(5)]
    result = []
    for j in range(4):
        head = jnp.where(lane >= 32 * j, tiles[j], tiles[j + 1]) if j else tiles[0]
        extra = jnp.zeros((third, HD), F32)
        for i in range(3):
            piece = tiles[j + 1][i * third : (i + 1) * third]
            piece = pltpu.roll(piece, 32 * i, 1) if i else piece
            extra = jnp.where(slot == (i + j) % 4, piece, extra)
        result.append(jnp.concatenate([head, extra], axis=0).astype(BF16))
    return result


def ffn_kernel(f_ref, mine_ref, theirs_ref, gain_ref, gate_hbm, down_hbm, *refs):
    ahead, refs = refs[:AHEAD], refs[AHEAD:]
    keep_ref, send_ref, rows, normed, gates, down, hidden, sems = refs
    copies = []
    for c in range(AHEAD, D // FCHUNK):
        part = pl.ds(c * FCHUNK, FCHUNK)
        copies.append(
            pltpu.make_async_copy(gate_hbm.at[:, :, part], gates.at[:, :, part], sems.at[c])
        )
    copies.append(pltpu.make_async_copy(down_hbm, down, sems.at[D // FCHUNK]))
    for copy in copies:
        copy.start()
    odd = lax.rem(f_ref[0], 2) == 1
    for s in range(0, 2 * mine_ref.shape[0], 4):
        messages = []
        for j in range(4):
            place = (s + j) // 2
            mine = mine_ref[place].astype(F32)
            theirs = theirs_ref[place].astype(F32)
            messages.append(
                jnp.where(odd, mine, theirs) if j % 2 else jnp.where(odd, theirs, mine)
            )
        for k, tile in enumerate(tiles_of(messages)):
            at = s * COLS + k * HD
            rows[:, at : at + HD] = tile
    full = rows[...]
    inverse = lax.rsqrt(jnp.sum(full * full, axis=1, keepdims=True) / D + EPS)
    normed[...] = (full * inverse * gain_ref[...]).astype(BF16)
    gate = jnp.zeros((QUARTER, down.shape[0]), F32)
    up = jnp.zeros((QUARTER, down.shape[0]), F32)
    for c in range(D // FCHUNK):
        part = pl.ds(c * FCHUNK, FCHUNK)
        block = normed[:, part]
        if c < AHEAD:
            both = ahead[c][0], ahead[c][1]
        else:
            copies[c - AHEAD].wait()
            both = gates[0, :, part], gates[1, :, part]
        gate = gate + turned_dot(block, both[0])
        up = up + turned_dot(block, both[1])
    hidden[...] = (gate / (1.0 + jnp.exp(-gate)) * up).astype(BF16)
    copies[-1].wait()
    wide = 4 * COLS
    for s in range(keep_ref.shape[0] // 2):
        product = jnp.dot(
            hidden[...], down[:, s * wide : (s + 1) * wide], preferred_element_type=F32
        )
        messages = messages_of(product)
        for j in range(2):
            even, uneven = messages[2 * j], messages[2 * j + 1]
            keep_ref[2 * s + j] = jnp.where(odd, uneven, even)
            send_ref[2 * s + j] = jnp.where(odd, even, uneven)


def join_kernel(left_ref, right_ref, out_ref):
    for i in range(out_ref.shape[0]):
        out_ref[i] = (left_ref[i].astype(F32) + right_ref[i].astype(F32)).astype(BF16)


def finish_kernel(f_ref, in_ref, own_ref, out_ref):
    total = in_ref[0].astype(F32)
    for s in range(1, in_ref.shape[0]):
        total = total + in_ref[s].astype(F32)
    total = turned_lanes(total, lax.rem(4 - lax.rem(f_ref[0], 4), 4))
    out_ref[...] = (own_ref[...].astype(F32) + unpacked(total)).astype(BF16)


def fetch_kernel(in_ref, *refs):
    *targets, sems = refs
    copies = [
        pltpu.make_async_copy(in_ref.at[:, :, pl.ds(c * FCHUNK, FCHUNK)], target, sems.at[c])
        for c, target in enumerate(targets)
    ]
    for copy in copies:
        copy.start()
    for copy in copies:
        copy.wait()


def fetched(gate_up):
    out = tuple(shape(*gate_up.shape[:2], FCHUNK) for _ in range(AHEAD))
    return call(
        fetch_kernel,
        out,
        [hbm],
        [pltpu.SemaphoreType.DMA((AHEAD,))],
        out_specs=(vmem,) * AHEAD,
    )(gate_up)


def call(kernel, out, specs, scratch=(), out_specs=None):
    function = pl.pallas_call(
        kernel,
        out_shape=out,
        in_specs=specs,
        out_specs=out_specs if out_specs is not None else vmem,
        scratch_shapes=list(scratch),
        compiler_params=params(),
    )

    def placed(*args):
        return function(
            *[
                pltpu.with_memory_space_constraint(a, pltpu.HBM) if spec is hbm else a
                for a, spec in zip(args, specs)
            ]
        )

    return placed


def shape(*dims, kind=BF16):
    return jax.ShapeDtypeStruct(dims, kind)


def swap(value, axis):
    return lax.all_to_all(value, axis, 0, 0)


def tables(f, span_offsets, decode_lengths):
    within = jnp.arange(SPAN, dtype=jnp.int32)
    prefill = (span_offsets[:, None] + within[None, :]).reshape(PRE * SPAN)
    positions = jnp.concatenate([prefill, decode_lengths])
    block = lax.rem(f, TOKENS // ROWS)
    positions = lax.dynamic_slice_in_dim(positions, block * ROWS, ROWS)
    half_width = HD // 2
    lane = jnp.arange(HD, dtype=jnp.int32)
    frequency = jnp.exp((lane % half_width).astype(F32) * (-2.0 * math.log(10000.0) / HD))
    angles = positions.astype(F32)[:, None] * frequency[None, :]
    sine = jnp.sin(angles) * jnp.where(lane < half_width, -1.0, 1.0)[None, :]
    return jnp.cos(angles), sine


def run_attention(
    lists, lefts, tokens, f1, fresh, own_block, key_cache, value_cache, grp, ffn
):
    pages = key_cache.shape[0]
    units = PRE * GH
    return call(
        attention_kernel,
        (shape(grp * ffn // 2, 16, HD), shape(grp * ffn // 2, 16, HD)),
        [smem] * 4 + [vmem] * 2 + [hbm] * 2,
        [
            pltpu.VMEM((pages, PAGE, GH * HD), BF16),
            pltpu.VMEM((pages, PAGE, GH * HD), BF16),
            pltpu.SemaphoreType.DMA((2, CHUNKS)),
            pltpu.VMEM((pages // 2 + 1, GH, SPAN, 2 * PAGE), F32),
            pltpu.VMEM((units, SPAN, PAGE), F32),
            pltpu.VMEM((units, SPAN, 2 * HD), F32),
            pltpu.VMEM((GH, DEC, HD), F32),
            pltpu.VMEM((DEC, 8, HD), F32),
            pltpu.VMEM((DEC, 8, HD), F32),
            pltpu.VMEM((DEC, 8, GH * HD), F32),
            pltpu.VMEM((GH, TOKENS + 16, HD), F32),
            pltpu.VMEM((GH, TOKENS + 16, HD), F32),
        ],
        out_specs=(vmem, vmem),
    )(lists, lefts, tokens, f1, fresh, own_block, key_cache, value_cache)


def run_ffn(f1, mine, theirs, gain, gate_up, down, ahead):
    hidden_units = down.shape[0]
    return call(
        ffn_kernel,
        (shape(*mine.shape), shape(*mine.shape)),
        [smem] + [vmem] * 3 + [hbm] * 2 + [vmem] * AHEAD,
        [
            pltpu.VMEM((QUARTER, D), F32),
            pltpu.VMEM((QUARTER, D), BF16),
            pltpu.VMEM((2, hidden_units, D), BF16),
            pltpu.VMEM((hidden_units, D), BF16),
            pltpu.VMEM((QUARTER, hidden_units), BF16),
            pltpu.SemaphoreType.DMA((D // FCHUNK + 1,)),
        ],
        out_specs=(vmem, vmem),
    )(f1, mine, theirs, gain, gate_up, down, *ahead)


def shards(
    layer_input,
    norm_gain,
    qkv_weight,
    key_cache,
    value_cache,
    out_weight,
    ffn_gain,
    gate_up_weight,
    down_weight,
    span_offsets,
    decode_lengths,
    page_table,
):
    ffn = lax.axis_size("ffn")
    grp = lax.axis_size("grp")
    f = lax.axis_index("ffn")
    g = lax.axis_index("grp")
    f1 = f.astype(jnp.int32).reshape(1)
    g1 = g.astype(jnp.int32).reshape(1)
    pages = key_cache.shape[0]

    parity = [[2 * i + c for i in range(ffn // 2)] for c in range(2)]
    neighbour = [(i, i ^ 1) for i in range(ffn)]

    def projected(which):
        return call(
            project_kernel,
            shape(ffn // 2, 3 * ROWS + STATS, HD),
            [smem, hbm, hbm, hbm],
            [
                pltpu.VMEM((COLS, TOKENS), BF16),
                pltpu.VMEM((1, COLS), F32),
                pltpu.VMEM(qkv_weight.shape, BF16),
                pltpu.VMEM((TOKENS, COLS), F32),
                pltpu.SemaphoreType.DMA((5,)),
            ],
        )(which, layer_input.T, norm_gain.reshape(1, -1), qkv_weight)

    core = lax.rem(f1, 2)
    sent = projected(1 - core)
    core, sent, page_table = lax.optimization_barrier((core, sent, page_table))
    received = lax.ppermute(sent, "ffn", neighbour)
    partial = call(add_kernel, shape(*sent.shape), [vmem] * 2)(projected(core), received)
    span_rows, partial = lax.optimization_barrier((span_offsets, partial))
    cosine, sine = tables(f, span_rows, decode_lengths)
    local_ids = f * pages + jnp.arange(pages, dtype=jnp.int32)
    requests = PRE + DEC
    numbers = jnp.arange(requests * MAXP, dtype=jnp.int32).reshape(requests, MAXP) + 1
    codes = jnp.sum(
        jnp.where(page_table[None] == local_ids[:, None, None], numbers[None], 0), axis=(1, 2)
    )
    prefixes = jnp.concatenate([span_offsets, decode_lengths])
    owners = (codes - 1) >> 7
    lefts = jnp.sum(
        jnp.where(owners[:, None] == jnp.arange(requests)[None], prefixes[None], 0), axis=1
    )
    lefts = jnp.clip(lefts - ((codes - 1) & 127) * PAGE, 0, PAGE)
    kinds = jnp.where((codes > 0) & (lefts > 0), jnp.minimum(owners, PRE), PRE + 1)
    order = jnp.arange(pages, dtype=jnp.int32)
    same = kinds[:, None] == kinds[None, :]
    rank = jnp.sum(jnp.where(same & (order[None, :] < order[:, None]), 1, 0), axis=1)
    of_kind = kinds[None, :] == jnp.arange(PRE + 1, dtype=jnp.int32)[:, None]
    place = jnp.where(of_kind, rank[None, :], -1)
    lists = jnp.sum(
        jnp.where(place[:, None, :] == order[None, :, None], order[None, None, :], 0), axis=2
    )
    bound = jnp.arange(CHUNKS + 1, dtype=jnp.int32) * (pages // CHUNKS)
    here = of_kind[:, None, :] & (order[None, None, :] < bound[None, :, None])
    counts = jnp.sum(here.astype(jnp.int32), axis=2)
    last = jnp.arange(CHUNKS + 1) == CHUNKS
    lists = jnp.concatenate(
        [lists, counts[:, CHUNKS:], (counts + last[None].astype(jnp.int32)) >> 1], axis=1
    )
    tokens = jnp.clip(owners - PRE, 0, DEC - 1)

    turned_weight, cosine = lax.optimization_barrier((out_weight.T, cosine))
    def passed(weight, amount):
        return lax.ppermute(weight, "grp", [(i, (i + amount) % grp) for i in range(grp)])

    near = [passed(turned_weight, 1)]
    partial = lax.all_to_all(partial, "ffn", 0, 0, axis_index_groups=parity)
    partial, *near = lax.optimization_barrier((partial, *near))
    fresh, own_block = call(
        rotate_kernel,
        (shape(ffn, ROWS, HD), shape(2, ROWS, HD)),
        [vmem] * 3,
        out_specs=(vmem, vmem),
    )(partial, cosine, sine)
    middle = []
    for _ in range(2, grp - 1):
        last, own_block = lax.optimization_barrier((middle[-1] if middle else near[0], own_block))
        middle.append(passed(last, 1))
    fresh = swap(fresh, "ffn").reshape(ffn * ROWS, HD)
    fresh, *middle = lax.optimization_barrier((fresh, *middle))
    kept, sent = run_attention(
        lists, lefts, tokens, f1, fresh, own_block, key_cache, value_cache, grp, ffn
    )
    received = lax.ppermute(sent, "ffn", neighbour)
    message = call(pair_kernel, shape(*kept.shape), [vmem] * 2)(kept, received)
    cores = [[g * ffn + i for g in range(grp) for i in group] for group in parity]
    message = lax.all_to_all(message, ("grp", "ffn"), 0, 0, axis_index_groups=cores)
    heads = call(merge_kernel, shape(ffn // 2, ROWS, HD), [vmem])(message)
    heads = lax.all_to_all(heads, "ffn", 0, 0, axis_index_groups=parity)
    others = lax.ppermute(heads, "ffn", neighbour)
    far = passed(out_weight.T, grp - 1)
    out_weights = [turned_weight, near[0], *middle, far]
    own, rows = call(
        output_kernel,
        (shape(QUARTER, COLS), shape(ffn // 2, MSG, HD)),
        [smem] * 2 + [vmem] * (3 + grp),
        [
            pltpu.VMEM((GH * (QUARTER // FEW), ROWS + 16, HD), F32),
            pltpu.VMEM((grp, 16 * (QUARTER // FEW), GH * HD), BF16),
            pltpu.VMEM((QUARTER, COLS), F32),
        ],
        out_specs=(vmem, vmem),
    )(g1, f1, heads, others, layer_input, *out_weights)
    gate_up, rows = lax.optimization_barrier((jnp.swapaxes(gate_up_weight, 1, 2), rows))
    mine = lax.all_to_all(rows, "ffn", 0, 0, axis_index_groups=parity)
    ahead = fetched(gate_up)
    theirs = lax.ppermute(mine, "ffn", neighbour)
    kept, sent = run_ffn(
        f1, mine, theirs, ffn_gain.reshape(1, -1), gate_up, down_weight, ahead
    )
    received = lax.ppermute(sent, "ffn", neighbour)
    down_terms = call(join_kernel, shape(*kept.shape), [vmem] * 2)(kept, received)
    down_terms = lax.all_to_all(down_terms, "ffn", 0, 0, axis_index_groups=parity)
    return call(finish_kernel, shape(QUARTER, COLS), [smem] + [vmem] * 2)(f1, down_terms, own)


def solution(mesh):
    in_specs = (
        P(None, "ffn"),
        P("ffn"),
        P(None, "ffn", "grp"),
        P("ffn", None, "grp"),
        P("ffn", None, "grp"),
        P("grp", "ffn"),
        P(),
        P(None, None, "ffn"),
        P("ffn", None),
        P(),
        P(),
        P(),
    )
    out_specs = P("grp", "ffn")
    return jax.shard_map(shards, mesh=mesh, in_specs=in_specs, out_specs=out_specs, check_vma=False)
```

```python
import functools
import math

import jax
import jax.numpy as jnp
from jax import lax
from jax.experimental import pallas as pl
from jax.experimental.pallas import tpu as pltpu
from jax.sharding import PartitionSpec as P

D = 5120
HD = 128
PAGE = 128
SPAN = 128
PRE = 2
DEC = 32
MAXP = 128
TOKENS = 288
GH = 5
ROWS = 48
QUARTER = 72
COLS = 160
MSG = 96
FEW = 12
STATS = 8

EPS = 1e-05
NEG = -1e30
SCALE2 = HD ** (-0.5) * math.log2(math.e)
F32 = jnp.float32
BF16 = jnp.bfloat16
LIMIT = 32 << 20
GROUP = 4
CHUNKS = 4
FCHUNK = 640
AHEAD = 3

vmem = pl.BlockSpec(memory_space=pltpu.VMEM)
smem = pl.BlockSpec(memory_space=pltpu.SMEM)
hbm = pl.BlockSpec(memory_space=pl.ANY)


def params():
    return pltpu.CompilerParams(vmem_limit_bytes=LIMIT)


def lanes(shape):
    return lax.broadcasted_iota(jnp.int32, shape, len(shape) - 1)


def rows_of(shape):
    return lax.broadcasted_iota(jnp.int32, shape, len(shape) - 2)


def split3(value):
    high = value.astype(BF16).astype(F32)
    rest = value - high
    middle = rest.astype(BF16).astype(F32)
    return high, middle, rest - middle


def stat_block(stat):
    row = rows_of((STATS, HD))
    high, middle, low = split3(stat)
    return jnp.where(
        row == 0, high, jnp.where(row == 1, middle, jnp.where(row == 2, low, 0.0))
    ).astype(BF16)


def project_kernel(
    p_ref, x_hbm, gain_hbm, w_hbm, out_ref, x_vmem, gain_ref, w_vmem, x_rows, sems
):
    copies = [pltpu.make_async_copy(x_hbm, x_vmem, sems.at[3])]
    gain_copy = pltpu.make_async_copy(gain_hbm, gain_ref, sems.at[4])
    gain_copy.start()
    for k in range(3):
        copies.append(pltpu.make_async_copy(w_hbm.at[k], w_vmem.at[k], sems.at[k]))
    for copy in copies:
        copy.start()
    copies[0].wait()
    gain_copy.wait()
    x_rows[...] = jnp.transpose(x_vmem[...].astype(F32))
    half = TOKENS // ROWS // 2
    x = jnp.concatenate(
        [
            x_rows[pl.ds(pl.multiple_of((2 * i + p_ref[0]) * ROWS, 16), ROWS), :]
            for i in range(half)
        ],
        axis=0,
    )
    scaled = (x * gain_ref[...]).astype(BF16)
    squares = jnp.sum(x * x, axis=1, keepdims=True)
    diagonal = rows_of((ROWS, HD)) == lanes((ROWS, HD))
    for i in range(half):
        part = jnp.broadcast_to(squares[i * ROWS : (i + 1) * ROWS], (ROWS, HD))
        stat = jnp.sum(jnp.where(diagonal, part, 0.0), axis=0, keepdims=True)
        block = stat_block(stat)
        for h in range(GH):
            out_ref[h * half + i, 3 * ROWS :, :] = block
    for k in range(3):
        copies[1 + k].wait()
        product = jnp.dot(scaled, w_vmem[k], preferred_element_type=F32).astype(BF16)
        for h in range(GH):
            for i in range(half):
                out_ref[h * half + i, k * ROWS : (k + 1) * ROWS, :] = product[
                    i * ROWS : (i + 1) * ROWS, h * HD : (h + 1) * HD
                ]
    for target in range(GH * half, out_ref.shape[0]):
        out_ref[target] = jnp.zeros(out_ref.shape[1:], BF16)


def add_kernel(left_ref, right_ref, out_ref):
    for i in range(out_ref.shape[0]):
        total = left_ref[i].astype(F32) + right_ref[i].astype(F32)
        stat = jnp.sum(total[3 * ROWS :], axis=0, keepdims=True)
        out_ref[i, : 3 * ROWS, :] = total[: 3 * ROWS].astype(BF16)
        out_ref[i, 3 * ROWS :, :] = stat_block(stat)


def rotate_kernel(in_ref, cos_ref, sin_ref, out_ref, own_ref):
    total = in_ref[0].astype(F32)
    for s in range(1, in_ref.shape[0]):
        total = total + in_ref[s].astype(F32)
    diagonal = rows_of((ROWS, HD)) == lanes((ROWS, HD))
    stat = jnp.sum(total[3 * ROWS :], axis=0, keepdims=True)
    squares = jnp.sum(
        jnp.where(diagonal, jnp.broadcast_to(stat, (ROWS, HD)), 0.0), axis=1, keepdims=True
    )
    inverse = lax.rsqrt(squares / D + EPS)

    def rotated(value):
        value = value * inverse
        turned = jnp.concatenate([value[:, HD // 2 :], value[:, : HD // 2]], axis=1)
        return (value * cos_ref[...] + turned * sin_ref[...]).astype(BF16)

    own_ref[0] = rotated(total[ROWS : 2 * ROWS])
    own_ref[1] = (total[2 * ROWS : 3 * ROWS] * inverse).astype(BF16)
    query = rotated(total[:ROWS])
    for s in range(out_ref.shape[0]):
        out_ref[s] = query


def attention_kernel(
    lists,
    left_ref,
    token_ref,
    f_ref,
    fresh_ref,
    own_ref,
    key_hbm,
    value_hbm,
    keep_ref,
    send_ref,
    keys,
    values,
    sems,
    scores,
    peak,
    summed,
    dec_query,
    dec_peak,
    dec_total,
    dec_sum,
    final,
    lse,
):
    pages = key_hbm.shape[0]
    step = pages // CHUNKS
    parts = [pl.ds(c * step, step) for c in range(CHUNKS)]
    copies = [
        pltpu.make_async_copy(key_hbm.at[part], keys.at[part], sems.at[0, c])
        for c, part in enumerate(parts)
    ] + [
        pltpu.make_async_copy(value_hbm.at[part], values.at[part], sems.at[1, c])
        for c, part in enumerate(parts)
    ]
    for copy in copies:
        copy.start()

    peak[...] = jnp.full(peak.shape, NEG, F32)
    summed[...] = jnp.zeros(summed.shape, F32)
    dec_peak[...] = jnp.full(dec_peak.shape, NEG, F32)
    dec_total[...] = jnp.zeros(dec_total.shape, F32)
    dec_sum[...] = jnp.zeros(dec_sum.shape, F32)
    final[:, TOKENS:, :] = jnp.zeros((GH, 16, HD), F32)
    lse[:, TOKENS:, :] = jnp.zeros((GH, 16, HD), F32)
    for h in range(GH):
        dec_query[h] = fresh_ref[h * TOKENS + PRE * SPAN : (h + 1) * TOKENS, :].astype(F32)

    n_pre = [lists[k, pages] for k in range(PRE)]
    n_dec = lists[PRE, pages]
    pairs = [lists[k, pages + 1 + CHUNKS] for k in range(PRE)]

    f = f_ref[0]
    blocks = TOKENS // ROWS
    has_own = f < GH * blocks
    own_head = jnp.where(has_own, f // blocks, 0)
    own_block = jnp.where(has_own, f - own_head * blocks, 0)
    filler = jnp.zeros((PAGE - ROWS, HD), BF16)
    own_keys = jnp.concatenate([own_ref[0], filler], axis=0)
    own_values = jnp.concatenate([own_ref[1], filler], axis=0)
    own_token = own_block * ROWS + lanes((SPAN, PAGE))
    in_block = lanes((SPAN, PAGE)) < ROWS

    def query_rows(request, h):
        return fresh_ref[pl.ds(pl.multiple_of(h * TOKENS + request * SPAN, 16), SPAN), :]

    def scored(query, key):
        product = lax.dot_general(
            query, key, (((1,), (1,)), ((), ())), preferred_element_type=F32
        )
        return product * SCALE2

    def own_scores(request):
        within = own_token - request * SPAN
        visible = in_block & (within >= 0) & (within <= rows_of((SPAN, PAGE)))
        return jnp.where(visible, scored(query_rows(request, own_head), own_keys), NEG), visible

    @pl.when(has_own)
    def _():
        for request in range(PRE):
            unit = request * GH + own_head
            peak[unit] = jnp.maximum(peak[unit], own_scores(request)[0])

    def pair(request, i):
        last = n_pre[request] - 1
        first_page = lists[request, 2 * i]
        second_page = lists[request, jnp.minimum(2 * i + 1, last)]
        return first_page, second_page

    def joined(ref, pages_of, h):
        return jnp.concatenate([ref[p, :, h * HD : (h + 1) * HD] for p in pages_of], axis=0)

    wide_lane = lanes((SPAN, 2 * PAGE))
    def in_chunks(which, one_pass):
        def chunk(c, _):
            part = pl.ds(c * step, step)
            source, target = ((key_hbm, keys), (value_hbm, values))[which]
            pltpu.make_async_copy(source.at[part], target.at[part], sems.at[which, c]).wait()
            for request in range(PRE):
                lower = lists[request, pages + 1 + c]
                upper = lists[request, pages + 2 + c]
                lax.fori_loop(lower, upper, one_pass(request), 0)
            return 0

        lax.fori_loop(0, CHUNKS, chunk, 0)

    def first_pass(request):
        def one_pair(i, _):
            both = pair(request, i)
            left = left_ref[both[0]]
            other = jnp.where(2 * i + 1 < n_pre[request], left_ref[both[1]], 0) + PAGE
            visible = wide_lane < jnp.where(wide_lane < PAGE, left, other)
            for h in range(GH):
                result = scored(query_rows(request, h), joined(keys, both, h))
                result = jnp.where(visible, result, NEG)
                scores[i + request * pairs[0], h] = result
                unit = request * GH + h
                peak[unit] = jnp.maximum(
                    peak[unit], jnp.maximum(result[:, :PAGE], result[:, PAGE:])
                )
            return 0

        return one_pair

    in_chunks(0, first_pass)

    for unit in range(PRE * GH):
        peak[unit] = jnp.broadcast_to(
            jnp.max(peak[unit], axis=1, keepdims=True), (SPAN, SPAN)
        )

    def weigh(unit, weights, value):
        ones = jnp.ones((value.shape[0], HD), BF16)
        both = jnp.concatenate([value, ones], axis=1)
        summed[unit] += jnp.dot(weights.astype(BF16), both, preferred_element_type=F32)

    def second_pass(request):
        def one_pair(i, _):
            both = pair(request, i)
            for h in range(GH):
                unit = request * GH + h
                top = peak[unit]
                top = jnp.concatenate([top, top], axis=1)
                weights = jnp.exp2(scores[i + request * pairs[0], h] - top)
                weigh(unit, weights, joined(values, both, h))
            return 0

        return one_pair

    in_chunks(1, second_pass)

    @pl.when(has_own)
    def _():
        for request in range(PRE):
            unit = request * GH + own_head
            result, visible = own_scores(request)
            weigh(unit, jnp.where(visible, jnp.exp2(result - peak[unit]), 0.0), own_values)

    tall = (8 * GROUP, GROUP * PAGE)
    owner_row = rows_of(tall) >> 3

    def decode_pass(step_index, _):
        tokens, picked, queries = [], [], []
        limit = jnp.zeros(tall, jnp.int32)
        row = rows_of((8, HD))
        for j in range(GROUP):
            position = step_index * GROUP + j
            p = lists[PRE, jnp.minimum(position, n_dec - 1)]
            token = token_ref[p]
            left = jnp.where(position < n_dec, left_ref[p], 0)
            limit = jnp.where(owner_row == j, j * PAGE + left, limit)
            tokens.append(token)
            picked.append(p)
            queries.append(
                jnp.concatenate(
                    [
                        jnp.where(
                            row == h,
                            jnp.broadcast_to(dec_query[h, pl.ds(token, 1), :], (8, HD)),
                            0.0,
                        )
                        for h in range(GH)
                    ],
                    axis=1,
                )
            )
        query = jnp.concatenate(queries, axis=0).astype(BF16)
        many_keys = jnp.concatenate([keys[p] for p in picked], axis=0)
        many_values = jnp.concatenate([values[p] for p in picked], axis=0)
        visible = (lanes(tall) >= owner_row * PAGE) & (lanes(tall) < limit)
        result = jnp.where(visible, scored(query, many_keys), NEG)
        tops = jnp.max(result, axis=1, keepdims=True)
        weights = jnp.where(visible, jnp.exp2(result - tops), 0.0)
        totals = jnp.sum(weights, axis=1, keepdims=True)
        products = jnp.dot(weights.astype(BF16), many_values, preferred_element_type=F32)
        found = [
            (
                tokens[j],
                tops[8 * j : 8 * j + 8],
                totals[8 * j : 8 * j + 8],
                products[8 * j : 8 * j + 8],
            )
            for j in range(GROUP)
        ]
        for token, top, total, product in found:
            before = dec_peak[token]
            after = jnp.maximum(before, top)
            keep = jnp.exp2(before - after)
            take = jnp.exp2(top - after)
            dec_peak[token] = after
            dec_total[token] = dec_total[token] * keep + total * take
            wide = jnp.concatenate([keep] * GH, axis=1)
            wide_take = jnp.concatenate([take] * GH, axis=1)
            dec_sum[token] = dec_sum[token] * wide + product * wide_take
        return 0

    lax.fori_loop(0, (n_dec + GROUP - 1) // GROUP, decode_pass, 0)

    for request in range(PRE):
        for h in range(GH):
            unit = request * GH + h
            total = summed[unit, :, HD:]
            some = total > 0.0
            safe = jnp.where(some, total, 1.0)
            part = pl.ds(request * SPAN, SPAN)
            final[h, part, :] = summed[unit, :, :HD] / safe
            lse[h, part, :] = jnp.where(some, peak[unit] + jnp.log2(safe), NEG)

    first = ROWS - DEC
    dec_rows = pl.ds(PRE * SPAN, DEC)
    for h in range(GH):
        mine = f == h * blocks + blocks - 1
        own = jnp.sum(dec_query[h] * own_ref[0].astype(F32)[first:], axis=1, keepdims=True)
        own = jnp.where(mine, jnp.broadcast_to(own, (DEC, HD)) * SCALE2, NEG)
        before = dec_peak[:, h, :]
        after = jnp.maximum(before, own)
        keep = jnp.exp2(before - after)
        take = jnp.where(mine, jnp.exp2(own - after), 0.0)
        total = dec_total[:, h, :] * keep + take
        value = dec_sum[:, h, h * HD : (h + 1) * HD] * keep
        value = value + take * own_ref[1].astype(F32)[first:]
        some = total > 0.0
        safe = jnp.where(some, total, 1.0)
        final[h, dec_rows, :] = value / safe
        lse[h, dec_rows, :] = jnp.where(some, after + jnp.log2(safe), NEG)

    row = rows_of((16, HD))
    diagonal = (row == lanes((16, HD))) & (row < FEW)
    odd = lax.rem(f, 2) == 1
    half = keep_ref.shape[0] // (TOKENS // QUARTER)
    per_head = QUARTER // FEW

    def block_of(q, h, b):
        part = pl.ds(q * QUARTER + b * FEW, 16)
        stat = jnp.sum(jnp.where(diagonal, lse[h, part, :], 0.0), axis=0, keepdims=True)
        return with_stat(jnp.where(row < FEW, final[h, part, :], 0.0), stat, row)

    for q in range(TOKENS // QUARTER):
        for h in range(GH):
            for b in range(0, per_head, 2):
                even, uneven = block_of(q, h, b), block_of(q, h, b + 1)
                target = q * half + (h * per_head + b) // 2
                keep_ref[target] = jnp.where(odd, uneven, even).astype(BF16)
                send_ref[target] = jnp.where(odd, even, uneven).astype(BF16)
        for target in range(GH * per_head // 2, half):
            keep_ref[q * half + target] = jnp.zeros((16, HD), BF16)
            send_ref[q * half + target] = jnp.zeros((16, HD), BF16)


def with_stat(block, stat, row):
    high, middle, low = split3(stat)
    block = jnp.where(row == FEW, high, block)
    block = jnp.where(row == FEW + 1, middle, block)
    return jnp.where(row == FEW + 2, low, block)


def stat_of(block, row):
    return jnp.sum(jnp.where(row >= FEW, block.astype(F32), 0.0), axis=0, keepdims=True)


def pair_kernel(left_ref, right_ref, out_ref):
    blocks = out_ref.shape[0]
    row = rows_of((16, HD))
    left = jnp.concatenate([stat_of(left_ref[i], row) for i in range(blocks)], axis=0)
    right = jnp.concatenate([stat_of(right_ref[i], row) for i in range(blocks)], axis=0)
    top = jnp.maximum(left, right)
    left = jnp.exp2(left - top)
    right = jnp.exp2(right - top)
    total = left + right
    stats = top + jnp.log2(total)
    turned = jnp.transpose(jnp.concatenate([left / total, right / total], axis=0))
    for i in range(blocks):
        block = turned[:16, i : i + 1] * left_ref[i].astype(F32)
        block = block + turned[:16, blocks + i : blocks + i + 1] * right_ref[i].astype(F32)
        block = jnp.where(row < FEW, block, 0.0)
        out_ref[i] = with_stat(block, stats[i : i + 1], row).astype(BF16)


def merge_kernel(in_ref, out_ref):
    sources = out_ref.shape[0]
    groups = in_ref.shape[0] // sources
    row = rows_of((16, HD))
    all_weights = []
    for g in range(groups):
        stats = jnp.concatenate(
            [
                jnp.sum(
                    jnp.where(row >= FEW, in_ref[g * sources + s].astype(F32), 0.0),
                    axis=0,
                    keepdims=True,
                )
                for s in range(sources)
            ],
            axis=0,
        )
        weights = jnp.exp2(stats - jnp.max(stats, axis=0, keepdims=True))
        all_weights.append(weights / jnp.sum(weights, axis=0, keepdims=True))
    filler = jnp.zeros((HD - groups * sources, HD), F32)
    turned = jnp.transpose(jnp.concatenate(all_weights + [filler], axis=0))
    pieces = []
    for g in range(groups):
        total = jnp.zeros((16, HD), F32)
        for s in range(sources):
            source = g * sources + s
            total = total + turned[:16, source : source + 1] * in_ref[source].astype(F32)
        pieces.append(total[:FEW])
    result = jnp.concatenate(pieces, axis=0).astype(BF16)
    for s in range(out_ref.shape[0]):
        out_ref[s] = result


def output_kernel(g_ref, f_ref, mine_ref, theirs_ref, x_ref, *refs):
    *w_refs, own_ref, out_ref, spread, heads, product = refs
    blocks = QUARTER // FEW
    groups = len(w_refs)
    odd = lax.rem(f_ref[0], 2) == 1
    for source in range(GH * blocks):
        pair = mine_ref[source // 2].astype(F32), theirs_ref[source // 2].astype(F32)
        first, second = pair if source % 2 else pair[::-1]
        spread[source, :ROWS, :] = jnp.where(odd, first, second)
        spread[source, ROWS:, :] = jnp.zeros((16, HD), F32)
    for g in range(groups):
        for h in range(GH):
            for b in range(blocks):
                heads[g, b * 16 : (b + 1) * 16, h * HD : (h + 1) * HD] = spread[
                    h * blocks + b, g * FEW : g * FEW + 16, :
                ].astype(BF16)
    attended = jnp.zeros((16 * blocks, COLS), F32)
    for s in range(groups):
        source = lax.rem(g_ref[0] + groups - s, groups)
        attended = attended + turned_dot(heads[source], w_refs[s][...])
    for b in range(blocks):
        product[b * FEW : (b + 1) * FEW, :] = attended[b * 16 : b * 16 + FEW]
    x = x_ref[...].astype(F32)
    own = jnp.zeros((QUARTER, COLS), F32)
    for i in range(groups):
        own = jnp.where(g_ref[0] == i, x[i * QUARTER : (i + 1) * QUARTER], own)
    own = (own + product[...]).astype(BF16)
    own_ref[...] = own
    message = turned_lanes(packed(own.astype(F32)), lax.rem(f_ref[0], 4)).astype(BF16)
    for s in range(out_ref.shape[0]):
        out_ref[s] = message


def packed(value):
    third = QUARTER // 3
    tail = value[:, HD:]
    extra = jnp.concatenate(
        [tail[i * third : (i + 1) * third] for i in range(3)]
        + [jnp.zeros((third, HD - 3 * (COLS - HD)), F32)],
        axis=1,
    )
    return jnp.concatenate([value[:, :HD], extra], axis=0)


def unpacked(message):
    third = QUARTER // 3
    wide = COLS - HD
    extra = message[QUARTER:]
    tail = jnp.concatenate([extra[:, i * wide : (i + 1) * wide] for i in range(3)], axis=0)
    assert tail.shape == (3 * third, wide)
    return jnp.concatenate([message[:QUARTER], tail], axis=1)


def turned_dot(left, right):
    return lax.dot_general(left, right, (((1,), (1,)), ((), ())), preferred_element_type=F32)


def turned_lanes(message, amount):
    result = message
    for j in range(1, 4):
        result = jnp.where(amount == j, pltpu.roll(message, 32 * j, 1), result)
    return result


def tiles_of(messages):
    third = QUARTER // 3
    lane = lanes((QUARTER, HD))
    heads = [m[:QUARTER] for m in messages]
    tails = [
        jnp.concatenate(
            [m[QUARTER:]] + [pltpu.roll(m[QUARTER:], HD - 32 * i, 1) for i in (1, 2)], axis=0
        )
        for m in messages
    ]
    assert tails[0].shape == (3 * third, HD)
    result = [heads[0]]
    for k in range(1, 5):
        tile = jnp.where(lane >= 32 * (k - 1), tails[k - 1], heads[k - 1])
        result.append(jnp.where(lane >= 32 * k, heads[k], tile) if k < 4 else tile)
    return result


def messages_of(product):
    third = QUARTER // 3
    lane = lanes((QUARTER, HD))
    slot = lanes((third, HD)) >> 5
    tiles = [product[:, k * HD : (k + 1) * HD] for k in range(5)]
    result = []
    for j in range(4):
        head = jnp.where(lane >= 32 * j, tiles[j], tiles[j + 1]) if j else tiles[0]
        extra = jnp.zeros((third, HD), F32)
        for i in range(3):
            piece = tiles[j + 1][i * third : (i + 1) * third]
            piece = pltpu.roll(piece, 32 * i, 1) if i else piece
            extra = jnp.where(slot == (i + j) % 4, piece, extra)
        result.append(jnp.concatenate([head, extra], axis=0).astype(BF16))
    return result


def ffn_kernel(f_ref, mine_ref, theirs_ref, gain_ref, gate_hbm, down_hbm, *refs):
    ahead, refs = refs[:AHEAD], refs[AHEAD:]
    keep_ref, send_ref, rows, normed, gates, down, hidden, sems = refs
    copies = []
    for c in range(AHEAD, D // FCHUNK):
        part = pl.ds(c * FCHUNK, FCHUNK)
        copies.append(
            pltpu.make_async_copy(gate_hbm.at[:, :, part], gates.at[:, :, part], sems.at[c])
        )
    copies.append(pltpu.make_async_copy(down_hbm, down, sems.at[D // FCHUNK]))
    for copy in copies:
        copy.start()
    odd = lax.rem(f_ref[0], 2) == 1
    for s in range(0, 2 * mine_ref.shape[0], 4):
        messages = []
        for j in range(4):
            place = (s + j) // 2
            mine = mine_ref[place].astype(F32)
            theirs = theirs_ref[place].astype(F32)
            messages.append(
                jnp.where(odd, mine, theirs) if j % 2 else jnp.where(odd, theirs, mine)
            )
        for k, tile in enumerate(tiles_of(messages)):
            at = s * COLS + k * HD
            rows[:, at : at + HD] = tile
    full = rows[...]
    inverse = lax.rsqrt(jnp.sum(full * full, axis=1, keepdims=True) / D + EPS)
    normed[...] = (full * inverse * gain_ref[...]).astype(BF16)
    gate = jnp.zeros((QUARTER, down.shape[0]), F32)
    up = jnp.zeros((QUARTER, down.shape[0]), F32)
    for c in range(D // FCHUNK):
        part = pl.ds(c * FCHUNK, FCHUNK)
        block = normed[:, part]
        if c < AHEAD:
            both = ahead[c][0], ahead[c][1]
        else:
            copies[c - AHEAD].wait()
            both = gates[0, :, part], gates[1, :, part]
        gate = gate + turned_dot(block, both[0])
        up = up + turned_dot(block, both[1])
    hidden[...] = (gate / (1.0 + jnp.exp(-gate)) * up).astype(BF16)
    copies[-1].wait()
    wide = 4 * COLS
    for s in range(keep_ref.shape[0] // 2):
        product = jnp.dot(
            hidden[...], down[:, s * wide : (s + 1) * wide], preferred_element_type=F32
        )
        messages = messages_of(product)
        for j in range(2):
            even, uneven = messages[2 * j], messages[2 * j + 1]
            keep_ref[2 * s + j] = jnp.where(odd, uneven, even)
            send_ref[2 * s + j] = jnp.where(odd, even, uneven)


def join_kernel(left_ref, right_ref, out_ref):
    for i in range(out_ref.shape[0]):
        out_ref[i] = (left_ref[i].astype(F32) + right_ref[i].astype(F32)).astype(BF16)


def finish_kernel(f_ref, in_ref, own_ref, out_ref):
    total = in_ref[0].astype(F32)
    for s in range(1, in_ref.shape[0]):
        total = total + in_ref[s].astype(F32)
    total = turned_lanes(total, lax.rem(4 - lax.rem(f_ref[0], 4), 4))
    out_ref[...] = (own_ref[...].astype(F32) + unpacked(total)).astype(BF16)


def fetch_kernel(in_ref, *refs):
    *targets, sems = refs
    copies = [
        pltpu.make_async_copy(in_ref.at[:, :, pl.ds(c * FCHUNK, FCHUNK)], target, sems.at[c])
        for c, target in enumerate(targets)
    ]
    for copy in copies:
        copy.start()
    for copy in copies:
        copy.wait()


def fetched(gate_up):
    out = tuple(shape(*gate_up.shape[:2], FCHUNK) for _ in range(AHEAD))
    return call(
        fetch_kernel,
        out,
        [hbm],
        [pltpu.SemaphoreType.DMA((AHEAD,))],
        out_specs=(vmem,) * AHEAD,
    )(gate_up)


def call(kernel, out, specs, scratch=(), out_specs=None):
    function = pl.pallas_call(
        kernel,
        out_shape=out,
        in_specs=specs,
        out_specs=out_specs if out_specs is not None else vmem,
        scratch_shapes=list(scratch),
        compiler_params=params(),
    )

    def placed(*args):
        return function(
            *[
                pltpu.with_memory_space_constraint(a, pltpu.HBM) if spec is hbm else a
                for a, spec in zip(args, specs)
            ]
        )

    return placed


def shape(*dims, kind=BF16):
    return jax.ShapeDtypeStruct(dims, kind)


def swap(value, axis):
    return lax.all_to_all(value, axis, 0, 0)


def tables(f, span_offsets, decode_lengths):
    within = jnp.arange(SPAN, dtype=jnp.int32)
    prefill = (span_offsets[:, None] + within[None, :]).reshape(PRE * SPAN)
    positions = jnp.concatenate([prefill, decode_lengths])
    block = lax.rem(f, TOKENS // ROWS)
    positions = lax.dynamic_slice_in_dim(positions, block * ROWS, ROWS)
    half_width = HD // 2
    lane = jnp.arange(HD, dtype=jnp.int32)
    frequency = jnp.exp((lane % half_width).astype(F32) * (-2.0 * math.log(10000.0) / HD))
    angles = positions.astype(F32)[:, None] * frequency[None, :]
    sine = jnp.sin(angles) * jnp.where(lane < half_width, -1.0, 1.0)[None, :]
    return jnp.cos(angles), sine


def run_attention(
    lists, lefts, tokens, f1, fresh, own_block, key_cache, value_cache, grp, ffn
):
    pages = key_cache.shape[0]
    units = PRE * GH
    return call(
        attention_kernel,
        (shape(grp * ffn // 2, 16, HD), shape(grp * ffn // 2, 16, HD)),
        [smem] * 4 + [vmem] * 2 + [hbm] * 2,
        [
            pltpu.VMEM((pages, PAGE, GH * HD), BF16),
            pltpu.VMEM((pages, PAGE, GH * HD), BF16),
            pltpu.SemaphoreType.DMA((2, CHUNKS)),
            pltpu.VMEM((pages // 2 + 1, GH, SPAN, 2 * PAGE), F32),
            pltpu.VMEM((units, SPAN, PAGE), F32),
            pltpu.VMEM((units, SPAN, 2 * HD), F32),
            pltpu.VMEM((GH, DEC, HD), F32),
            pltpu.VMEM((DEC, 8, HD), F32),
            pltpu.VMEM((DEC, 8, HD), F32),
            pltpu.VMEM((DEC, 8, GH * HD), F32),
            pltpu.VMEM((GH, TOKENS + 16, HD), F32),
            pltpu.VMEM((GH, TOKENS + 16, HD), F32),
        ],
        out_specs=(vmem, vmem),
    )(lists, lefts, tokens, f1, fresh, own_block, key_cache, value_cache)


def run_ffn(f1, mine, theirs, gain, gate_up, down, ahead):
    hidden_units = down.shape[0]
    return call(
        ffn_kernel,
        (shape(*mine.shape), shape(*mine.shape)),
        [smem] + [vmem] * 3 + [hbm] * 2 + [vmem] * AHEAD,
        [
            pltpu.VMEM((QUARTER, D), F32),
            pltpu.VMEM((QUARTER, D), BF16),
            pltpu.VMEM((2, hidden_units, D), BF16),
            pltpu.VMEM((hidden_units, D), BF16),
            pltpu.VMEM((QUARTER, hidden_units), BF16),
            pltpu.SemaphoreType.DMA((D // FCHUNK + 1,)),
        ],
        out_specs=(vmem, vmem),
    )(f1, mine, theirs, gain, gate_up, down, *ahead)


def shards(
    layer_input,
    norm_gain,
    qkv_weight,
    key_cache,
    value_cache,
    out_weight,
    ffn_gain,
    gate_up_weight,
    down_weight,
    span_offsets,
    decode_lengths,
    page_table,
):
    ffn = lax.axis_size("ffn")
    grp = lax.axis_size("grp")
    f = lax.axis_index("ffn")
    g = lax.axis_index("grp")
    f1 = f.astype(jnp.int32).reshape(1)
    g1 = g.astype(jnp.int32).reshape(1)
    pages = key_cache.shape[0]

    parity = [[2 * i + c for i in range(ffn // 2)] for c in range(2)]
    neighbour = [(i, i ^ 1) for i in range(ffn)]

    def projected(which):
        return call(
            project_kernel,
            shape(ffn // 2, 3 * ROWS + STATS, HD),
            [smem, hbm, hbm, hbm],
            [
                pltpu.VMEM((COLS, TOKENS), BF16),
                pltpu.VMEM((1, COLS), F32),
                pltpu.VMEM(qkv_weight.shape, BF16),
                pltpu.VMEM((TOKENS, COLS), F32),
                pltpu.SemaphoreType.DMA((5,)),
            ],
        )(which, layer_input.T, norm_gain.reshape(1, -1), qkv_weight)

    core = lax.rem(f1, 2)
    sent = projected(1 - core)
    core, sent = lax.optimization_barrier((core, sent))
    received = lax.ppermute(sent, "ffn", neighbour)
    partial = call(add_kernel, shape(*sent.shape), [vmem] * 2)(projected(core), received)
    span_rows, page_table, partial = lax.optimization_barrier((span_offsets, page_table, partial))
    cosine, sine = tables(f, span_rows, decode_lengths)
    local_ids = f * pages + jnp.arange(pages, dtype=jnp.int32)
    requests = PRE + DEC
    numbers = jnp.arange(requests * MAXP, dtype=jnp.int32).reshape(requests, MAXP) + 1
    codes = jnp.sum(
        jnp.where(page_table[None] == local_ids[:, None, None], numbers[None], 0), axis=(1, 2)
    )
    prefixes = jnp.concatenate([span_offsets, decode_lengths])
    owners = (codes - 1) >> 7
    lefts = jnp.sum(
        jnp.where(owners[:, None] == jnp.arange(requests)[None], prefixes[None], 0), axis=1
    )
    lefts = jnp.clip(lefts - ((codes - 1) & 127) * PAGE, 0, PAGE)
    kinds = jnp.where((codes > 0) & (lefts > 0), jnp.minimum(owners, PRE), PRE + 1)
    order = jnp.arange(pages, dtype=jnp.int32)
    same = kinds[:, None] == kinds[None, :]
    rank = jnp.sum(jnp.where(same & (order[None, :] < order[:, None]), 1, 0), axis=1)
    of_kind = kinds[None, :] == jnp.arange(PRE + 1, dtype=jnp.int32)[:, None]
    place = jnp.where(of_kind, rank[None, :], -1)
    lists = jnp.sum(
        jnp.where(place[:, None, :] == order[None, :, None], order[None, None, :], 0), axis=2
    )
    bound = jnp.arange(CHUNKS + 1, dtype=jnp.int32) * (pages // CHUNKS)
    here = of_kind[:, None, :] & (order[None, None, :] < bound[None, :, None])
    counts = jnp.sum(here.astype(jnp.int32), axis=2)
    last = jnp.arange(CHUNKS + 1) == CHUNKS
    lists = jnp.concatenate(
        [lists, counts[:, CHUNKS:], (counts + last[None].astype(jnp.int32)) >> 1], axis=1
    )
    tokens = jnp.clip(owners - PRE, 0, DEC - 1)

    turned_weight, cosine, lists = lax.optimization_barrier((out_weight.T, cosine, lists))
    def passed(weight, amount):
        return lax.ppermute(weight, "grp", [(i, (i + amount) % grp) for i in range(grp)])

    near = [passed(turned_weight, 1)]
    partial = lax.all_to_all(partial, "ffn", 0, 0, axis_index_groups=parity)
    partial, *near = lax.optimization_barrier((partial, *near))
    fresh, own_block = call(
        rotate_kernel,
        (shape(ffn, ROWS, HD), shape(2, ROWS, HD)),
        [vmem] * 3,
        out_specs=(vmem, vmem),
    )(partial, cosine, sine)
    middle = []
    for _ in range(2, grp - 1):
        last, own_block = lax.optimization_barrier((middle[-1] if middle else near[0], own_block))
        middle.append(passed(last, 1))
    fresh = swap(fresh, "ffn").reshape(ffn * ROWS, HD)
    fresh, *middle = lax.optimization_barrier((fresh, *middle))
    kept, sent = run_attention(
        lists, lefts, tokens, f1, fresh, own_block, key_cache, value_cache, grp, ffn
    )
    received = lax.ppermute(sent, "ffn", neighbour)
    message = call(pair_kernel, shape(*kept.shape), [vmem] * 2)(kept, received)
    cores = [[g * ffn + i for g in range(grp) for i in group] for group in parity]
    message = lax.all_to_all(message, ("grp", "ffn"), 0, 0, axis_index_groups=cores)
    heads = call(merge_kernel, shape(ffn // 2, ROWS, HD), [vmem])(message)
    heads = lax.all_to_all(heads, "ffn", 0, 0, axis_index_groups=parity)
    others = lax.ppermute(heads, "ffn", neighbour)
    far = passed(out_weight.T, grp - 1)
    out_weights = [turned_weight, near[0], *middle, far]
    own, rows = call(
        output_kernel,
        (shape(QUARTER, COLS), shape(ffn // 2, MSG, HD)),
        [smem] * 2 + [vmem] * (3 + grp),
        [
            pltpu.VMEM((GH * (QUARTER // FEW), ROWS + 16, HD), F32),
            pltpu.VMEM((grp, 16 * (QUARTER // FEW), GH * HD), BF16),
            pltpu.VMEM((QUARTER, COLS), F32),
        ],
        out_specs=(vmem, vmem),
    )(g1, f1, heads, others, layer_input, *out_weights)
    gate_up, rows = lax.optimization_barrier((jnp.swapaxes(gate_up_weight, 1, 2), rows))
    mine = lax.all_to_all(rows, "ffn", 0, 0, axis_index_groups=parity)
    ahead = fetched(gate_up)
    theirs = lax.ppermute(mine, "ffn", neighbour)
    kept, sent = run_ffn(
        f1, mine, theirs, ffn_gain.reshape(1, -1), gate_up, down_weight, ahead
    )
    received = lax.ppermute(sent, "ffn", neighbour)
    down_terms = call(join_kernel, shape(*kept.shape), [vmem] * 2)(kept, received)
    down_terms = lax.all_to_all(down_terms, "ffn", 0, 0, axis_index_groups=parity)
    return call(finish_kernel, shape(QUARTER, COLS), [smem] + [vmem] * 2)(f1, down_terms, own)


def solution(mesh):
    in_specs = (
        P(None, "ffn"),
        P("ffn"),
        P(None, "ffn", "grp"),
        P("ffn", None, "grp"),
        P("ffn", None, "grp"),
        P("grp", "ffn"),
        P(),
        P(None, None, "ffn"),
        P("ffn", None),
        P(),
        P(),
        P(),
    )
    out_specs = P("grp", "ffn")
    return jax.shard_map(shards, mesh=mesh, in_specs=in_specs, out_specs=out_specs, check_vma=False)
```
